32 devices in a mesh: gx: 8 (over y, x, core), gy: 4 (over z).
Axes of the slice: x: 2, y: 2, z: 4, core: 2. Of those that a mesh axis runs over, the one named last changes fastest.
Arguments:
- adjoint_end: float32 [19, 2, 128, 512], P(None, None, 'gx', 'gy'), may hold values from -6 to 6
- forward_pop: bfloat16 [19, 2, 128, 512], P(None, None, 'gx', 'gy'), may hold values from 0 to 1, as said below
- porosity_level: int32 [2, 128, 512], P(None, 'gx', 'gy'), may hold values from 0 to 7
- fluid_mask: int32 [2, 128, 512], P(None, 'gx', 'gy'), may hold values 0 or 1
- design_index: int32 [128, 512], P('gx', 'gy'), may hold values from 0 to 4095, as said below
Outputs:
- adjoint_start: float32 [19, 2, 128, 512], P(None, None, 'gx', 'gy')
- design_grad: float32 [128, 32], P(('gx', 'gy'))
The draws below stay inside these ranges and needn't reach their ends.
Inputs may be any that keep to these rules, and one draw needn't show every extreme that they name: `forward_pop`: every population is positive and a cell's populations sum to between 0.5 and 1.5. `design_index`: the design cell of column (x, y) is (cx, cy) stored as cy * 32 + cx, with cx within two of x // 4 and cy within two of y // 4.
All inputs are finite; a program needn't handle non-finite values. No bound on the sum of `fluid_mask` on one device may be relied on, other than what follows from the above.
Results may differ from the reference program's by a relative error of at most 0.0018.
Values sent between devices are 32-bit elements; how exact they have to be, the bound alone decides.
No kernel may reach another device: no remote copies, remote signals or barrier semaphores. Data moves between devices by JAX's collectives and lax.ppermute only.
A program may use at most 64 MiB of HBM per device.

```python
import jax
import jax.numpy as jnp
import numpy as np

Z = 2
STEPS = 3
LEVELS = 8
NX = 128
NY = 512
DX = 32
DY = 128


def table_speeds():
    speeds = [[0, 0, 0]]
    for axis_index in range(3):
        for sign_value in (1, -1):
            vector_row = [0, 0, 0]
            vector_row[axis_index] = sign_value
            speeds.append(vector_row)
    for plane_pair in ((0, 1), (0, 2), (1, 2)):
        for first_sign in (1, -1):
            for second_sign in (1, -1):
                vector_row = [0, 0, 0]
                vector_row[plane_pair[0]] = first_sign
                vector_row[plane_pair[1]] = second_sign
                speeds.append(vector_row)
    return speeds


def draw_forward_pop(key, part):
    speeds = table_speeds()
    weight_col = jnp.asarray(np.array([1.0 / 3.0] + [1.0 / 18.0] * 6 + [1.0 / 36.0] * 12, dtype=np.float32))[:, None, None, None]
    keys = jax.random.split(key, 3)
    density = jax.random.uniform(keys[0], (Z, NX, NY), jnp.float32, 0.8, 1.2)
    velocity = jax.random.uniform(keys[1], (3, Z, NX, NY), jnp.float32, -0.1, 0.1)
    noise = jax.random.uniform(keys[2], (19, Z, NX, NY), jnp.float32, -0.2, 0.2)
    projected = jnp.zeros((19, Z, NX, NY), jnp.float32)
    for k in range(3):
        column_speed = jnp.asarray(np.array([speed_row[k] for speed_row in speeds], dtype=np.float32))[:, None, None, None]
        projected = projected + column_speed * velocity[k]
    speed_sq = jnp.sum(velocity * velocity, axis=0)
    popul = weight_col * density * (1.0 + 3.0 * projected + 4.5 * projected * projected - 1.5 * speed_sq + noise)
    return popul.astype(jnp.bfloat16)


def draw_design_index(key, part):
    key_x, key_y = jax.random.split(key)
    column_cell = jnp.arange(NX)[:, None] // 4 + jax.random.randint(key_x, (NX, NY), -2, 3)
    row_cell = jnp.arange(NY)[None, :] // 4 + jax.random.randint(key_y, (NX, NY), -2, 3)
    column_cell = jnp.clip(column_cell, 0, DX - 1)
    row_cell = jnp.clip(row_cell, 0, DY - 1)
    flat_index = row_cell * DX + column_cell
    flat_index = flat_index.at[0, 0].set(0).at[NX - 1, NY - 1].set(DX * DY - 1)
    return flat_index.astype(jnp.int32)


def place_ends(result, own_key, least, largest):
    longest = result.shape.index(max(result.shape))
    spots = []
    for shift in (0, 1):
        where = [jax.random.randint(jax.random.fold_in(own_key, axis), (), 0, length) for axis, length in enumerate(result.shape)]
        where[longest] = (where[longest] + shift) % result.shape[longest]
        spots.append(tuple(where))
    return result.at[spots[0]].set(least).at[spots[1]].set(largest)


def levels(own_key, shape, shards, low, high):
    level = 1.0
    for axis_at, blocks in shards:
        heights = jax.random.uniform(jax.random.fold_in(jax.random.fold_in(own_key, 6), axis_at), (blocks,), jnp.float32, low / len(shards), high / len(shards))
        level = level * jnp.repeat(jnp.exp(heights), shape[axis_at] // blocks).reshape((-1,) + (1,) * (len(shape) - 1 - axis_at))
    return level


def centred(stream_key, shape, scale, reach, shards=(), held_as=jnp.bfloat16):
    level = levels(stream_key, shape, shards, -0.22, 0.18) if shards else 1.0
    values = jax.random.normal(stream_key, shape, jnp.float32) * scale * level
    return jnp.minimum(jnp.maximum(values, -reach), reach).astype(held_as)


def setup_inputs(seed: int = 0) -> dict:
    key_of = jax.random.split(jax.random.key(seed), 6)
    adjoint_end = centred(key_of[0], (19, Z, NX, NY), 1.0, 6.0, ((2, 8), (3, 4)), jnp.float32)
    forward_pop = draw_forward_pop(jax.random.fold_in(key_of[5], 71), 0)
    porosity_level = place_ends(jax.random.randint(key_of[2], (Z, NX, NY), 0, LEVELS), jax.random.fold_in(key_of[2], 1), 0, LEVELS - 1).astype(jnp.int32)
    fluid_mask = place_ends((jax.random.randint(key_of[3], (Z, NX, NY), 0, 8) < 7).astype(jnp.int32), jax.random.fold_in(key_of[3], 1), 0, 1)
    design_index = draw_design_index(jax.random.fold_in(key_of[5], 71), 0)
    return {"adjoint_end": adjoint_end, "forward_pop": forward_pop, "porosity_level": porosity_level, "fluid_mask": fluid_mask, "design_index": design_index}


relax_rate = 1.25
porous_max = 0.5


def lattice_table():
    speeds = [[0, 0, 0]]
    for axis_index in range(3):
        for sign_value in (1, -1):
            vector_row = [0, 0, 0]
            vector_row[axis_index] = sign_value
            speeds.append(vector_row)
    for plane_pair in ((0, 1), (0, 2), (1, 2)):
        for first_sign in (1, -1):
            for second_sign in (1, -1):
                vector_row = [0, 0, 0]
                vector_row[plane_pair[0]] = first_sign
                vector_row[plane_pair[1]] = second_sign
                speeds.append(vector_row)
    weights = [1.0 / 3.0] + [1.0 / 18.0] * 6 + [1.0 / 36.0] * 12
    opposite = [speeds.index([-component for component in speed_row]) for speed_row in speeds]
    return speeds, weights, opposite


def speed_columns(speeds):
    return [jnp.asarray(np.array([speed_row[k] for speed_row in speeds], dtype=np.float32))[:, None, None, None] for k in range(3)]


def cell_terms(forward_pop, porosity_level, fluid_mask):
    speeds, weights, opposite = lattice_table()
    speed_axis = speed_columns(speeds)
    weight_col = jnp.asarray(np.array(weights, dtype=np.float32))[:, None, None, None]
    popul = forward_pop.astype(jnp.float32)
    density = jnp.sum(popul, axis=0)
    velocity = [jnp.sum(popul * speed_axis[k], axis=0) / density for k in range(3)]
    speed_sq = velocity[0] * velocity[0] + velocity[1] * velocity[1] + velocity[2] * velocity[2]
    projected = speed_axis[0] * velocity[0] + speed_axis[1] * velocity[1] + speed_axis[2] * velocity[2]
    equilib = weight_col * density * (1.0 + 3.0 * projected + 4.5 * projected * projected - 1.5 * speed_sq)
    relaxed = popul - relax_rate * (popul - equilib)
    response = jnp.stack([popul[opposite[q]] for q in range(19)]) - relaxed
    fluid_frac = fluid_mask.astype(jnp.float32)
    porosity = jnp.where(fluid_mask == 1, porous_max * porosity_level.astype(jnp.float32) / (LEVELS - 1), jnp.float32(1.0))
    return velocity, porosity, response, fluid_frac


def pull_from(padded):
    speeds, weights, opposite = lattice_table()
    size_x = padded.shape[2]
    size_y = padded.shape[3]
    pieces = []
    for q in range(19):
        shift_x, shift_y, shift_z = speeds[q]
        sliced = padded[q, :, 1 + shift_x:size_x - 1 + shift_x, 1 + shift_y:size_y - 1 + shift_y]
        pieces.append(jnp.roll(sliced, -shift_z, axis=0))
    return jnp.stack(pieces)


def collide(pulled, velocity, porosity):
    speeds, weights, opposite = lattice_table()
    speed_axis = speed_columns(speeds)
    weight_col = jnp.asarray(np.array(weights, dtype=np.float32))[:, None, None, None]
    speed_sq = velocity[0] * velocity[0] + velocity[1] * velocity[1] + velocity[2] * velocity[2]
    projected = speed_axis[0] * velocity[0] + speed_axis[1] * velocity[1] + speed_axis[2] * velocity[2]
    weighted = weight_col * pulled
    a_zero = jnp.sum(weighted, axis=0)
    b_sq = jnp.sum(weighted * projected * projected, axis=0)
    kernel = a_zero * (1.0 + 1.5 * speed_sq) - 4.5 * b_sq
    for k in range(3):
        a_one = jnp.sum(weighted * speed_axis[k], axis=0)
        b_vec = jnp.sum(weighted * projected * speed_axis[k], axis=0)
        kernel = kernel + speed_axis[k] * (3.0 * a_one + 9.0 * b_vec - 3.0 * velocity[k] * a_zero)
    flipped = jnp.stack([pulled[opposite[q]] for q in range(19)])
    return (1.0 - porosity) * ((1.0 - relax_rate) * pulled + relax_rate * kernel) + porosity * flipped


def reference(adjoint_end, forward_pop, porosity_level, fluid_mask, design_index):
    velocity, porosity, response, fluid_frac = cell_terms(forward_pop, porosity_level, fluid_mask)
    adjoint = adjoint_end
    sensitivity = jnp.zeros(porosity.shape, jnp.float32)
    for step_num in range(STEPS):
        padded = jnp.pad(adjoint, ((0, 0), (0, 0), (1, 1), (1, 1)))
        pulled = pull_from(padded)
        sensitivity = sensitivity + jnp.sum(pulled * response, axis=0)
        adjoint = collide(pulled, velocity, porosity)
    column_sum = jnp.sum(sensitivity * fluid_frac, axis=0) * (porous_max / (LEVELS - 1))
    partial_grid = jax.ops.segment_sum(column_sum.reshape(-1), design_index.reshape(-1), num_segments=DY * DX)
    return adjoint, partial_grid.reshape(DY, DX)
```

```python
import jax
import jax.numpy as jnp
import numpy as np
from jax import lax
from jax.sharding import PartitionSpec as P

STEPS = 3
LEVELS = 8
BOTH = ("gx", "gy")

relax_rate = 1.25
porous_max = 0.5


def lattice_table():
    speeds = [[0, 0, 0]]
    for axis_index in range(3):
        for sign_value in (1, -1):
            vector_row = [0, 0, 0]
            vector_row[axis_index] = sign_value
            speeds.append(vector_row)
    for plane_pair in ((0, 1), (0, 2), (1, 2)):
        for first_sign in (1, -1):
            for second_sign in (1, -1):
                vector_row = [0, 0, 0]
                vector_row[plane_pair[0]] = first_sign
                vector_row[plane_pair[1]] = second_sign
                speeds.append(vector_row)
    weights = [1.0 / 3.0] + [1.0 / 18.0] * 6 + [1.0 / 36.0] * 12
    opposite = [speeds.index([-component for component in speed_row]) for speed_row in speeds]
    return (speeds, weights, opposite)


def swap_pairs(count, parity):
    pairs = []
    for i in range(count):
        j = (i ^ 1) if parity == 0 else ((i - 1) ^ 1) + 1
        if 0 <= j < count:
            pairs.append((i, j))
    return pairs


def swap_halo(low_face, high_face, axis):
    count = lax.axis_size(axis)
    even = lax.axis_index(axis) % 2 == 0
    inner = jnp.where(even, high_face, low_face)
    outer = jnp.where(even, low_face, high_face)
    got_outer = lax.ppermute(outer, axis, swap_pairs(count, 1))
    got_inner = lax.ppermute(inner, axis, swap_pairs(count, 0))
    return (jnp.where(even, got_outer, got_inner), jnp.where(even, got_inner, got_outer))


def cell_terms(forward_pop, porosity_level, fluid_mask):
    speeds, weights, opposite = lattice_table()
    popul = [forward_pop[q].astype(jnp.float32) for q in range(19)]
    density = sum(popul[1:], popul[0])
    velocity = []
    for k in range(3):
        total = None
        for q in range(19):
            if speeds[q][k] != 0:
                term = popul[q] * float(speeds[q][k])
                total = term if total is None else total + term
        velocity.append(total / density)
    speed_sq = velocity[0] * velocity[0] + velocity[1] * velocity[1] + velocity[2] * velocity[2]
    response = []
    for q in range(19):
        projected = None
        for k in range(3):
            if speeds[q][k] != 0:
                term = velocity[k] * float(speeds[q][k])
                projected = term if projected is None else projected + term
        if projected is None:
            equilib = weights[q] * density * (1.0 - 1.5 * speed_sq)
        else:
            equilib = (
                weights[q]
                * density
                * (1.0 + 3.0 * projected + 4.5 * projected * projected - 1.5 * speed_sq)
            )
        relaxed = popul[q] - relax_rate * (popul[q] - equilib)
        response.append(popul[opposite[q]] - relaxed)
    fluid_frac = fluid_mask.astype(jnp.float32)
    porosity = jnp.where(
        fluid_mask == 1,
        porous_max * porosity_level.astype(jnp.float32) / (LEVELS - 1),
        jnp.float32(1.0),
    )
    return (velocity, porosity, response, fluid_frac)


def pull_list(padded):
    speeds, weights, opposite = lattice_table()
    size_x = padded[0].shape[1]
    size_y = padded[0].shape[2]
    pieces = []
    for q in range(19):
        shift_x, shift_y, shift_z = speeds[q]
        sliced = padded[q][:, 1 + shift_x : size_x - 1 + shift_x, 1 + shift_y : size_y - 1 + shift_y]
        pieces.append(sliced if shift_z == 0 else jnp.roll(sliced, -shift_z, axis=0))
    return pieces


def weighted_total(pieces, coeffs):
    total = None
    for q in range(19):
        if coeffs[q] != 0.0:
            term = pieces[q] * coeffs[q]
            total = term if total is None else total + term
    return total


def collide_list(pulled, velocity, keep, porosity):
    speeds, weights, opposite = lattice_table()
    speed_sq = velocity[0] * velocity[0] + velocity[1] * velocity[1] + velocity[2] * velocity[2]
    a_zero = weighted_total(pulled, weights)
    a_one = [
        weighted_total(pulled, [weights[q] * speeds[q][k] for q in range(19)]) for k in range(3)
    ]
    second = {}
    for k in range(3):
        for l in range(k, 3):
            second[k, l] = weighted_total(
                pulled, [weights[q] * speeds[q][k] * speeds[q][l] for q in range(19)]
            )
            second[l, k] = second[k, l]
    b_vec = []
    for k in range(3):
        b_vec.append(
            velocity[0] * second[k, 0] + velocity[1] * second[k, 1] + velocity[2] * second[k, 2]
        )
    b_sq = velocity[0] * b_vec[0] + velocity[1] * b_vec[1] + velocity[2] * b_vec[2]
    base = a_zero * (1.0 + 1.5 * speed_sq) - 4.5 * b_sq
    vector_part = [3.0 * a_one[k] + 9.0 * b_vec[k] - 3.0 * velocity[k] * a_zero for k in range(3)]
    results = []
    for j in range(19):
        kernel = base
        for k in range(3):
            if speeds[j][k] != 0:
                kernel = kernel + float(speeds[j][k]) * vector_part[k]
        results.append(
            keep * ((1.0 - relax_rate) * pulled[j] + relax_rate * kernel)
            + porosity * pulled[opposite[j]]
        )
    return results


def per_device(adjoint_end, forward_pop, porosity_level, fluid_mask, design_index):
    velocity, porosity, response, fluid_frac = cell_terms(forward_pop, porosity_level, fluid_mask)
    depth = adjoint_end.shape[1]
    tile_x = adjoint_end.shape[2]
    tile_y = adjoint_end.shape[3]
    fields = jnp.stack(velocity + [1.0 - porosity, porosity])

    def pack_x(first):
        adj_rows = adjoint_end[:, :, first : first + 3].reshape(-1, tile_y)
        near = 0 if first == 0 else tile_x - 2
        return jnp.concatenate([adj_rows, fields[:, :, near : near + 2].reshape(-1, tile_y)], axis=0)

    low, high = swap_halo(pack_x(0), pack_x(tile_x - 3), "gx")
    cut = 19 * depth * 3
    adj = jnp.concatenate(
        [
            low[:cut].reshape(19, depth, 3, tile_y),
            adjoint_end,
            high[:cut].reshape(19, depth, 3, tile_y),
        ],
        axis=2,
    )
    fields = jnp.concatenate(
        [low[cut:].reshape(5, depth, 2, tile_y), fields, high[cut:].reshape(5, depth, 2, tile_y)],
        axis=2,
    )
    wide = tile_x + 6

    def pack_y(first):
        cols = jnp.transpose(adj[:, :, :, first : first + 3], (3, 0, 1, 2)).reshape(-1, wide)
        near = 0 if first == 0 else tile_y - 2
        more = jnp.transpose(fields[:, :, :, near : near + 2], (3, 0, 1, 2)).reshape(-1, wide - 2)
        return jnp.concatenate([cols, jnp.pad(more, ((0, 0), (0, 2)))], axis=0)

    def unpack_y(got):
        cols = jnp.transpose(got[:cut].reshape(3, 19, depth, wide), (1, 2, 3, 0))
        more = jnp.transpose(got[cut:, : wide - 2].reshape(2, 5, depth, wide - 2), (1, 2, 3, 0))
        return (cols, more)

    low, high = swap_halo(pack_y(0), pack_y(tile_y - 3), "gy")
    low_adj, low_fields = unpack_y(low)
    high_adj, high_fields = unpack_y(high)
    adj = jnp.concatenate([low_adj, adj, high_adj], axis=3)
    fields = jnp.concatenate([low_fields, fields, high_fields], axis=3)

    padded = [adj[q] for q in range(19)]
    sensitivity = None
    for step_num in range(STEPS):
        edge = STEPS - 1 - step_num
        pulled = pull_list(padded)
        cut_out = slice(None) if edge == 0 else slice(edge, -edge)
        for q in range(19):
            term = pulled[q][:, cut_out, cut_out] * response[q]
            sensitivity = term if sensitivity is None else sensitivity + term
        trim = step_num
        inside = slice(trim, -trim) if trim else slice(None)
        here = [fields[k][:, inside, inside] for k in range(5)]
        padded = collide_list(pulled, here[:3], here[3], here[4])
    adjoint = jnp.stack(padded)
    column_sum = jnp.sum(sensitivity * fluid_frac, axis=0) * (porous_max / (LEVELS - 1))

    owners = lax.axis_size("gx") * lax.axis_size("gy")
    design_cols = tile_x * lax.axis_size("gx") // 4
    design_rows = tile_y * lax.axis_size("gy") // 4
    chunk = design_rows * design_cols // owners
    owner_hot = (design_index // chunk)[:, None, :] == jnp.arange(owners)[None, :, None]
    owner_val = jnp.where(owner_hot, column_sum[:, None, :], 0.0)
    slot_hot = ((design_index % chunk)[:, None, :] == jnp.arange(chunk)[None, :, None]).astype(
        jnp.float32
    )
    partial_grid = lax.dot_general(
        owner_val, slot_hot, (((0, 2), (0, 2)), ((), ())), precision=lax.Precision.HIGHEST
    )
    received = lax.all_to_all(
        partial_grid.reshape(owners, 1, chunk), BOTH, split_axis=0, concat_axis=0, tiled=True
    )
    owned = jnp.sum(received, axis=0).reshape(design_rows // owners, design_cols)
    return (adjoint, owned)


def solution(mesh):
    in_specs = (
        P(None, None, "gx", "gy"),
        P(None, None, "gx", "gy"),
        P(None, "gx", "gy"),
        P(None, "gx", "gy"),
        P("gx", "gy"),
    )
    out_specs = (P(None, None, "gx", "gy"), P(("gx", "gy"), None))
    return jax.shard_map(
        per_device, mesh=mesh, in_specs=in_specs, out_specs=out_specs, check_vma=False
    )
```

```python
import jax
import jax.numpy as jnp
from jax import lax
from jax.experimental import pallas as pl
from jax.experimental.pallas import tpu as pltpu
from jax.sharding import PartitionSpec as P

STEPS = 3
LEVELS = 8
BOTH = ("gx", "gy")
FIELDS = 5

relax_rate = 1.25
porous_max = 0.5


def lattice_table():
    speeds = [[0, 0, 0]]
    for axis_index in range(3):
        for sign_value in (1, -1):
            vector_row = [0, 0, 0]
            vector_row[axis_index] = sign_value
            speeds.append(vector_row)
    for plane_pair in ((0, 1), (0, 2), (1, 2)):
        for first_sign in (1, -1):
            for second_sign in (1, -1):
                vector_row = [0, 0, 0]
                vector_row[plane_pair[0]] = first_sign
                vector_row[plane_pair[1]] = second_sign
                speeds.append(vector_row)
    return speeds


SPEEDS = lattice_table()
PAIRS = ((1, 2), (3, 4), (5, 6), (7, 10), (8, 9), (11, 14), (12, 13), (15, 18), (16, 17))

WIDTHS = [3 if SPEEDS[q][1] != 0 else 2 for q in range(19)] + [2] * FIELDS
STARTS = [sum(WIDTHS[:n]) for n in range(19 + FIELDS)]
Z_LANES = 64


def swap_pairs(count, parity):
    pairs = []
    for i in range(count):
        j = (i ^ 1) if parity == 0 else ((i - 1) ^ 1) + 1
        if 0 <= j < count:
            pairs.append((i, j))
    return pairs


def is_even(axis):
    return lax.rem(lax.axis_index(axis), 2) == 0


def iota(shape, dim):
    return lax.broadcasted_iota(jnp.int32, shape, dim)


def moments(even, odd, rest):
    e_x, e_y, e_z, e_xy, e_xw, e_xz, e_xv, e_yz, e_yv = even
    o_x, o_y, o_z, o_xy, o_xw, o_xz, o_xv, o_yz, o_yv = odd
    d_xy = e_xy + e_xw
    d_xz = e_xz + e_xv
    d_yz = e_yz + e_yv
    s_xx = 2.0 * e_x + (d_xy + d_xz)
    s_yy = 2.0 * e_y + (d_xy + d_yz)
    s_zz = 2.0 * e_z + (d_xz + d_yz)
    s_xy = e_xy - e_xw
    s_xz = e_xz - e_xv
    s_yz = e_yz - e_yv
    total = 12.0 * rest + 2.0 * ((e_x + e_y) + e_z) + ((d_xy + d_xz) + d_yz)
    v_x = 2.0 * o_x + ((o_xy + o_xw) + (o_xz + o_xv))
    v_y = 2.0 * o_y + ((o_xy - o_xw) + (o_yz + o_yv))
    v_z = 2.0 * o_z + ((o_xz - o_xv) + (o_yz - o_yv))
    return total, (v_x, v_y, v_z), ((s_xx, s_xy, s_xz), (s_xy, s_yy, s_yz), (s_xz, s_yz, s_zz))


def contract(second, velocity):
    return [
        second[k][0] * velocity[0] + second[k][1] * velocity[1] + second[k][2] * velocity[2]
        for k in range(3)
    ]


def dot3(a, b):
    return a[0] * b[0] + a[1] * b[1] + a[2] * b[2]


def split_pairs(pulled):
    even = [pulled[i] + pulled[j] for i, j in PAIRS]
    odd = [pulled[i] - pulled[j] for i, j in PAIRS]
    return even, odd


def collide(pulled, velocity, keep, porosity):
    even, odd = split_pairs(pulled)
    total, first, second = moments(even, odd, pulled[0])
    flux = contract(second, velocity)
    twice = dot3(velocity, flux)
    gain = keep * (relax_rate / 36.0)
    stay = keep * (1.0 - relax_rate)
    base = gain * (total * (1.0 + 1.5 * dot3(velocity, velocity)) - 4.5 * twice)
    turn = [gain * (3.0 * (first[k] - velocity[k] * total) + 9.0 * flux[k]) for k in range(3)]
    both = 0.5 * (stay + porosity)
    diff = 0.5 * (stay - porosity)
    results = [None] * 19
    results[0] = (stay + porosity) * pulled[0] + base
    for n, (i, j) in enumerate(PAIRS):
        along = None
        for k in range(3):
            if SPEEDS[i][k] == 1:
                along = turn[k] if along is None else along + turn[k]
            elif SPEEDS[i][k] == -1:
                along = along - turn[k]
        same = both * even[n] + base
        swing = diff * odd[n] + along
        results[i] = same + swing
        results[j] = same - swing
    return results


MIRRORS = [
    (q, SPEEDS.index([-SPEEDS[q][0], SPEEDS[q][1], SPEEDS[q][2]]))
    for q in range(19)
    if SPEEDS[q][0] == 1
]
FLAT = [q for q in range(19) if SPEEDS[q][0] == 0] + list(range(19, 19 + FIELDS))
X_TILES = len(MIRRORS) + (len(FLAT) + 1) // 2


def turned(tile, shift, axis):
    shift = shift % tile.shape[axis]
    return tile if shift == 0 else pltpu.roll(tile, shift, axis)


def edge_kernel(
    adj_hbm, fwd_hbm, level_hbm, mask_hbm, index_hbm,
    outer, inner, fields, adj, fwd, mask, index, level, sems,
):
    copies = [
        pltpu.make_async_copy(src, dst, sems.at[n])
        for n, (src, dst) in enumerate(
            (
                (fwd_hbm, fwd), (mask_hbm, mask), (level_hbm, level),
                (adj_hbm, adj), (index_hbm, index),
            )
        )
    ]
    for copy in copies:
        copy.start()
    for copy in copies[:3]:
        copy.wait()
    depth, rows = adj.shape[1], adj.shape[2]
    for z in range(depth):
        popul = [fwd[q, z].astype(jnp.float32) for q in range(19)]
        even, odd = split_pairs(popul)
        density = popul[0]
        for n in range(9):
            density = density + even[n]
        o_x, o_y, o_z, o_xy, o_xw, o_xz, o_xv, o_yz, o_yv = odd
        per_mass = 1.0 / density
        fields[0, z] = (o_x + ((o_xy + o_xw) + (o_xz + o_xv))) * per_mass
        fields[1, z] = (o_y + ((o_xy - o_xw) + (o_yz + o_yv))) * per_mass
        fields[2, z] = (o_z + ((o_xz - o_xv) + (o_yz - o_yv))) * per_mass
        porosity = jnp.where(
            mask[z] == 1, level[z].astype(jnp.float32) * (porous_max / (LEVELS - 1)), 1.0
        )
        fields[3, z] = 1.0 - porosity
        fields[4, z] = porosity
    copies[3].wait()
    even_x = is_even("gx")
    row = iota((8, 128), 0)

    def top(n, z):
        return adj[n, z, 0:8, :] if n < 19 else fields[n - 19, z, 0:8, :]

    def bottom(n, z):
        at = slice(rows - 8, rows)
        return adj[n, z, at, :] if n < 19 else fields[n - 19, z, at, :]

    for n, (up, down) in enumerate(MIRRORS):
        low = jnp.where(row < 3, top(up, 0), turned(top(up, 1), 3, 0))
        low = jnp.where(row < 6, low, turned(top(down, 0), 6, 0))
        low = jnp.where(row < 7, low, turned(top(down, 1), 7, 0))
        high = jnp.where(row < 3, turned(bottom(down, 0), 3, 0), turned(bottom(down, 1), 6, 0))
        high = jnp.where(row < 6, high, turned(bottom(up, 0), 7, 0))
        high = jnp.where(row < 7, high, bottom(up, 1))
        inner[n] = jnp.where(even_x, high, low)
        outer[n] = jnp.where(even_x, low, high)
    for n in range(0, len(FLAT), 2):
        low = high = None
        for m, item in enumerate(FLAT[n : n + 2]):
            for z in range(depth):
                at = 4 * m + 2 * z
                up = turned(top(item, z), at, 0)
                down = turned(bottom(item, z), at + 2, 0)
                low = up if low is None else jnp.where(row < at, low, up)
                high = down if high is None else jnp.where(row < at, high, down)
        tile = len(MIRRORS) + n // 2
        inner[tile] = jnp.where(even_x, high, low)
        outer[tile] = jnp.where(even_x, low, high)
    copies[4].wait()


def side_kernel(adj, fields, got_outer, got_inner, inner, outer, adj_rim, field_rim):
    depth = adj.shape[1]
    even_x = is_even("gx")
    row = iota((8, 128), 0)

    def received(tile):
        from_in = got_inner[tile]
        from_out = got_outer[tile]
        return jnp.where(even_x, from_out, from_in), jnp.where(even_x, from_in, from_out)

    for n, (up, down) in enumerate(MIRRORS):
        low, high = received(n)
        for z in range(depth):
            adj_rim[up, z] = jnp.where(row < 4, turned(high, -3 * z, 0), turned(low, 1 - z, 0))
            adj_rim[down, z] = jnp.where(row < 4, turned(high, 2 - z, 0), turned(low, 5 - 3 * z, 0))
    for n in range(0, len(FLAT), 2):
        low, high = received(len(MIRRORS) + n // 2)
        for m, item in enumerate(FLAT[n : n + 2]):
            for z in range(depth):
                at = 4 * m + 2 * z
                rim = jnp.where(row < 4, turned(high, -at, 0), turned(low, 6 - at, 0))
                if item < 19:
                    adj_rim[item, z] = rim
                else:
                    field_rim[item - 19, z] = rim
    full = adj.shape[2] + 8
    lane = iota((full, 128), 1)
    low = high = None
    for z in range(depth):
        for n in range(19 + FIELDS):
            at = z * Z_LANES + STARTS[n]
            if n < 19:
                tile = jnp.concatenate([adj[n, z], adj_rim[n, z]], axis=0)
            else:
                tile = jnp.concatenate([fields[n - 19, z], field_rim[n - 19, z]], axis=0)
            up = turned(tile, at, 1)
            down = turned(tile, at + WIDTHS[n], 1)
            low = up if low is None else jnp.where(lane >= at, up, low)
            high = down if high is None else jnp.where(lane >= at, down, high)
    even_y = is_even("gy")
    inner[...] = jnp.where(even_y, high, low)
    outer[...] = jnp.where(even_y, low, high)


def step_kernel(
    owners, chunk, adj, adj_rim, fields, field_rim, got_inner, got_outer, fwd, mask, index,
    grid, last, adj_m, adj_h, pull_m, pull_h, field_h, summed,
):
    depth, rows = adj.shape[1], adj.shape[2]
    full = rows + 8
    lane = iota((full, 128), 1)
    even_y = is_even("gy")
    from_in = got_inner[...]
    from_out = got_outer[...]
    low = jnp.where(even_y, from_out, from_in)
    high = jnp.where(even_y, from_in, from_out)
    for n in range(19 + FIELDS):
        for z in range(depth):
            at = z * Z_LANES + STARTS[n]
            above = high if at == 0 else pltpu.roll(high, 128 - at, 1)
            turn = (256 - WIDTHS[n] - at) % 128
            below = low if turn == 0 else pltpu.roll(low, turn, 1)
            halo = jnp.where(lane < 64, above, below)
            if n < 19:
                adj_h[n, z] = halo
            else:
                field_h[n - 19, z] = halo

    for step_num in range(STEPS):
        final = step_num == STEPS - 1
        for q in range(19):
            shift_x, shift_y, shift_z = SPEEDS[q]
            for z in range(depth):
                src = (z + shift_z) % depth
                if step_num == 0:
                    main = jnp.concatenate([adj[q, src], adj_rim[q, src]], axis=0)
                else:
                    main = adj_m[q, src]
                side = adj_h[q, src]
                if shift_x:
                    main = pltpu.roll(main, (-shift_x) % full, 0)
                    side = pltpu.roll(side, (-shift_x) % full, 0)
                if shift_y:
                    main = pltpu.roll(main, (-shift_y) % 128, 1)
                    side = pltpu.roll(side, (-shift_y) % 128, 1)
                    cross = lane == (127 if shift_y == 1 else 0)
                    main, side = jnp.where(cross, side, main), jnp.where(cross, main, side)
                own = main[:rows]
                if final:
                    last[q, z] = own
                    summed[q, z] = summed[q, z] + own
                else:
                    pull_m[q, z] = main
                    pull_h[q, z] = side
                    summed[q, z] = own if step_num == 0 else summed[q, z] + own
        if not final:
            for z in range(depth):
                for t in range(full // 8):
                    at = slice(8 * t, 8 * t + 8)
                    pulled = [pull_m[q, z, at, :] for q in range(19)]
                    if 8 * t < rows:
                        here = [fields[k, z, at, :] for k in range(FIELDS)]
                    else:
                        here = [field_rim[k, z] for k in range(FIELDS)]
                    out = collide(pulled, here[:3], here[3], here[4])
                    for q in range(19):
                        adj_m[q, z, at, :] = out[q]
                    pulled = [pull_h[q, z, at, :] for q in range(19)]
                    here = [field_h[k, z, at, :] for k in range(FIELDS)]
                    out = collide(pulled, here[:3], here[3], here[4])
                    for q in range(19):
                        adj_h[q, z, at, :] = out[q]

    column = None
    for z in range(depth):
        popul = [fwd[q, z].astype(jnp.float32) for q in range(19)]
        f_even, f_odd = split_pairs(popul)
        density = popul[0]
        for n in range(9):
            density = density + f_even[n]
        pulled = [summed[q, z] for q in range(19)]
        even, odd = split_pairs(pulled)
        total, first, second = moments(even, odd, pulled[0])
        velocity = [fields[k, z] for k in range(3)]
        flux = contract(second, velocity)
        even_sum = even[0] * f_even[0]
        odd_sum = odd[0] * f_odd[0]
        for n in range(1, 9):
            even_sum = even_sum + even[n] * f_even[n]
            odd_sum = odd_sum + odd[n] * f_odd[n]
        relaxed = (
            total * (1.0 - 1.5 * dot3(velocity, velocity))
            + 3.0 * dot3(velocity, first)
            + 4.5 * dot3(velocity, flux)
        )
        half = 0.5 * relax_rate
        sensitivity = (
            half * even_sum
            + (half - 1.0) * odd_sum
            + relax_rate * (popul[0] * pulled[0])
            - (relax_rate / 36.0) * (density * relaxed)
        )
        term = sensitivity * mask[z].astype(jnp.float32)
        column = term if column is None else column + term
    column = column * (porous_max / (LEVELS - 1))
    top = column.astype(jnp.bfloat16).astype(jnp.float32)
    rest = column - top
    owner = lax.div(index[...], chunk) if chunk & (chunk - 1) else index[...] >> (chunk.bit_length() - 1)
    slot = index[...] - owner * chunk
    owner_row = iota((owners, 128), 0)
    slot_row = iota((chunk, 128), 0)
    acc = None
    for x in range(0, rows, 2):
        lhs = []
        rhs = []
        for r in (x, x + 1):
            hot = owner_row == owner[r : r + 1, :]
            lhs.append(
                jnp.concatenate(
                    [
                        jnp.where(hot, top[r : r + 1, :], 0.0).astype(jnp.bfloat16),
                        jnp.where(hot, rest[r : r + 1, :], 0.0).astype(jnp.bfloat16),
                    ],
                    axis=0,
                )
            )
            rhs.append(jnp.where(slot_row == slot[r : r + 1, :], 1.0, 0.0).astype(jnp.bfloat16))
        part = lax.dot_general(
            jnp.concatenate(lhs, axis=1),
            jnp.concatenate(rhs, axis=1),
            (((1,), (1,)), ((), ())),
            preferred_element_type=jnp.float32,
        )
        acc = part if acc is None else acc + part
    grid[...] = acc[:owners] + acc[owners:]


def final_kernel(last, fields, out):
    depth, rows = last.shape[1], last.shape[2]
    for z in range(depth):
        for t in range(rows // 8):
            at = slice(8 * t, 8 * t + 8)
            here = [fields[k, z, at, :] for k in range(FIELDS)]
            result = collide([last[q, z, at, :] for q in range(19)], here[:3], here[3], here[4])
            for q in range(19):
                out[q, z, at, :] = result[q]


def call(kernel, out_types, args, scratch=(), flops=0, where=pltpu.VMEM):
    moved = sum(a.size * a.dtype.itemsize for a in args)
    return pl.pallas_call(
        kernel,
        out_shape=[pltpu.VMEM(shape, dtype) for shape, dtype in out_types],
        in_specs=[pl.BlockSpec(memory_space=where)] * len(args),
        out_specs=[pl.BlockSpec(memory_space=pltpu.VMEM)] * len(out_types),
        scratch_shapes=list(scratch),
        compiler_params=pltpu.CompilerParams(vmem_limit_bytes=16 << 20),
        cost_estimate=pl.CostEstimate(flops=flops, bytes_accessed=moved, transcendentals=0),
    )(*[pltpu.with_memory_space_constraint(a, where) for a in args])


def per_device(adjoint_end, forward_pop, porosity_level, fluid_mask, design_index):
    depth, tile_x, tile_y = adjoint_end.shape[1:]
    full = tile_x + 8
    gx_count = lax.axis_size("gx")
    gy_count = lax.axis_size("gy")
    owners = gx_count * gy_count
    design_cols = tile_x * gx_count // 4
    design_rows = tile_y * gy_count // 4
    chunk = design_rows * design_cols // owners
    f32 = jnp.float32
    own = ((19, depth, tile_x, tile_y), f32)
    wide = pltpu.VMEM((19, depth, full, tile_y), f32)

    outer, inner, fields, adj, fwd, mask, index = call(
        edge_kernel,
        [
            ((X_TILES, 8, tile_y), f32), ((X_TILES, 8, tile_y), f32),
            ((FIELDS, depth, tile_x, tile_y), f32), own, (forward_pop.shape, forward_pop.dtype),
            (fluid_mask.shape, fluid_mask.dtype), (design_index.shape, design_index.dtype),
        ],
        [adjoint_end, forward_pop, porosity_level, fluid_mask, design_index],
        [
            pltpu.VMEM(porosity_level.shape, porosity_level.dtype),
            pltpu.SemaphoreType.DMA((5,)),
        ],
        where=pltpu.HBM,
    )
    got_outer = lax.ppermute(outer, "gx", swap_pairs(gx_count, 1))
    got_inner = lax.ppermute(inner, "gx", swap_pairs(gx_count, 0))
    inner, outer, adj_rim, field_rim = call(
        side_kernel,
        [
            ((full, 128), f32), ((full, 128), f32), ((19, depth, 8, tile_y), f32),
            ((FIELDS, depth, 8, tile_y), f32),
        ],
        [adj, fields, got_outer, got_inner],
    )
    got_inner = lax.ppermute(inner, "gy", swap_pairs(gy_count, 0))
    got_outer = lax.ppermute(outer, "gy", swap_pairs(gy_count, 1))
    grid, last = call(
        lambda *refs: step_kernel(owners, chunk, *refs),
        [((owners, chunk), f32), own],
        [adj, adj_rim, fields, field_rim, got_inner, got_outer, fwd, mask, index],
        [
            wide, wide, wide, wide, pltpu.VMEM((FIELDS, depth, full, tile_y), f32),
            pltpu.VMEM(*own),
        ],
    )
    received = lax.all_to_all(
        grid.reshape(owners, 1, chunk), BOTH, split_axis=0, concat_axis=0, tiled=True
    )
    (adjoint_start,) = call(final_kernel, [own], [last, fields], flops=10**6)
    owned = jnp.sum(received, axis=0).reshape(design_rows // owners, design_cols)
    return (adjoint_start, owned)


def solution(mesh):
    in_specs = (
        P(None, None, "gx", "gy"),
        P(None, None, "gx", "gy"),
        P(None, "gx", "gy"),
        P(None, "gx", "gy"),
        P("gx", "gy"),
    )
    out_specs = (P(None, None, "gx", "gy"), P(("gx", "gy"), None))
    return jax.shard_map(
        per_device, mesh=mesh, in_specs=in_specs, out_specs=out_specs, check_vma=False
    )
```

```python
import jax
import jax.numpy as jnp
from jax import lax
from jax.experimental import pallas as pl
from jax.experimental.pallas import tpu as pltpu
from jax.sharding import PartitionSpec as P

STEPS = 3
LEVELS = 8
BOTH = ("gx", "gy")
FIELDS = 5

relax_rate = 1.25
porous_max = 0.5


def lattice_table():
    speeds = [[0, 0, 0]]
    for axis_index in range(3):
        for sign_value in (1, -1):
            vector_row = [0, 0, 0]
            vector_row[axis_index] = sign_value
            speeds.append(vector_row)
    for plane_pair in ((0, 1), (0, 2), (1, 2)):
        for first_sign in (1, -1):
            for second_sign in (1, -1):
                vector_row = [0, 0, 0]
                vector_row[plane_pair[0]] = first_sign
                vector_row[plane_pair[1]] = second_sign
                speeds.append(vector_row)
    return speeds


SPEEDS = lattice_table()
PAIRS = ((1, 2), (3, 4), (5, 6), (7, 10), (8, 9), (11, 14), (12, 13), (15, 18), (16, 17))

WIDTHS = [3 if SPEEDS[q][1] != 0 else 2 for q in range(19)] + [2] * FIELDS
STARTS = [sum(WIDTHS[:n]) for n in range(19 + FIELDS)]
Z_LANES = 64


def swap_pairs(count, parity):
    pairs = []
    for i in range(count):
        j = (i ^ 1) if parity == 0 else ((i - 1) ^ 1) + 1
        if 0 <= j < count:
            pairs.append((i, j))
    return pairs


def is_even(axis):
    return lax.rem(lax.axis_index(axis), 2) == 0


def iota(shape, dim):
    return lax.broadcasted_iota(jnp.int32, shape, dim)


def moments(even, odd, rest):
    e_x, e_y, e_z, e_xy, e_xw, e_xz, e_xv, e_yz, e_yv = even
    o_x, o_y, o_z, o_xy, o_xw, o_xz, o_xv, o_yz, o_yv = odd
    d_xy = e_xy + e_xw
    d_xz = e_xz + e_xv
    d_yz = e_yz + e_yv
    s_xx = 2.0 * e_x + (d_xy + d_xz)
    s_yy = 2.0 * e_y + (d_xy + d_yz)
    s_zz = 2.0 * e_z + (d_xz + d_yz)
    s_xy = e_xy - e_xw
    s_xz = e_xz - e_xv
    s_yz = e_yz - e_yv
    total = 12.0 * rest + 2.0 * ((e_x + e_y) + e_z) + ((d_xy + d_xz) + d_yz)
    v_x = 2.0 * o_x + ((o_xy + o_xw) + (o_xz + o_xv))
    v_y = 2.0 * o_y + ((o_xy - o_xw) + (o_yz + o_yv))
    v_z = 2.0 * o_z + ((o_xz - o_xv) + (o_yz - o_yv))
    return total, (v_x, v_y, v_z), ((s_xx, s_xy, s_xz), (s_xy, s_yy, s_yz), (s_xz, s_yz, s_zz))


def contract(second, velocity):
    return [
        second[k][0] * velocity[0] + second[k][1] * velocity[1] + second[k][2] * velocity[2]
        for k in range(3)
    ]


def dot3(a, b):
    return a[0] * b[0] + a[1] * b[1] + a[2] * b[2]


def split_pairs(pulled):
    even = [pulled[i] + pulled[j] for i, j in PAIRS]
    odd = [pulled[i] - pulled[j] for i, j in PAIRS]
    return even, odd


def collide(pulled, velocity, keep, porosity):
    even, odd = split_pairs(pulled)
    total, first, second = moments(even, odd, pulled[0])
    flux = contract(second, velocity)
    twice = dot3(velocity, flux)
    gain = keep * (relax_rate / 36.0)
    stay = keep * (1.0 - relax_rate)
    base = gain * (total * (1.0 + 1.5 * dot3(velocity, velocity)) - 4.5 * twice)
    turn = [gain * (3.0 * (first[k] - velocity[k] * total) + 9.0 * flux[k]) for k in range(3)]
    both = 0.5 * (stay + porosity)
    diff = 0.5 * (stay - porosity)
    results = [None] * 19
    results[0] = (stay + porosity) * pulled[0] + base
    for n, (i, j) in enumerate(PAIRS):
        along = None
        for k in range(3):
            if SPEEDS[i][k] == 1:
                along = turn[k] if along is None else along + turn[k]
            elif SPEEDS[i][k] == -1:
                along = along - turn[k]
        same = both * even[n] + base
        swing = diff * odd[n] + along
        results[i] = same + swing
        results[j] = same - swing
    return results


MIRRORS = [
    (q, SPEEDS.index([-SPEEDS[q][0], SPEEDS[q][1], SPEEDS[q][2]]))
    for q in range(19)
    if SPEEDS[q][0] == 1
]
FLAT = [q for q in range(19) if SPEEDS[q][0] == 0] + list(range(19, 19 + FIELDS))
X_TILES = len(MIRRORS) + (len(FLAT) + 1) // 2


def turned(tile, shift, axis):
    shift = shift % tile.shape[axis]
    return tile if shift == 0 else pltpu.roll(tile, shift, axis)


def edge_kernel(
    adj_hbm, fwd_hbm, level_hbm, mask_hbm, index_hbm,
    outer, inner, fields, adj, fwd, mask, index, level, sems,
):
    copies = [
        pltpu.make_async_copy(src, dst, sems.at[n])
        for n, (src, dst) in enumerate(
            (
                (fwd_hbm, fwd), (mask_hbm, mask), (level_hbm, level),
                (adj_hbm, adj), (index_hbm, index),
            )
        )
    ]
    for copy in copies:
        copy.start()
    for copy in copies[:3]:
        copy.wait()
    depth, rows = adj.shape[1], adj.shape[2]
    for z in range(depth):
        popul = [fwd[q, z].astype(jnp.float32) for q in range(19)]
        even, odd = split_pairs(popul)
        density = popul[0]
        for n in range(9):
            density = density + even[n]
        o_x, o_y, o_z, o_xy, o_xw, o_xz, o_xv, o_yz, o_yv = odd
        per_mass = 1.0 / density
        fields[0, z] = (o_x + ((o_xy + o_xw) + (o_xz + o_xv))) * per_mass
        fields[1, z] = (o_y + ((o_xy - o_xw) + (o_yz + o_yv))) * per_mass
        fields[2, z] = (o_z + ((o_xz - o_xv) + (o_yz - o_yv))) * per_mass
        porosity = jnp.where(
            mask[z] == 1, level[z].astype(jnp.float32) * (porous_max / (LEVELS - 1)), 1.0
        )
        fields[3, z] = 1.0 - porosity
        fields[4, z] = porosity
    copies[3].wait()
    even_x = is_even("gx")
    row = iota((8, 128), 0)

    def top(n, z):
        return adj[n, z, 0:8, :] if n < 19 else fields[n - 19, z, 0:8, :]

    def bottom(n, z):
        at = slice(rows - 8, rows)
        return adj[n, z, at, :] if n < 19 else fields[n - 19, z, at, :]

    for n, (up, down) in enumerate(MIRRORS):
        low = jnp.where(row < 3, top(up, 0), turned(top(up, 1), 3, 0))
        low = jnp.where(row < 6, low, turned(top(down, 0), 6, 0))
        low = jnp.where(row < 7, low, turned(top(down, 1), 7, 0))
        high = jnp.where(row < 3, turned(bottom(down, 0), 3, 0), turned(bottom(down, 1), 6, 0))
        high = jnp.where(row < 6, high, turned(bottom(up, 0), 7, 0))
        high = jnp.where(row < 7, high, bottom(up, 1))
        inner[n] = jnp.where(even_x, high, low)
        outer[n] = jnp.where(even_x, low, high)
    for n in range(0, len(FLAT), 2):
        low = high = None
        for m, item in enumerate(FLAT[n : n + 2]):
            for z in range(depth):
                at = 4 * m + 2 * z
                up = turned(top(item, z), at, 0)
                down = turned(bottom(item, z), at + 2, 0)
                low = up if low is None else jnp.where(row < at, low, up)
                high = down if high is None else jnp.where(row < at, high, down)
        tile = len(MIRRORS) + n // 2
        inner[tile] = jnp.where(even_x, high, low)
        outer[tile] = jnp.where(even_x, low, high)
    copies[4].wait()


RIGHT = 16
LEFT = 43


def strip_of(pair):
    lane = iota(pair[0].shape, 1)
    parts = [turned(pair[z], side + z * Z_LANES, 1) for z in range(2) for side in (RIGHT, LEFT)]
    strip = parts[3]
    for n in (2, 1, 0):
        strip = jnp.where(lane < 32 * (n + 1), parts[n], strip)
    return strip


def pack_sides(tiles):
    low = high = None
    for z in range(2):
        for n in range(19 + FIELDS):
            at = z * Z_LANES + STARTS[n]
            tile = tiles(n, z)
            up = turned(tile, at, 1)
            down = turned(tile, at + WIDTHS[n], 1)
            lane = iota(tile.shape, 1)
            low = up if low is None else jnp.where(lane >= at, up, low)
            high = down if high is None else jnp.where(lane >= at, down, high)
    return low, high


def edge_line(right, left):
    lane = iota(right.shape, 1)
    block = jnp.where(lane < 3, right, jnp.where(lane < 6, left, 0.0))
    return jnp.sum(pltpu.roll(block, 0, 1, stride=8, stride_axis=0), axis=0, keepdims=True)


def own_kernel(adj, fields, fwd, mask, index, low_own, high_own, fwd_strip, mask_strip, line):
    low, high = pack_sides(lambda n, z: adj[n, z] if n < 19 else fields[n - 19, z])
    low_own[...] = low
    high_own[...] = high
    for q in range(19):
        fwd_strip[q] = strip_of([fwd[q, z].astype(jnp.float32) for z in range(2)])
    mask_strip[...] = strip_of([mask[z].astype(jnp.float32) for z in range(2)])
    where = index[...].astype(jnp.float32)
    line[...] = jnp.broadcast_to(
        edge_line(turned(where, -125, 1), turned(where, 3, 1)), line.shape
    )


def side_kernel(got_outer, got_inner, low_own, high_own, outer, inner, adj_rim, field_rim):
    even_x = is_even("gx")
    row = iota((8, 128), 0)

    def received(tile):
        from_in = got_inner[tile]
        from_out = got_outer[tile]
        return jnp.where(even_x, from_out, from_in), jnp.where(even_x, from_in, from_out)

    for n, (up, down) in enumerate(MIRRORS):
        low, high = received(n)
        for z in range(2):
            adj_rim[up, z] = jnp.where(row < 4, turned(high, -3 * z, 0), turned(low, 1 - z, 0))
            adj_rim[down, z] = jnp.where(row < 4, turned(high, 2 - z, 0), turned(low, 5 - 3 * z, 0))
    for n in range(0, len(FLAT), 2):
        low, high = received(len(MIRRORS) + n // 2)
        for m, item in enumerate(FLAT[n : n + 2]):
            for z in range(2):
                at = 4 * m + 2 * z
                rim = jnp.where(row < 4, turned(high, -at, 0), turned(low, 6 - at, 0))
                if item < 19:
                    adj_rim[item, z] = rim
                else:
                    field_rim[item - 19, z] = rim
    low, high = pack_sides(lambda n, z: adj_rim[n, z] if n < 19 else field_rim[n - 19, z])
    low = jnp.concatenate([low_own[...], low], axis=0)
    high = jnp.concatenate([high_own[...], high], axis=0)
    even_y = is_even("gy")
    inner[...] = jnp.where(even_y, high, low)
    outer[...] = jnp.where(even_y, low, high)


def sensitivity_of(pulled, popul, velocity):
    f_even, f_odd = split_pairs(popul)
    density = popul[0]
    for n in range(9):
        density = density + f_even[n]
    even, odd = split_pairs(pulled)
    total, first, second = moments(even, odd, pulled[0])
    flux = contract(second, velocity)
    even_sum = even[0] * f_even[0]
    odd_sum = odd[0] * f_odd[0]
    for n in range(1, 9):
        even_sum = even_sum + even[n] * f_even[n]
        odd_sum = odd_sum + odd[n] * f_odd[n]
    relaxed = (
        total * (1.0 - 1.5 * dot3(velocity, velocity))
        + 3.0 * dot3(velocity, first)
        + 4.5 * dot3(velocity, flux)
    )
    half = 0.5 * relax_rate
    return (
        half * even_sum
        + (half - 1.0) * odd_sum
        + relax_rate * (popul[0] * pulled[0])
        - (relax_rate / 36.0) * (density * relaxed)
    )


def hot_rows(values, owner, slot, owners, chunk):
    top = values.astype(jnp.bfloat16).astype(jnp.float32)
    hot = iota((owners, 128), 0) == owner
    lhs = jnp.concatenate(
        [
            jnp.where(hot, top, 0.0).astype(jnp.bfloat16),
            jnp.where(hot, values - top, 0.0).astype(jnp.bfloat16),
        ],
        axis=0,
    )
    rhs = jnp.where(iota((chunk, 128), 0) == slot, 1.0, 0.0).astype(jnp.bfloat16)
    return lhs, rhs


def hot_product(lhs, rhs):
    return lax.dot_general(
        lhs, rhs, (((1,), (1,)), ((), ())), preferred_element_type=jnp.float32
    )


def split_index(index, chunk):
    if chunk & (chunk - 1):
        owner = lax.div(index, jnp.full(index.shape, chunk, index.dtype))
    else:
        owner = index >> (chunk.bit_length() - 1)
    return owner, index - owner * chunk


def main_kernel(
    owners, chunk, adj, adj_rim, fields, field_rim, fwd, mask, index,
    grid, inside, strip, field_strip, state, pulls, summed,
):
    rows = adj.shape[2]
    full = rows + 8
    for step_num in range(STEPS):
        final = step_num == STEPS - 1
        for q in range(19):
            shift_x, shift_y, shift_z = SPEEDS[q]
            if step_num == 0:
                start = [jnp.concatenate([adj[q, z], adj_rim[q, z]], axis=0) for z in range(2)]
                strip[q] = strip_of(start)
            for z in range(2):
                src = (z + shift_z) % 2
                main = start[src] if step_num == 0 else state[q, src]
                main = turned(turned(main, -shift_x, 0), -shift_y, 1)
                pulls[q, z] = main
                own = main[:rows]
                summed[q, z] = own if step_num == 0 else summed[q, z] + own
        for z in range(2):
            for t in range((rows if final else full) // 8):
                at = slice(8 * t, 8 * t + 8)
                if 8 * t < rows:
                    here = [fields[k, z, at, :] for k in range(FIELDS)]
                else:
                    here = [field_rim[k, z] for k in range(FIELDS)]
                out = collide([pulls[q, z, at, :] for q in range(19)], here[:3], here[3], here[4])
                into = inside if final else state
                for q in range(19):
                    into[q, z, at, :] = out[q]
    for k in range(FIELDS):
        field_strip[k] = strip_of(
            [jnp.concatenate([fields[k, z], field_rim[k, z]], axis=0) for z in range(2)]
        )
    column = None
    for z in range(2):
        term = sensitivity_of(
            [summed[q, z] for q in range(19)],
            [fwd[q, z].astype(jnp.float32) for q in range(19)],
            [fields[k, z] for k in range(3)],
        ) * mask[z].astype(jnp.float32)
        column = term if column is None else column + term
    lane = iota(column.shape, 1)
    column = jnp.where((lane >= 3) & (lane < 125), column * (porous_max / (LEVELS - 1)), 0.0)
    owner, slot = split_index(index[...], chunk)
    acc = None
    for x in range(0, rows, 2):
        parts = [
            hot_rows(column[r : r + 1], owner[r : r + 1], slot[r : r + 1], owners, chunk)
            for r in (x, x + 1)
        ]
        part = hot_product(
            jnp.concatenate([p[0] for p in parts], axis=1),
            jnp.concatenate([p[1] for p in parts], axis=1),
        )
        acc = part if acc is None else acc + part
    grid[...] = acc[:owners] + acc[owners:]


def strip_kernel(
    got_outer, got_inner, strip, field_strip, state, summed, pulls, field_state,
):
    full = strip.shape[1]
    rows = full - 8
    even_y = is_even("gy")
    from_in = got_inner[...]
    from_out = got_outer[...]
    low = jnp.where(even_y, from_out, from_in)
    high = jnp.where(even_y, from_in, from_out)
    lane = iota((full, 128), 1) & (Z_LANES - 1)
    at_right = (lane >= RIGHT) & (lane < RIGHT + 3)
    at_left = (lane >= LEFT - 3) & (lane < LEFT)

    def joined(n, own):
        right = turned(high, RIGHT - STARTS[n], 1)
        left = turned(low, LEFT - WIDTHS[n] - STARTS[n], 1)
        return jnp.where(at_left, left, jnp.where(at_right, right, own))

    for k in range(FIELDS):
        field_state[k] = joined(19 + k, field_strip[k])
    for step_num in range(STEPS):
        final = step_num == STEPS - 1
        for q in range(19):
            shift_x, shift_y, shift_z = SPEEDS[q]
            tile = joined(q, strip[q]) if step_num == 0 else state[q]
            tile = turned(turned(tile, -shift_x, 0), Z_LANES * (shift_z % 2) - shift_y, 1)
            own = tile[:rows]
            pulls[q] = tile
            summed[q] = own if step_num == 0 else summed[q] + own
        for t in range((rows if final else full) // 8):
            at = slice(8 * t, 8 * t + 8)
            here = [field_state[k, at, :] for k in range(FIELDS)]
            result = collide([pulls[q, at, :] for q in range(19)], here[:3], here[3], here[4])
            for q in range(19):
                state[q, at, :] = result[q]


def sum_kernel(
    owners, chunk, summed, field_strip, fwd_strip, mask_strip, line, grid_inside, after, grid
):
    rows = summed.shape[1]
    column = sensitivity_of(
        [summed[q] for q in range(19)],
        [fwd_strip[q] for q in range(19)],
        [field_strip[k, :rows, :] for k in range(3)],
    ) * mask_strip[...]
    column = (column + turned(column, Z_LANES, 1)) * (porous_max / (LEVELS - 1))
    values = edge_line(turned(column, 3 - RIGHT, 1), turned(column, 3 - LEFT, 1))
    owner, slot = split_index(line[0:1, :].astype(jnp.int32), chunk)
    acc = hot_product(*hot_rows(values, owner, slot, owners, chunk))
    grid[...] = grid_inside[...] + (acc[:owners] + acc[owners:])


def merge_kernel(state, inside, out):
    rows = inside.shape[2]
    lane = iota((rows, 128), 1)
    spot = lane & (Z_LANES - 1)
    for q in range(19):
        edge = state[q, :rows, :]
        edge = jnp.where(spot < RIGHT, edge, turned(edge, RIGHT - LEFT, 1))
        for z in range(2):
            out[q, z] = jnp.where(
                (lane >= 125) | (lane < 3), turned(edge, -RIGHT - z * Z_LANES, 1), inside[q, z]
            )


def tail_kernel(received, out, adjoint_start, owned, block, sems):
    copy_out = pltpu.make_async_copy(out, adjoint_start, sems.at[0])
    copy_out.start()
    total = jnp.sum(received[...], axis=0, keepdims=True)
    cols = block.shape[1]
    for r in range(block.shape[0]):
        block[r : r + 1, :] = turned(total, -r * cols, 1)[:, :cols]
    copy_owned = pltpu.make_async_copy(block, owned, sems.at[1])
    copy_owned.start()
    copy_owned.wait()
    copy_out.wait()


def call(kernel, out_types, args, scratch=(), flops=0, where=pltpu.VMEM, to=pltpu.VMEM):
    moved = sum(a.size * a.dtype.itemsize for a in args)
    return pl.pallas_call(
        kernel,
        out_shape=[to(shape, dtype) for shape, dtype in out_types],
        in_specs=[pl.BlockSpec(memory_space=where)] * len(args),
        out_specs=[pl.BlockSpec(memory_space=to)] * len(out_types),
        scratch_shapes=list(scratch),
        compiler_params=pltpu.CompilerParams(vmem_limit_bytes=16 << 20),
        cost_estimate=pl.CostEstimate(flops=flops, bytes_accessed=moved, transcendentals=0),
    )(*[pltpu.with_memory_space_constraint(a, where) for a in args])


def per_device(adjoint_end, forward_pop, porosity_level, fluid_mask, design_index):
    depth, tile_x, tile_y = adjoint_end.shape[1:]
    full = tile_x + 8
    gx_count = lax.axis_size("gx")
    gy_count = lax.axis_size("gy")
    owners = gx_count * gy_count
    design_cols = tile_x * gx_count // 4
    design_rows = tile_y * gy_count // 4
    chunk = design_rows * design_cols // owners
    f32 = jnp.float32
    own = ((19, depth, tile_x, tile_y), f32)
    wide = pltpu.VMEM((19, depth, full, tile_y), f32)

    outer, inner, fields, adj, fwd, mask, index = call(
        edge_kernel,
        [
            ((X_TILES, 8, tile_y), f32), ((X_TILES, 8, tile_y), f32),
            ((FIELDS, depth, tile_x, tile_y), f32), own, (forward_pop.shape, forward_pop.dtype),
            (fluid_mask.shape, fluid_mask.dtype), (design_index.shape, design_index.dtype),
        ],
        [adjoint_end, forward_pop, porosity_level, fluid_mask, design_index],
        [
            pltpu.VMEM(porosity_level.shape, porosity_level.dtype),
            pltpu.SemaphoreType.DMA((5,)),
        ],
        where=pltpu.HBM,
    )
    got_outer = lax.ppermute(outer, "gx", swap_pairs(gx_count, 1))
    got_inner = lax.ppermute(inner, "gx", swap_pairs(gx_count, 0))
    flat = ((tile_x, 128), f32)
    low_own, high_own, fwd_strip, mask_strip, line = call(
        own_kernel,
        [flat, flat, ((19, tile_x, 128), f32), flat, ((8, 128), f32)],
        [adj, fields, fwd, mask, index],
        flops=10**6,
    )
    outer, inner, adj_rim, field_rim = call(
        side_kernel,
        [
            ((full, 128), f32), ((full, 128), f32), ((19, depth, 8, tile_y), f32),
            ((FIELDS, depth, 8, tile_y), f32),
        ],
        [got_outer, got_inner, low_own, high_own],
    )
    got_outer = lax.ppermute(outer, "gy", swap_pairs(gy_count, 1))
    got_inner = lax.ppermute(inner, "gy", swap_pairs(gy_count, 0))
    grid, inside, strip, field_strip = call(
        lambda *refs: main_kernel(owners, chunk, *refs),
        [((owners, chunk), f32), own, ((19, full, 128), f32), ((FIELDS, full, 128), f32)],
        [adj, adj_rim, fields, field_rim, fwd, mask, index],
        [wide, wide, pltpu.VMEM(*own)],
        flops=10**6,
    )
    state, summed = call(
        strip_kernel,
        [((19, full, 128), f32), ((19, tile_x, 128), f32)],
        [got_outer, got_inner, strip, field_strip],
        [pltpu.VMEM((19, full, 128), f32), pltpu.VMEM((FIELDS, full, 128), f32)],
    )
    (out,) = call(merge_kernel, [own], [state, inside])
    (grid,) = call(
        lambda *refs: sum_kernel(owners, chunk, *refs),
        [((owners, chunk), f32)],
        [summed, field_strip, fwd_strip, mask_strip, line, grid, out],
    )
    received = lax.all_to_all(
        grid.reshape(owners, 1, chunk), BOTH, split_axis=0, concat_axis=0, tiled=True
    )
    block = ((design_rows // owners, design_cols), f32)
    return tuple(
        call(
            tail_kernel,
            [own, block],
            [received.reshape(owners, chunk), out],
            [pltpu.VMEM(*block), pltpu.SemaphoreType.DMA((2,))],
            to=pltpu.HBM,
        )
    )


def solution(mesh):
    in_specs = (
        P(None, None, "gx", "gy"),
        P(None, None, "gx", "gy"),
        P(None, "gx", "gy"),
        P(None, "gx", "gy"),
        P("gx", "gy"),
    )
    out_specs = (P(None, None, "gx", "gy"), P(("gx", "gy"), None))
    return jax.shard_map(
        per_device, mesh=mesh, in_specs=in_specs, out_specs=out_specs, check_vma=False
    )
```

```python
import jax
import jax.numpy as jnp
from jax import lax
from jax.experimental import pallas as pl
from jax.experimental.pallas import tpu as pltpu
from jax.sharding import PartitionSpec as P

STEPS = 3
LEVELS = 8
BOTH = ("gx", "gy")
FIELDS = 5

relax_rate = 1.25
porous_max = 0.5


def lattice_table():
    speeds = [[0, 0, 0]]
    for axis_index in range(3):
        for sign_value in (1, -1):
            vector_row = [0, 0, 0]
            vector_row[axis_index] = sign_value
            speeds.append(vector_row)
    for plane_pair in ((0, 1), (0, 2), (1, 2)):
        for first_sign in (1, -1):
            for second_sign in (1, -1):
                vector_row = [0, 0, 0]
                vector_row[plane_pair[0]] = first_sign
                vector_row[plane_pair[1]] = second_sign
                speeds.append(vector_row)
    return speeds


SPEEDS = lattice_table()
PAIRS = ((1, 2), (3, 4), (5, 6), (7, 10), (8, 9), (11, 14), (12, 13), (15, 18), (16, 17))

Z_LANES = 64
WIDTHS = [3 if SPEEDS[q][1] != 0 else 2 for q in range(19)] + [2] * FIELDS
DEEP = [n for n in range(19) if WIDTHS[n] == 3]
THIN = [n for n in range(19 + FIELDS) if WIDTHS[n] == 2]
STARTS = [
    3 * DEEP.index(n) if n in DEEP else Z_LANES // 2 + 2 * THIN.index(n) for n in range(19 + FIELDS)
]


def swap_pairs(count, parity):
    pairs = []
    for i in range(count):
        j = (i ^ 1) if parity == 0 else ((i - 1) ^ 1) + 1
        if 0 <= j < count:
            pairs.append((i, j))
    return pairs


def is_even(axis):
    return lax.rem(lax.axis_index(axis), 2) == 0


def iota(shape, dim):
    return lax.broadcasted_iota(jnp.int32, shape, dim)


def moments(even, odd, rest):
    e_x, e_y, e_z, e_xy, e_xw, e_xz, e_xv, e_yz, e_yv = even
    o_x, o_y, o_z, o_xy, o_xw, o_xz, o_xv, o_yz, o_yv = odd
    d_xy = e_xy + e_xw
    d_xz = e_xz + e_xv
    d_yz = e_yz + e_yv
    s_xx = 2.0 * e_x + (d_xy + d_xz)
    s_yy = 2.0 * e_y + (d_xy + d_yz)
    s_zz = 2.0 * e_z + (d_xz + d_yz)
    s_xy = e_xy - e_xw
    s_xz = e_xz - e_xv
    s_yz = e_yz - e_yv
    total = 12.0 * rest + 2.0 * ((e_x + e_y) + e_z) + ((d_xy + d_xz) + d_yz)
    v_x = 2.0 * o_x + ((o_xy + o_xw) + (o_xz + o_xv))
    v_y = 2.0 * o_y + ((o_xy - o_xw) + (o_yz + o_yv))
    v_z = 2.0 * o_z + ((o_xz - o_xv) + (o_yz - o_yv))
    return total, (v_x, v_y, v_z), ((s_xx, s_xy, s_xz), (s_xy, s_yy, s_yz), (s_xz, s_yz, s_zz))


def contract(second, velocity):
    return [
        second[k][0] * velocity[0] + second[k][1] * velocity[1] + second[k][2] * velocity[2]
        for k in range(3)
    ]


def dot3(a, b):
    return a[0] * b[0] + a[1] * b[1] + a[2] * b[2]


def split_pairs(pulled):
    even = [pulled[i] + pulled[j] for i, j in PAIRS]
    odd = [pulled[i] - pulled[j] for i, j in PAIRS]
    return even, odd


def collide(pulled, velocity, keep, porosity):
    even, odd = split_pairs(pulled)
    total, first, second = moments(even, odd, pulled[0])
    flux = contract(second, velocity)
    twice = dot3(velocity, flux)
    gain = keep * (relax_rate / 36.0)
    stay = keep * (1.0 - relax_rate)
    base = gain * (total * (1.0 + 1.5 * dot3(velocity, velocity)) - 4.5 * twice)
    turn = [gain * (3.0 * (first[k] - velocity[k] * total) + 9.0 * flux[k]) for k in range(3)]
    both = 0.5 * (stay + porosity)
    diff = 0.5 * (stay - porosity)
    results = [None] * 19
    results[0] = (stay + porosity) * pulled[0] + base
    for n, (i, j) in enumerate(PAIRS):
        along = None
        for k in range(3):
            if SPEEDS[i][k] == 1:
                along = turn[k] if along is None else along + turn[k]
            elif SPEEDS[i][k] == -1:
                along = along - turn[k]
        same = both * even[n] + base
        swing = diff * odd[n] + along
        results[i] = same + swing
        results[j] = same - swing
    return results


MIRRORS = [
    (q, SPEEDS.index([-SPEEDS[q][0], SPEEDS[q][1], SPEEDS[q][2]]))
    for q in range(19)
    if SPEEDS[q][0] == 1
]
FLAT = [q for q in range(19) if SPEEDS[q][0] == 0] + list(range(19, 19 + FIELDS))
X_TILES = len(MIRRORS) + (len(FLAT) + 1) // 2


def turned(tile, shift, axis):
    shift = shift % tile.shape[axis]
    return tile if shift == 0 else pltpu.roll(tile, shift, axis)


def edge_kernel(
    adj_hbm, fwd_hbm, level_hbm, mask_hbm, index_hbm,
    outer, inner, fields, adj, fwd, mask, index, level, sems,
):
    copies = [
        pltpu.make_async_copy(src, dst, sems.at[n])
        for n, (src, dst) in enumerate(
            (
                (fwd_hbm, fwd), (mask_hbm, mask), (level_hbm, level),
                (adj_hbm, adj), (index_hbm, index),
            )
        )
    ]
    for copy in copies:
        copy.start()
    for copy in copies[:3]:
        copy.wait()
    depth, rows = adj.shape[1], adj.shape[2]
    for z in range(depth):
        popul = [fwd[q, z].astype(jnp.float32) for q in range(19)]
        even, odd = split_pairs(popul)
        density = popul[0]
        for n in range(9):
            density = density + even[n]
        o_x, o_y, o_z, o_xy, o_xw, o_xz, o_xv, o_yz, o_yv = odd
        per_mass = 1.0 / density
        fields[0, z] = (o_x + ((o_xy + o_xw) + (o_xz + o_xv))) * per_mass
        fields[1, z] = (o_y + ((o_xy - o_xw) + (o_yz + o_yv))) * per_mass
        fields[2, z] = (o_z + ((o_xz - o_xv) + (o_yz - o_yv))) * per_mass
        porosity = jnp.where(
            mask[z] == 1, level[z].astype(jnp.float32) * (porous_max / (LEVELS - 1)), 1.0
        )
        fields[3, z] = 1.0 - porosity
        fields[4, z] = porosity
    copies[3].wait()
    even_x = is_even("gx")
    row = iota((8, 128), 0)

    def top(n, z):
        return adj[n, z, 0:8, :] if n < 19 else fields[n - 19, z, 0:8, :]

    def bottom(n, z):
        at = slice(rows - 8, rows)
        return adj[n, z, at, :] if n < 19 else fields[n - 19, z, at, :]

    for n, (up, down) in enumerate(MIRRORS):
        low = jnp.where(row < 3, top(up, 0), turned(top(up, 1), 3, 0))
        low = jnp.where(row < 6, low, turned(top(down, 0), 6, 0))
        low = jnp.where(row < 7, low, turned(top(down, 1), 7, 0))
        high = jnp.where(row < 3, turned(bottom(down, 0), 3, 0), turned(bottom(down, 1), 6, 0))
        high = jnp.where(row < 6, high, turned(bottom(up, 0), 7, 0))
        high = jnp.where(row < 7, high, bottom(up, 1))
        inner[n] = jnp.where(even_x, high, low)
        outer[n] = jnp.where(even_x, low, high)
    for n in range(0, len(FLAT), 2):
        low = high = None
        for m, item in enumerate(FLAT[n : n + 2]):
            for z in range(depth):
                at = 4 * m + 2 * z
                up = turned(top(item, z), at, 0)
                down = turned(bottom(item, z), at + 2, 0)
                low = up if low is None else jnp.where(row < at, low, up)
                high = down if high is None else jnp.where(row < at, high, down)
        tile = len(MIRRORS) + n // 2
        inner[tile] = jnp.where(even_x, high, low)
        outer[tile] = jnp.where(even_x, low, high)
    copies[4].wait()


RIGHT = 16
LEFT = 51


def strip_of(pair):
    lane = iota(pair[0].shape, 1)
    parts = [turned(pair[z], side + z * Z_LANES, 1) for z in range(2) for side in (RIGHT, LEFT)]
    strip = parts[3]
    for n in (2, 1, 0):
        strip = jnp.where(lane < 32 * (n + 1), parts[n], strip)
    return strip


def pack_sides(tiles):
    low = high = None
    for z in range(2):
        for n in DEEP + THIN:
            at = z * Z_LANES + STARTS[n]
            tile = tiles(n, z)
            up = turned(tile, at, 1)
            down = turned(tile, at + WIDTHS[n], 1)
            lane = iota(tile.shape, 1)
            low = up if low is None else jnp.where(lane >= at, up, low)
            high = down if high is None else jnp.where(lane >= at, down, high)
    return low, high


def edge_line(right, left):
    lane = iota(right.shape, 1)
    block = jnp.where(lane < 3, right, jnp.where(lane < 6, left, 0.0))
    return jnp.sum(pltpu.roll(block, 0, 1, stride=8, stride_axis=0), axis=0, keepdims=True)


def own_kernel(adj, fields, fwd, mask, index, low_own, high_own, fwd_strip, mask_strip, line):
    low, high = pack_sides(lambda n, z: adj[n, z] if n < 19 else fields[n - 19, z])
    low_own[...] = low
    high_own[...] = high
    for q in range(19):
        fwd_strip[q] = strip_of([fwd[q, z].astype(jnp.float32) for z in range(2)])
    mask_strip[...] = strip_of([mask[z].astype(jnp.float32) for z in range(2)])
    where = index[...].astype(jnp.float32)
    line[...] = jnp.broadcast_to(
        edge_line(turned(where, -125, 1), turned(where, 3, 1)), line.shape
    )


def side_kernel(got_outer, got_inner, low_own, high_own, outer, inner, adj_rim, field_rim):
    even_x = is_even("gx")
    row = iota((8, 128), 0)

    def received(tile):
        from_in = got_inner[tile]
        from_out = got_outer[tile]
        return jnp.where(even_x, from_out, from_in), jnp.where(even_x, from_in, from_out)

    for n, (up, down) in enumerate(MIRRORS):
        low, high = received(n)
        for z in range(2):
            adj_rim[up, z] = jnp.where(row < 4, turned(high, -3 * z, 0), turned(low, 1 - z, 0))
            adj_rim[down, z] = jnp.where(row < 4, turned(high, 2 - z, 0), turned(low, 5 - 3 * z, 0))
    for n in range(0, len(FLAT), 2):
        low, high = received(len(MIRRORS) + n // 2)
        for m, item in enumerate(FLAT[n : n + 2]):
            for z in range(2):
                at = 4 * m + 2 * z
                rim = jnp.where(row < 4, turned(high, -at, 0), turned(low, 6 - at, 0))
                if item < 19:
                    adj_rim[item, z] = rim
                else:
                    field_rim[item - 19, z] = rim
    low, high = pack_sides(lambda n, z: adj_rim[n, z] if n < 19 else field_rim[n - 19, z])
    low = jnp.concatenate([low_own[...], low], axis=0)
    high = jnp.concatenate([high_own[...], high], axis=0)
    even_y = is_even("gy")
    inner[...] = jnp.where(even_y, high, low)
    outer[...] = jnp.where(even_y, low, high)


def sensitivity_of(pulled, popul, velocity):
    f_even, f_odd = split_pairs(popul)
    density = popul[0]
    for n in range(9):
        density = density + f_even[n]
    even, odd = split_pairs(pulled)
    total, first, second = moments(even, odd, pulled[0])
    flux = contract(second, velocity)
    even_sum = even[0] * f_even[0]
    odd_sum = odd[0] * f_odd[0]
    for n in range(1, 9):
        even_sum = even_sum + even[n] * f_even[n]
        odd_sum = odd_sum + odd[n] * f_odd[n]
    relaxed = (
        total * (1.0 - 1.5 * dot3(velocity, velocity))
        + 3.0 * dot3(velocity, first)
        + 4.5 * dot3(velocity, flux)
    )
    half = 0.5 * relax_rate
    return (
        half * even_sum
        + (half - 1.0) * odd_sum
        + relax_rate * (popul[0] * pulled[0])
        - (relax_rate / 36.0) * (density * relaxed)
    )


def hot_rows(values, owner, slot, owners, chunk):
    top = values.astype(jnp.bfloat16).astype(jnp.float32)
    hot = iota((owners, 128), 0) == owner
    lhs = jnp.concatenate(
        [
            jnp.where(hot, top, 0.0).astype(jnp.bfloat16),
            jnp.where(hot, values - top, 0.0).astype(jnp.bfloat16),
        ],
        axis=0,
    )
    rhs = jnp.where(iota((chunk, 128), 0) == slot, 1.0, 0.0).astype(jnp.bfloat16)
    return lhs, rhs


def hot_product(lhs, rhs):
    return lax.dot_general(
        lhs, rhs, (((1,), (1,)), ((), ())), preferred_element_type=jnp.float32
    )


def split_index(index, chunk):
    if chunk & (chunk - 1):
        owner = lax.div(index, jnp.full(index.shape, chunk, index.dtype))
    else:
        owner = index >> (chunk.bit_length() - 1)
    return owner, index - owner * chunk


def main_kernel(
    owners, chunk, adj, adj_rim, fields, field_rim, fwd, mask, index,
    grid, inside, strip, field_strip, state, pulls, summed,
):
    rows = adj.shape[2]
    full = rows + 8
    for step_num in range(STEPS):
        final = step_num == STEPS - 1
        for q in range(19):
            shift_x, shift_y, shift_z = SPEEDS[q]
            if step_num == 0:
                start = [jnp.concatenate([adj[q, z], adj_rim[q, z]], axis=0) for z in range(2)]
            both = []
            for z in range(2):
                src = (z + shift_z) % 2
                main = start[src] if step_num == 0 else state[q, src]
                main = turned(turned(main, -shift_x, 0), -shift_y, 1)
                pulls[q, z] = main
                both.append(main)
                own = main[:rows]
                summed[q, z] = own if step_num == 0 else summed[q, z] + own
            if step_num == 0:
                strip[q] = strip_of(both)
        for z in range(2):
            for t in range((rows if final else full) // 8):
                at = slice(8 * t, 8 * t + 8)
                if 8 * t < rows:
                    here = [fields[k, z, at, :] for k in range(FIELDS)]
                else:
                    here = [field_rim[k, z] for k in range(FIELDS)]
                out = collide([pulls[q, z, at, :] for q in range(19)], here[:3], here[3], here[4])
                into = inside if final else state
                for q in range(19):
                    into[q, z, at, :] = out[q]
    for k in range(FIELDS):
        field_strip[k] = strip_of(
            [jnp.concatenate([fields[k, z], field_rim[k, z]], axis=0) for z in range(2)]
        )
    column = None
    for z in range(2):
        term = sensitivity_of(
            [summed[q, z] for q in range(19)],
            [fwd[q, z].astype(jnp.float32) for q in range(19)],
            [fields[k, z] for k in range(3)],
        ) * mask[z].astype(jnp.float32)
        column = term if column is None else column + term
    lane = iota(column.shape, 1)
    column = jnp.where((lane >= 3) & (lane < 125), column * (porous_max / (LEVELS - 1)), 0.0)
    owner, slot = split_index(index[...], chunk)
    acc = None
    for x in range(0, rows, 2):
        parts = [
            hot_rows(column[r : r + 1], owner[r : r + 1], slot[r : r + 1], owners, chunk)
            for r in (x, x + 1)
        ]
        part = hot_product(
            jnp.concatenate([p[0] for p in parts], axis=1),
            jnp.concatenate([p[1] for p in parts], axis=1),
        )
        acc = part if acc is None else acc + part
    grid[...] = acc[:owners] + acc[owners:]


def strip_kernel(
    got_outer, got_inner, strip, field_strip, fwd_strip, mask_strip, inside,
    column, out, state, summed, pulls, field_state,
):
    full = strip.shape[1]
    rows = full - 8
    even_y = is_even("gy")
    from_in = got_inner[...]
    from_out = got_outer[...]
    low = jnp.where(even_y, from_out, from_in)
    high = jnp.where(even_y, from_in, from_out)
    lane = iota((full, 128), 1) & (Z_LANES - 1)
    half = Z_LANES // 2
    deep = jnp.where(lane < half, high, turned(low, LEFT - 3 - RIGHT, 1))
    thin = jnp.where(lane >= half, high, turned(low, LEFT - 2 - RIGHT, 1))
    moved = {
        (width, shift): turned(both, -shift, 0)
        for width, both in ((3, deep), (2, thin))
        for shift in (-1, 0, 1)
    }

    def joined(n, own, shift_x=0, shift_y=0, shift_z=0):
        width = WIDTHS[n]
        turn = RIGHT - STARTS[n] - shift_y + Z_LANES * (shift_z % 2)
        right = RIGHT - shift_y
        left = LEFT - width - shift_y
        inside = ((lane >= right) & (lane < right + width)) | ((lane >= left) & (lane < left + width))
        return jnp.where(inside, turned(moved[width, shift_x], turn, 1), own)

    for k in range(FIELDS):
        field_state[k] = joined(19 + k, field_strip[k])
    for step_num in range(STEPS):
        final = step_num == STEPS - 1
        for q in range(19):
            shift_x, shift_y, shift_z = SPEEDS[q]
            if step_num == 0:
                tile = joined(q, strip[q], shift_x, shift_y, shift_z)
            else:
                tile = turned(state[q], -shift_x, 0)
                tile = turned(tile, Z_LANES * (shift_z % 2) - shift_y, 1)
            own = tile[:rows]
            pulls[q] = tile
            summed[q] = own if step_num == 0 else summed[q] + own
        for t in range((rows if final else full) // 8):
            at = slice(8 * t, 8 * t + 8)
            here = [field_state[k, at, :] for k in range(FIELDS)]
            result = collide([pulls[q, at, :] for q in range(19)], here[:3], here[3], here[4])
            for q in range(19):
                state[q, at, :] = result[q]
    term = sensitivity_of(
        [summed[q] for q in range(19)],
        [fwd_strip[q] for q in range(19)],
        [field_strip[k, :rows, :] for k in range(3)],
    ) * mask_strip[...]
    column[...] = (term + turned(term, Z_LANES, 1)) * (porous_max / (LEVELS - 1))
    own_lane = iota((rows, 128), 1)
    spot = own_lane & (Z_LANES - 1)
    for q in range(19):
        edge = state[q, :rows, :]
        edge = jnp.where(spot < RIGHT, edge, turned(edge, RIGHT - LEFT, 1))
        for z in range(2):
            out[q, z] = jnp.where(
                (own_lane >= 125) | (own_lane < 3),
                turned(edge, -RIGHT - z * Z_LANES, 1),
                inside[q, z],
            )


def sum_kernel(owners, chunk, column, line, grid_inside, after, grid):
    values = edge_line(turned(column[...], 3 - RIGHT, 1), turned(column[...], 3 - LEFT, 1))
    owner, slot = split_index(line[0:1, :].astype(jnp.int32), chunk)
    acc = hot_product(*hot_rows(values, owner, slot, owners, chunk))
    grid[...] = grid_inside[...] + (acc[:owners] + acc[owners:])


def tail_kernel(received, out, adjoint_start, owned, block, sems):
    copy_out = pltpu.make_async_copy(out, adjoint_start, sems.at[0])
    copy_out.start()
    total = jnp.sum(received[...], axis=0, keepdims=True)
    cols = block.shape[1]
    for r in range(block.shape[0]):
        block[r : r + 1, :] = turned(total, -r * cols, 1)[:, :cols]
    copy_owned = pltpu.make_async_copy(block, owned, sems.at[1])
    copy_owned.start()
    copy_owned.wait()
    copy_out.wait()


def call(kernel, out_types, args, scratch=(), flops=0, where=pltpu.VMEM, to=pltpu.VMEM):
    moved = sum(a.size * a.dtype.itemsize for a in args)
    return pl.pallas_call(
        kernel,
        out_shape=[to(shape, dtype) for shape, dtype in out_types],
        in_specs=[pl.BlockSpec(memory_space=where)] * len(args),
        out_specs=[pl.BlockSpec(memory_space=to)] * len(out_types),
        scratch_shapes=list(scratch),
        compiler_params=pltpu.CompilerParams(vmem_limit_bytes=16 << 20),
        cost_estimate=pl.CostEstimate(flops=flops, bytes_accessed=moved, transcendentals=0),
    )(*[pltpu.with_memory_space_constraint(a, where) for a in args])


def per_device(adjoint_end, forward_pop, porosity_level, fluid_mask, design_index):
    depth, tile_x, tile_y = adjoint_end.shape[1:]
    full = tile_x + 8
    gx_count = lax.axis_size("gx")
    gy_count = lax.axis_size("gy")
    owners = gx_count * gy_count
    design_cols = tile_x * gx_count // 4
    design_rows = tile_y * gy_count // 4
    chunk = design_rows * design_cols // owners
    f32 = jnp.float32
    own = ((19, depth, tile_x, tile_y), f32)
    wide = pltpu.VMEM((19, depth, full, tile_y), f32)

    outer, inner, fields, adj, fwd, mask, index = call(
        edge_kernel,
        [
            ((X_TILES, 8, tile_y), f32), ((X_TILES, 8, tile_y), f32),
            ((FIELDS, depth, tile_x, tile_y), f32), own, (forward_pop.shape, forward_pop.dtype),
            (fluid_mask.shape, fluid_mask.dtype), (design_index.shape, design_index.dtype),
        ],
        [adjoint_end, forward_pop, porosity_level, fluid_mask, design_index],
        [
            pltpu.VMEM(porosity_level.shape, porosity_level.dtype),
            pltpu.SemaphoreType.DMA((5,)),
        ],
        where=pltpu.HBM,
    )
    got_outer = lax.ppermute(outer, "gx", swap_pairs(gx_count, 1))
    got_inner = lax.ppermute(inner, "gx", swap_pairs(gx_count, 0))
    flat = ((tile_x, 128), f32)
    low_own, high_own, fwd_strip, mask_strip, line = call(
        own_kernel,
        [flat, flat, ((19, tile_x, 128), f32), flat, ((8, 128), f32)],
        [adj, fields, fwd, mask, index],
        flops=10**6,
    )
    outer, inner, adj_rim, field_rim = call(
        side_kernel,
        [
            ((full, 128), f32), ((full, 128), f32), ((19, depth, 8, tile_y), f32),
            ((FIELDS, depth, 8, tile_y), f32),
        ],
        [got_outer, got_inner, low_own, high_own],
    )
    got_outer = lax.ppermute(outer, "gy", swap_pairs(gy_count, 1))
    got_inner = lax.ppermute(inner, "gy", swap_pairs(gy_count, 0))
    grid, inside, strip, field_strip = call(
        lambda *refs: main_kernel(owners, chunk, *refs),
        [((owners, chunk), f32), own, ((19, full, 128), f32), ((FIELDS, full, 128), f32)],
        [adj, adj_rim, fields, field_rim, fwd, mask, index],
        [wide, wide, pltpu.VMEM(*own)],
        flops=10**6,
    )
    column, out = call(
        strip_kernel,
        [flat, own],
        [got_outer, got_inner, strip, field_strip, fwd_strip, mask_strip, inside],
        [
            pltpu.VMEM((19, full, 128), f32), pltpu.VMEM((19, tile_x, 128), f32),
            pltpu.VMEM((19, full, 128), f32), pltpu.VMEM((FIELDS, full, 128), f32),
        ],
    )
    (grid,) = call(
        lambda *refs: sum_kernel(owners, chunk, *refs),
        [((owners, chunk), f32)],
        [column, line, grid, out],
    )
    received = lax.all_to_all(
        grid.reshape(owners, 1, chunk), BOTH, split_axis=0, concat_axis=0, tiled=True
    )
    block = ((design_rows // owners, design_cols), f32)
    return tuple(
        call(
            tail_kernel,
            [own, block],
            [received.reshape(owners, chunk), out],
            [pltpu.VMEM(*block), pltpu.SemaphoreType.DMA((2,))],
            to=pltpu.HBM,
        )
    )


def solution(mesh):
    in_specs = (
        P(None, None, "gx", "gy"),
        P(None, None, "gx", "gy"),
        P(None, "gx", "gy"),
        P(None, "gx", "gy"),
        P("gx", "gy"),
    )
    out_specs = (P(None, None, "gx", "gy"), P(("gx", "gy"), None))
    return jax.shard_map(
        per_device, mesh=mesh, in_specs=in_specs, out_specs=out_specs, check_vma=False
    )
```

```python
import jax
import jax.numpy as jnp
from jax import lax
from jax.experimental import pallas as pl
from jax.experimental.pallas import tpu as pltpu
from jax.sharding import PartitionSpec as P

STEPS = 3
LEVELS = 8
BOTH = ("gx", "gy")
FIELDS = 5

relax_rate = 1.25
porous_max = 0.5


def lattice_table():
    speeds = [[0, 0, 0]]
    for axis_index in range(3):
        for sign_value in (1, -1):
            vector_row = [0, 0, 0]
            vector_row[axis_index] = sign_value
            speeds.append(vector_row)
    for plane_pair in ((0, 1), (0, 2), (1, 2)):
        for first_sign in (1, -1):
            for second_sign in (1, -1):
                vector_row = [0, 0, 0]
                vector_row[plane_pair[0]] = first_sign
                vector_row[plane_pair[1]] = second_sign
                speeds.append(vector_row)
    return speeds


SPEEDS = lattice_table()
PAIRS = ((1, 2), (3, 4), (5, 6), (7, 10), (8, 9), (11, 14), (12, 13), (15, 18), (16, 17))

Z_LANES = 64
WIDTHS = [3 if SPEEDS[q][1] != 0 else 2 for q in range(19)] + [2] * FIELDS
DEEP = [n for n in range(19) if WIDTHS[n] == 3]
THIN = [n for n in range(19 + FIELDS) if WIDTHS[n] == 2]
STARTS = [
    3 * DEEP.index(n) if n in DEEP else Z_LANES // 2 + 2 * THIN.index(n) for n in range(19 + FIELDS)
]


def swap_pairs(count, parity):
    pairs = []
    for i in range(count):
        j = (i ^ 1) if parity == 0 else ((i - 1) ^ 1) + 1
        if 0 <= j < count:
            pairs.append((i, j))
    return pairs


def is_even(axis):
    return lax.rem(lax.axis_index(axis), 2) == 0


def iota(shape, dim):
    return lax.broadcasted_iota(jnp.int32, shape, dim)


def moments(even, odd, rest):
    e_x, e_y, e_z, e_xy, e_xw, e_xz, e_xv, e_yz, e_yv = even
    o_x, o_y, o_z, o_xy, o_xw, o_xz, o_xv, o_yz, o_yv = odd
    d_xy = e_xy + e_xw
    d_xz = e_xz + e_xv
    d_yz = e_yz + e_yv
    s_xx = 2.0 * e_x + (d_xy + d_xz)
    s_yy = 2.0 * e_y + (d_xy + d_yz)
    s_zz = 2.0 * e_z + (d_xz + d_yz)
    s_xy = e_xy - e_xw
    s_xz = e_xz - e_xv
    s_yz = e_yz - e_yv
    total = 12.0 * rest + 2.0 * ((e_x + e_y) + e_z) + ((d_xy + d_xz) + d_yz)
    v_x = 2.0 * o_x + ((o_xy + o_xw) + (o_xz + o_xv))
    v_y = 2.0 * o_y + ((o_xy - o_xw) + (o_yz + o_yv))
    v_z = 2.0 * o_z + ((o_xz - o_xv) + (o_yz - o_yv))
    return total, (v_x, v_y, v_z), ((s_xx, s_xy, s_xz), (s_xy, s_yy, s_yz), (s_xz, s_yz, s_zz))


def contract(second, velocity):
    return [
        second[k][0] * velocity[0] + second[k][1] * velocity[1] + second[k][2] * velocity[2]
        for k in range(3)
    ]


def dot3(a, b):
    return a[0] * b[0] + a[1] * b[1] + a[2] * b[2]


def split_pairs(pulled):
    even = [pulled[i] + pulled[j] for i, j in PAIRS]
    odd = [pulled[i] - pulled[j] for i, j in PAIRS]
    return even, odd


def collide(pulled, velocity, keep, porosity):
    even, odd = split_pairs(pulled)
    total, first, second = moments(even, odd, pulled[0])
    flux = contract(second, velocity)
    twice = dot3(velocity, flux)
    gain = keep * (relax_rate / 36.0)
    stay = keep * (1.0 - relax_rate)
    base = gain * (total * (1.0 + 1.5 * dot3(velocity, velocity)) - 4.5 * twice)
    turn = [gain * (3.0 * (first[k] - velocity[k] * total) + 9.0 * flux[k]) for k in range(3)]
    both = 0.5 * (stay + porosity)
    diff = 0.5 * (stay - porosity)
    results = [None] * 19
    results[0] = (stay + porosity) * pulled[0] + base
    for n, (i, j) in enumerate(PAIRS):
        along = None
        for k in range(3):
            if SPEEDS[i][k] == 1:
                along = turn[k] if along is None else along + turn[k]
            elif SPEEDS[i][k] == -1:
                along = along - turn[k]
        same = both * even[n] + base
        swing = diff * odd[n] + along
        results[i] = same + swing
        results[j] = same - swing
    return results


MIRRORS = [
    (q, SPEEDS.index([-SPEEDS[q][0], SPEEDS[q][1], SPEEDS[q][2]]))
    for q in range(19)
    if SPEEDS[q][0] == 1
]
FLAT = [q for q in range(19) if SPEEDS[q][0] == 0] + list(range(19, 19 + FIELDS))
X_TILES = len(MIRRORS) + (len(FLAT) + 1) // 2


def turned(tile, shift, axis):
    shift = shift % tile.shape[axis]
    return tile if shift == 0 else pltpu.roll(tile, shift, axis)


def flow_fields(popul, level, mask):
    even, odd = split_pairs(popul)
    density = popul[0]
    for n in range(9):
        density = density + even[n]
    o_x, o_y, o_z, o_xy, o_xw, o_xz, o_xv, o_yz, o_yv = odd
    per_mass = 1.0 / density
    porosity = jnp.where(mask == 1, level.astype(jnp.float32) * (porous_max / (LEVELS - 1)), 1.0)
    return (
        (o_x + ((o_xy + o_xw) + (o_xz + o_xv))) * per_mass,
        (o_y + ((o_xy - o_xw) + (o_yz + o_yv))) * per_mass,
        (o_z + ((o_xz - o_xv) + (o_yz - o_yv))) * per_mass,
        1.0 - porosity,
        porosity,
    )


def edge_kernel(
    adj_hbm, fwd_hbm, level_hbm, mask_hbm, outer, inner, adj, fwd_top, fwd_end, level, mask,
    fields, sems,
):
    rows = adj_hbm.shape[2]
    copies = [
        pltpu.make_async_copy(src, dst, sems.at[n])
        for n, (src, dst) in enumerate(
            (
                (fwd_hbm.at[:, :, pl.ds(0, 2), :], fwd_top),
                (fwd_hbm.at[:, :, pl.ds(rows - 2, 2), :], fwd_end),
                (mask_hbm, mask),
                (level_hbm, level),
                (adj_hbm.at[:, :, pl.ds(0, 3), :], adj.at[:, :, pl.ds(0, 3), :]),
                (adj_hbm.at[:, :, pl.ds(rows - 3, 3), :], adj.at[:, :, pl.ds(5, 3), :]),
            )
        )
    ]
    for copy in copies:
        copy.start()
    for copy in copies[:4]:
        copy.wait()
    for z in range(2):
        for fwd, at, to in ((fwd_top, 0, 0), (fwd_end, rows - 2, 6)):
            values = flow_fields(
                [fwd[q, z].astype(jnp.float32) for q in range(19)],
                level[z, at : at + 2, :],
                mask[z, at : at + 2, :],
            )
            for k in range(FIELDS):
                fields[k, z, to : to + 2, :] = values[k]
    for copy in copies[4:]:
        copy.wait()
    even_x = is_even("gx")
    row = iota((8, 128), 0)

    def tile_of(n, z):
        return adj[n, z] if n < 19 else fields[n - 19, z]

    for n, (up, down) in enumerate(MIRRORS):
        low = jnp.where(row < 3, tile_of(up, 0), turned(tile_of(up, 1), 3, 0))
        low = jnp.where(row < 6, low, turned(tile_of(down, 0), 6, 0))
        low = jnp.where(row < 7, low, turned(tile_of(down, 1), 7, 0))
        high = jnp.where(row < 3, turned(tile_of(down, 0), 3, 0), turned(tile_of(down, 1), 6, 0))
        high = jnp.where(row < 6, high, turned(tile_of(up, 0), 7, 0))
        high = jnp.where(row < 7, high, tile_of(up, 1))
        inner[n] = jnp.where(even_x, high, low)
        outer[n] = jnp.where(even_x, low, high)
    for n in range(0, len(FLAT), 2):
        low = high = None
        for m, item in enumerate(FLAT[n : n + 2]):
            for z in range(2):
                at = 4 * m + 2 * z
                up = turned(tile_of(item, z), at, 0)
                down = turned(tile_of(item, z), at + 2, 0)
                low = up if low is None else jnp.where(row < at, low, up)
                high = down if high is None else jnp.where(row < at, high, down)
        tile = len(MIRRORS) + n // 2
        inner[tile] = jnp.where(even_x, high, low)
        outer[tile] = jnp.where(even_x, low, high)


RIGHT = 16
LEFT = 51


def strip_of(pair):
    lane = iota(pair[0].shape, 1)
    parts = [turned(pair[z], side + z * Z_LANES, 1) for z in range(2) for side in (RIGHT, LEFT)]
    strip = parts[3]
    for n in (2, 1, 0):
        strip = jnp.where(lane < 32 * (n + 1), parts[n], strip)
    return strip


def pack_sides(tiles):
    low = high = None
    for z in range(2):
        for n in DEEP + THIN:
            at = z * Z_LANES + STARTS[n]
            tile = tiles(n, z)
            up = turned(tile, at, 1)
            down = turned(tile, at + WIDTHS[n], 1)
            lane = iota(tile.shape, 1)
            low = up if low is None else jnp.where(lane >= at, up, low)
            high = down if high is None else jnp.where(lane >= at, down, high)
    return low, high


def edge_line(right, left):
    lane = iota(right.shape, 1)
    block = jnp.where(lane < 3, right, jnp.where(lane < 6, left, 0.0))
    return jnp.sum(pltpu.roll(block, 0, 1, stride=8, stride_axis=0), axis=0, keepdims=True)


def own_kernel(
    adj_hbm, fwd_hbm, level_hbm, mask_hbm, index_hbm, after,
    adj, fwd, mask, index, fields, low_own, high_own, fwd_strip, mask_strip, line, level, sems,
):
    copies = [
        pltpu.make_async_copy(src, dst, sems.at[n])
        for n, (src, dst) in enumerate(
            (
                (fwd_hbm, fwd), (mask_hbm, mask), (level_hbm, level), (index_hbm, index),
                (adj_hbm, adj),
            )
        )
    ]
    for copy in copies:
        copy.start()
    for copy in copies[:4]:
        copy.wait()
    for z in range(2):
        values = flow_fields(
            [fwd[q, z].astype(jnp.float32) for q in range(19)], level[z], mask[z]
        )
        for k in range(FIELDS):
            fields[k, z] = values[k]
    for q in range(19):
        fwd_strip[q] = strip_of([fwd[q, z].astype(jnp.float32) for z in range(2)])
    mask_strip[...] = strip_of([mask[z].astype(jnp.float32) for z in range(2)])
    where = index[...].astype(jnp.float32)
    line[...] = jnp.broadcast_to(
        edge_line(turned(where, -125, 1), turned(where, 3, 1)), line.shape
    )
    copies[4].wait()
    low, high = pack_sides(lambda n, z: adj[n, z] if n < 19 else fields[n - 19, z])
    low_own[...] = low
    high_own[...] = high


def side_kernel(got_outer, got_inner, low_own, high_own, outer, inner, adj_rim, field_rim):
    even_x = is_even("gx")
    row = iota((8, 128), 0)

    def received(tile):
        from_in = got_inner[tile]
        from_out = got_outer[tile]
        return jnp.where(even_x, from_out, from_in), jnp.where(even_x, from_in, from_out)

    for n, (up, down) in enumerate(MIRRORS):
        low, high = received(n)
        for z in range(2):
            adj_rim[up, z] = jnp.where(row < 4, turned(high, -3 * z, 0), turned(low, 1 - z, 0))
            adj_rim[down, z] = jnp.where(row < 4, turned(high, 2 - z, 0), turned(low, 5 - 3 * z, 0))
    for n in range(0, len(FLAT), 2):
        low, high = received(len(MIRRORS) + n // 2)
        for m, item in enumerate(FLAT[n : n + 2]):
            for z in range(2):
                at = 4 * m + 2 * z
                rim = jnp.where(row < 4, turned(high, -at, 0), turned(low, 6 - at, 0))
                if item < 19:
                    adj_rim[item, z] = rim
                else:
                    field_rim[item - 19, z] = rim
    low, high = pack_sides(lambda n, z: adj_rim[n, z] if n < 19 else field_rim[n - 19, z])
    low = jnp.concatenate([low_own[...], low], axis=0)
    high = jnp.concatenate([high_own[...], high], axis=0)
    even_y = is_even("gy")
    inner[...] = jnp.where(even_y, high, low)
    outer[...] = jnp.where(even_y, low, high)


def sensitivity_of(pulled, popul, velocity):
    f_even, f_odd = split_pairs(popul)
    density = popul[0]
    for n in range(9):
        density = density + f_even[n]
    even, odd = split_pairs(pulled)
    total, first, second = moments(even, odd, pulled[0])
    flux = contract(second, velocity)
    even_sum = even[0] * f_even[0]
    odd_sum = odd[0] * f_odd[0]
    for n in range(1, 9):
        even_sum = even_sum + even[n] * f_even[n]
        odd_sum = odd_sum + odd[n] * f_odd[n]
    relaxed = (
        total * (1.0 - 1.5 * dot3(velocity, velocity))
        + 3.0 * dot3(velocity, first)
        + 4.5 * dot3(velocity, flux)
    )
    half = 0.5 * relax_rate
    return (
        half * even_sum
        + (half - 1.0) * odd_sum
        + relax_rate * (popul[0] * pulled[0])
        - (relax_rate / 36.0) * (density * relaxed)
    )


def hot_rows(values, owner, slot, owners, chunk):
    top = values.astype(jnp.bfloat16).astype(jnp.float32)
    hot = iota((owners, 128), 0) == owner
    lhs = jnp.concatenate(
        [
            jnp.where(hot, top, 0.0).astype(jnp.bfloat16),
            jnp.where(hot, values - top, 0.0).astype(jnp.bfloat16),
        ],
        axis=0,
    )
    rhs = jnp.where(iota((chunk, 128), 0) == slot, 1.0, 0.0).astype(jnp.bfloat16)
    return lhs, rhs


def hot_product(lhs, rhs):
    return lax.dot_general(
        lhs, rhs, (((1,), (1,)), ((), ())), preferred_element_type=jnp.float32
    )


def split_index(index, chunk):
    if chunk & (chunk - 1):
        owner = lax.div(index, jnp.full(index.shape, chunk, index.dtype))
    else:
        owner = index >> (chunk.bit_length() - 1)
    return owner, index - owner * chunk


def main_kernel(
    owners, chunk, adj, adj_rim, fields, field_rim, fwd, mask, index,
    grid, inside, strip, field_strip, state, pulls, summed,
):
    rows = adj.shape[2]
    full = rows + 8
    for step_num in range(STEPS):
        final = step_num == STEPS - 1
        for q in range(19):
            shift_x, shift_y, shift_z = SPEEDS[q]
            if step_num == 0:
                start = [jnp.concatenate([adj[q, z], adj_rim[q, z]], axis=0) for z in range(2)]
            both = []
            for z in range(2):
                src = (z + shift_z) % 2
                main = start[src] if step_num == 0 else state[q, src]
                main = turned(turned(main, -shift_x, 0), -shift_y, 1)
                pulls[q, z] = main
                both.append(main)
                own = main[:rows]
                summed[q, z] = own if step_num == 0 else summed[q, z] + own
            if step_num == 0:
                strip[q] = strip_of(both)
        for z in range(2):
            for t in range((rows if final else full) // 8):
                at = slice(8 * t, 8 * t + 8)
                if 8 * t < rows:
                    here = [fields[k, z, at, :] for k in range(FIELDS)]
                else:
                    here = [field_rim[k, z] for k in range(FIELDS)]
                out = collide([pulls[q, z, at, :] for q in range(19)], here[:3], here[3], here[4])
                into = inside if final else state
                for q in range(19):
                    into[q, z, at, :] = out[q]
    for k in range(FIELDS):
        field_strip[k] = strip_of(
            [jnp.concatenate([fields[k, z], field_rim[k, z]], axis=0) for z in range(2)]
        )
    column = None
    for z in range(2):
        term = sensitivity_of(
            [summed[q, z] for q in range(19)],
            [fwd[q, z].astype(jnp.float32) for q in range(19)],
            [fields[k, z] for k in range(3)],
        ) * mask[z].astype(jnp.float32)
        column = term if column is None else column + term
    lane = iota(column.shape, 1)
    column = jnp.where((lane >= 3) & (lane < 125), column * (porous_max / (LEVELS - 1)), 0.0)
    owner, slot = split_index(index[...], chunk)
    acc = None
    for x in range(0, rows, 2):
        parts = [
            hot_rows(column[r : r + 1], owner[r : r + 1], slot[r : r + 1], owners, chunk)
            for r in (x, x + 1)
        ]
        part = hot_product(
            jnp.concatenate([p[0] for p in parts], axis=1),
            jnp.concatenate([p[1] for p in parts], axis=1),
        )
        acc = part if acc is None else acc + part
    grid[...] = acc[:owners] + acc[owners:]


def strip_kernel(
    got_outer, got_inner, strip, field_strip, fwd_strip, mask_strip, inside,
    column, out, state, summed, pulls, field_state,
):
    full = strip.shape[1]
    rows = full - 8
    even_y = is_even("gy")
    from_in = got_inner[...]
    from_out = got_outer[...]
    low = jnp.where(even_y, from_out, from_in)
    high = jnp.where(even_y, from_in, from_out)
    lane = iota((full, 128), 1) & (Z_LANES - 1)
    half = Z_LANES // 2
    deep = jnp.where(lane < half, high, turned(low, LEFT - 3 - RIGHT, 1))
    thin = jnp.where(lane >= half, high, turned(low, LEFT - 2 - RIGHT, 1))
    moved = {
        (width, shift): turned(both, -shift, 0)
        for width, both in ((3, deep), (2, thin))
        for shift in (-1, 0, 1)
    }

    def joined(n, own, shift_x=0, shift_y=0, shift_z=0):
        width = WIDTHS[n]
        turn = RIGHT - STARTS[n] - shift_y + Z_LANES * (shift_z % 2)
        right = RIGHT - shift_y
        left = LEFT - width - shift_y
        inside = ((lane >= right) & (lane < right + width)) | ((lane >= left) & (lane < left + width))
        return jnp.where(inside, turned(moved[width, shift_x], turn, 1), own)

    for k in range(FIELDS):
        field_state[k] = joined(19 + k, field_strip[k])
    for step_num in range(STEPS):
        final = step_num == STEPS - 1
        for q in range(19):
            shift_x, shift_y, shift_z = SPEEDS[q]
            if step_num == 0:
                tile = joined(q, strip[q], shift_x, shift_y, shift_z)
            else:
                tile = turned(state[q], -shift_x, 0)
                tile = turned(tile, Z_LANES * (shift_z % 2) - shift_y, 1)
            own = tile[:rows]
            pulls[q] = tile
            summed[q] = own if step_num == 0 else summed[q] + own
        for t in range((rows if final else full) // 8):
            at = slice(8 * t, 8 * t + 8)
            here = [field_state[k, at, :] for k in range(FIELDS)]
            result = collide([pulls[q, at, :] for q in range(19)], here[:3], here[3], here[4])
            for q in range(19):
                state[q, at, :] = result[q]
    term = sensitivity_of(
        [summed[q] for q in range(19)],
        [fwd_strip[q] for q in range(19)],
        [field_strip[k, :rows, :] for k in range(3)],
    ) * mask_strip[...]
    column[...] = (term + turned(term, Z_LANES, 1)) * (porous_max / (LEVELS - 1))
    own_lane = iota((rows, 128), 1)
    spot = own_lane & (Z_LANES - 1)
    for q in range(19):
        edge = state[q, :rows, :]
        edge = jnp.where(spot < RIGHT, edge, turned(edge, RIGHT - LEFT, 1))
        for z in range(2):
            out[q, z] = jnp.where(
                (own_lane >= 125) | (own_lane < 3),
                turned(edge, -RIGHT - z * Z_LANES, 1),
                inside[q, z],
            )


def sum_kernel(owners, chunk, column, line, grid_inside, after, grid):
    values = edge_line(turned(column[...], 3 - RIGHT, 1), turned(column[...], 3 - LEFT, 1))
    owner, slot = split_index(line[0:1, :].astype(jnp.int32), chunk)
    acc = hot_product(*hot_rows(values, owner, slot, owners, chunk))
    grid[...] = grid_inside[...] + (acc[:owners] + acc[owners:])


def tail_kernel(received, out, adjoint_start, owned, block, sems):
    copy_out = pltpu.make_async_copy(out, adjoint_start, sems.at[0])
    copy_out.start()
    total = jnp.sum(received[...], axis=0, keepdims=True)
    cols = block.shape[1]
    for r in range(block.shape[0]):
        block[r : r + 1, :] = turned(total, -r * cols, 1)[:, :cols]
    copy_owned = pltpu.make_async_copy(block, owned, sems.at[1])
    copy_owned.start()
    copy_owned.wait()
    copy_out.wait()


def call(kernel, out_types, args, scratch=(), flops=0, from_hbm=0, to=pltpu.VMEM):
    moved = sum(a.size * a.dtype.itemsize for a in args)
    spaces = [pltpu.HBM] * from_hbm + [pltpu.VMEM] * (len(args) - from_hbm)
    return pl.pallas_call(
        kernel,
        out_shape=[to(shape, dtype) for shape, dtype in out_types],
        in_specs=[pl.BlockSpec(memory_space=space) for space in spaces],
        out_specs=[pl.BlockSpec(memory_space=to)] * len(out_types),
        scratch_shapes=list(scratch),
        compiler_params=pltpu.CompilerParams(vmem_limit_bytes=16 << 20),
        cost_estimate=pl.CostEstimate(flops=flops, bytes_accessed=moved, transcendentals=0),
    )(*[pltpu.with_memory_space_constraint(a, space) for a, space in zip(args, spaces)])


def per_device(adjoint_end, forward_pop, porosity_level, fluid_mask, design_index):
    depth, tile_x, tile_y = adjoint_end.shape[1:]
    full = tile_x + 8
    gx_count = lax.axis_size("gx")
    gy_count = lax.axis_size("gy")
    owners = gx_count * gy_count
    design_cols = tile_x * gx_count // 4
    design_rows = tile_y * gy_count // 4
    chunk = design_rows * design_cols // owners
    f32 = jnp.float32
    own = ((19, depth, tile_x, tile_y), f32)
    wide = pltpu.VMEM((19, depth, full, tile_y), f32)

    message = ((X_TILES, 8, tile_y), f32)
    static = [porosity_level, fluid_mask]
    outer, inner = call(
        edge_kernel,
        [message, message],
        [adjoint_end, forward_pop, *static],
        [
            pltpu.VMEM((19, depth, 8, tile_y), f32),
            pltpu.VMEM((19, depth, 2, tile_y), forward_pop.dtype),
            pltpu.VMEM((19, depth, 2, tile_y), forward_pop.dtype),
            *[pltpu.VMEM(a.shape, a.dtype) for a in static],
            pltpu.VMEM((FIELDS, depth, 8, tile_y), f32),
            pltpu.SemaphoreType.DMA((6,)),
        ],
        from_hbm=4,
    )
    got_outer = lax.ppermute(outer, "gx", swap_pairs(gx_count, 1))
    got_inner = lax.ppermute(inner, "gx", swap_pairs(gx_count, 0))
    flat = ((tile_x, 128), f32)
    adj, fwd, mask, index, fields, low_own, high_own, fwd_strip, mask_strip, line = call(
        own_kernel,
        [
            own, (forward_pop.shape, forward_pop.dtype), (fluid_mask.shape, fluid_mask.dtype),
            (design_index.shape, design_index.dtype), ((FIELDS, depth, tile_x, tile_y), f32),
            flat, flat, ((19, tile_x, 128), f32), flat, ((8, 128), f32),
        ],
        [adjoint_end, forward_pop, *static, design_index, outer],
        [
            pltpu.VMEM(porosity_level.shape, porosity_level.dtype),
            pltpu.SemaphoreType.DMA((5,)),
        ],
        flops=10**6,
        from_hbm=5,
    )
    outer, inner, adj_rim, field_rim = call(
        side_kernel,
        [
            ((full, 128), f32), ((full, 128), f32), ((19, depth, 8, tile_y), f32),
            ((FIELDS, depth, 8, tile_y), f32),
        ],
        [got_outer, got_inner, low_own, high_own],
    )
    got_outer = lax.ppermute(outer, "gy", swap_pairs(gy_count, 1))
    got_inner = lax.ppermute(inner, "gy", swap_pairs(gy_count, 0))
    grid, inside, strip, field_strip = call(
        lambda *refs: main_kernel(owners, chunk, *refs),
        [((owners, chunk), f32), own, ((19, full, 128), f32), ((FIELDS, full, 128), f32)],
        [adj, adj_rim, fields, field_rim, fwd, mask, index],
        [wide, wide, pltpu.VMEM(*own)],
        flops=10**6,
    )
    column, out = call(
        strip_kernel,
        [flat, own],
        [got_outer, got_inner, strip, field_strip, fwd_strip, mask_strip, inside],
        [
            pltpu.VMEM((19, full, 128), f32), pltpu.VMEM((19, tile_x, 128), f32),
            pltpu.VMEM((19, full, 128), f32), pltpu.VMEM((FIELDS, full, 128), f32),
        ],
    )
    (grid,) = call(
        lambda *refs: sum_kernel(owners, chunk, *refs),
        [((owners, chunk), f32)],
        [column, line, grid, out],
    )
    received = lax.all_to_all(
        grid.reshape(owners, 1, chunk), BOTH, split_axis=0, concat_axis=0, tiled=True
    )
    block = ((design_rows // owners, design_cols), f32)
    return tuple(
        call(
            tail_kernel,
            [own, block],
            [received.reshape(owners, chunk), out],
            [pltpu.VMEM(*block), pltpu.SemaphoreType.DMA((2,))],
            to=pltpu.HBM,
        )
    )


def solution(mesh):
    in_specs = (
        P(None, None, "gx", "gy"),
        P(None, None, "gx", "gy"),
        P(None, "gx", "gy"),
        P(None, "gx", "gy"),
        P("gx", "gy"),
    )
    out_specs = (P(None, None, "gx", "gy"), P(("gx", "gy"), None))
    return jax.shard_map(
        per_device, mesh=mesh, in_specs=in_specs, out_specs=out_specs, check_vma=False
    )
```

```python
import jax
import jax.numpy as jnp
from jax import lax
from jax.experimental import pallas as pl
from jax.experimental.pallas import tpu as pltpu
from jax.sharding import PartitionSpec as P

STEPS = 3
LEVELS = 8
BOTH = ("gx", "gy")
FIELDS = 5

relax_rate = 1.25
porous_max = 0.5


def lattice_table():
    speeds = [[0, 0, 0]]
    for axis_index in range(3):
        for sign_value in (1, -1):
            vector_row = [0, 0, 0]
            vector_row[axis_index] = sign_value
            speeds.append(vector_row)
    for plane_pair in ((0, 1), (0, 2), (1, 2)):
        for first_sign in (1, -1):
            for second_sign in (1, -1):
                vector_row = [0, 0, 0]
                vector_row[plane_pair[0]] = first_sign
                vector_row[plane_pair[1]] = second_sign
                speeds.append(vector_row)
    return speeds


SPEEDS = lattice_table()
PAIRS = ((1, 2), (3, 4), (5, 6), (7, 10), (8, 9), (11, 14), (12, 13), (15, 18), (16, 17))

Z_LANES = 64
WIDTHS = [3 if SPEEDS[q][1] != 0 else 2 for q in range(19)] + [2] * FIELDS
DEEP = [n for n in range(19) if WIDTHS[n] == 3]
THIN = [n for n in range(19 + FIELDS) if WIDTHS[n] == 2]
STARTS = [
    3 * DEEP.index(n) if n in DEEP else Z_LANES // 2 + 2 * THIN.index(n) for n in range(19 + FIELDS)
]


def swap_pairs(count, parity):
    pairs = []
    for i in range(count):
        j = (i ^ 1) if parity == 0 else ((i - 1) ^ 1) + 1
        if 0 <= j < count:
            pairs.append((i, j))
    return pairs


def is_even(axis):
    return lax.rem(lax.axis_index(axis), 2) == 0


def iota(shape, dim):
    return lax.broadcasted_iota(jnp.int32, shape, dim)


def moments(even, odd, rest):
    e_x, e_y, e_z, e_xy, e_xw, e_xz, e_xv, e_yz, e_yv = even
    o_x, o_y, o_z, o_xy, o_xw, o_xz, o_xv, o_yz, o_yv = odd
    d_xy = e_xy + e_xw
    d_xz = e_xz + e_xv
    d_yz = e_yz + e_yv
    s_xx = 2.0 * e_x + (d_xy + d_xz)
    s_yy = 2.0 * e_y + (d_xy + d_yz)
    s_zz = 2.0 * e_z + (d_xz + d_yz)
    s_xy = e_xy - e_xw
    s_xz = e_xz - e_xv
    s_yz = e_yz - e_yv
    total = 12.0 * rest + 2.0 * ((e_x + e_y) + e_z) + ((d_xy + d_xz) + d_yz)
    v_x = 2.0 * o_x + ((o_xy + o_xw) + (o_xz + o_xv))
    v_y = 2.0 * o_y + ((o_xy - o_xw) + (o_yz + o_yv))
    v_z = 2.0 * o_z + ((o_xz - o_xv) + (o_yz - o_yv))
    return total, (v_x, v_y, v_z), ((s_xx, s_xy, s_xz), (s_xy, s_yy, s_yz), (s_xz, s_yz, s_zz))


def contract(second, velocity):
    return [
        second[k][0] * velocity[0] + second[k][1] * velocity[1] + second[k][2] * velocity[2]
        for k in range(3)
    ]


def dot3(a, b):
    return a[0] * b[0] + a[1] * b[1] + a[2] * b[2]


def split_pairs(pulled):
    even = [pulled[i] + pulled[j] for i, j in PAIRS]
    odd = [pulled[i] - pulled[j] for i, j in PAIRS]
    return even, odd


def collide(pulled, velocity, keep, porosity):
    even, odd = split_pairs(pulled)
    total, first, second = moments(even, odd, pulled[0])
    flux = contract(second, velocity)
    twice = dot3(velocity, flux)
    gain = keep * (relax_rate / 36.0)
    stay = keep * (1.0 - relax_rate)
    base = gain * (total * (1.0 + 1.5 * dot3(velocity, velocity)) - 4.5 * twice)
    turn = [gain * (3.0 * (first[k] - velocity[k] * total) + 9.0 * flux[k]) for k in range(3)]
    both = 0.5 * (stay + porosity)
    diff = 0.5 * (stay - porosity)
    results = [None] * 19
    results[0] = (stay + porosity) * pulled[0] + base
    for n, (i, j) in enumerate(PAIRS):
        along = None
        for k in range(3):
            if SPEEDS[i][k] == 1:
                along = turn[k] if along is None else along + turn[k]
            elif SPEEDS[i][k] == -1:
                along = along - turn[k]
        same = both * even[n] + base
        swing = diff * odd[n] + along
        results[i] = same + swing
        results[j] = same - swing
    return results


MIRRORS = [
    (q, SPEEDS.index([-SPEEDS[q][0], SPEEDS[q][1], SPEEDS[q][2]]))
    for q in range(19)
    if SPEEDS[q][0] == 1
]
FLAT = [q for q in range(19) if SPEEDS[q][0] == 0] + list(range(19, 19 + FIELDS))
X_TILES = len(MIRRORS) + (len(FLAT) + 1) // 2


def turned(tile, shift, axis):
    shift = shift % tile.shape[axis]
    return tile if shift == 0 else pltpu.roll(tile, shift, axis)


def flow_fields(popul, level, mask):
    even, odd = split_pairs(popul)
    density = popul[0]
    for n in range(9):
        density = density + even[n]
    o_x, o_y, o_z, o_xy, o_xw, o_xz, o_xv, o_yz, o_yv = odd
    per_mass = 1.0 / density
    porosity = jnp.where(mask == 1, level.astype(jnp.float32) * (porous_max / (LEVELS - 1)), 1.0)
    return (
        (o_x + ((o_xy + o_xw) + (o_xz + o_xv))) * per_mass,
        (o_y + ((o_xy - o_xw) + (o_yz + o_yv))) * per_mass,
        (o_z + ((o_xz - o_xv) + (o_yz - o_yv))) * per_mass,
        1.0 - porosity,
        porosity,
    )


def edge_kernel(
    adj_hbm, fwd_hbm, level_hbm, mask_hbm, outer, inner, adj, fwd_top, fwd_end, level, mask,
    fields, sems,
):
    rows = adj_hbm.shape[2]
    copies = [
        pltpu.make_async_copy(src, dst, sems.at[n])
        for n, (src, dst) in enumerate(
            (
                (fwd_hbm.at[:, :, pl.ds(0, 2), :], fwd_top),
                (fwd_hbm.at[:, :, pl.ds(rows - 2, 2), :], fwd_end),
                (mask_hbm, mask),
                (level_hbm, level),
                (adj_hbm.at[:, :, pl.ds(0, 3), :], adj.at[:, :, pl.ds(0, 3), :]),
                (adj_hbm.at[:, :, pl.ds(rows - 3, 3), :], adj.at[:, :, pl.ds(5, 3), :]),
            )
        )
    ]
    for copy in copies:
        copy.start()
    for copy in copies[:4]:
        copy.wait()
    for z in range(2):
        for fwd, at, to in ((fwd_top, 0, 0), (fwd_end, rows - 2, 6)):
            values = flow_fields(
                [fwd[q, z].astype(jnp.float32) for q in range(19)],
                level[z, at : at + 2, :],
                mask[z, at : at + 2, :],
            )
            for k in range(FIELDS):
                fields[k, z, to : to + 2, :] = values[k]
    for copy in copies[4:]:
        copy.wait()
    even_x = is_even("gx")
    row = iota((8, 128), 0)

    def tile_of(n, z):
        return adj[n, z] if n < 19 else fields[n - 19, z]

    for n, (up, down) in enumerate(MIRRORS):
        low = jnp.where(row < 3, tile_of(up, 0), turned(tile_of(up, 1), 3, 0))
        low = jnp.where(row < 6, low, turned(tile_of(down, 0), 6, 0))
        low = jnp.where(row < 7, low, turned(tile_of(down, 1), 7, 0))
        high = jnp.where(row < 3, turned(tile_of(down, 0), 3, 0), turned(tile_of(down, 1), 6, 0))
        high = jnp.where(row < 6, high, turned(tile_of(up, 0), 7, 0))
        high = jnp.where(row < 7, high, tile_of(up, 1))
        inner[n] = jnp.where(even_x, high, low)
        outer[n] = jnp.where(even_x, low, high)
    for n in range(0, len(FLAT), 2):
        low = high = None
        for m, item in enumerate(FLAT[n : n + 2]):
            for z in range(2):
                at = 4 * m + 2 * z
                up = turned(tile_of(item, z), at, 0)
                down = turned(tile_of(item, z), at + 2, 0)
                low = up if low is None else jnp.where(row < at, low, up)
                high = down if high is None else jnp.where(row < at, high, down)
        tile = len(MIRRORS) + n // 2
        inner[tile] = jnp.where(even_x, high, low)
        outer[tile] = jnp.where(even_x, low, high)


RIGHT = 16
LEFT = 50


def strip_of(pair):
    lane = iota(pair[0].shape, 1)
    parts = [turned(pair[z], side + z * Z_LANES, 1) for z in range(2) for side in (RIGHT, LEFT)]
    strip = parts[3]
    for n in (2, 1, 0):
        strip = jnp.where(lane < 32 * (n + 1), parts[n], strip)
    return strip


def pack_sides(tiles):
    low = high = None
    for z in range(2):
        for n in DEEP + THIN:
            at = z * Z_LANES + STARTS[n]
            tile = tiles(n, z)
            up = turned(tile, at, 1)
            down = turned(tile, at + WIDTHS[n], 1)
            lane = iota(tile.shape, 1)
            low = up if low is None else jnp.where(lane >= at, up, low)
            high = down if high is None else jnp.where(lane >= at, down, high)
    return low, high


def edge_line(block):
    lane = iota(block.shape, 1)
    right = (lane >= RIGHT - 3) & (lane < RIGHT)
    left = (lane >= LEFT) & (lane < LEFT + 3)
    block = jnp.where(right | left, block, 0.0)
    return jnp.sum(pltpu.roll(block, 0, 1, stride=8, stride_axis=0), axis=0, keepdims=True)


def own_kernel(
    adj_hbm, fwd_hbm, level_hbm, mask_hbm, index_hbm, after,
    adj, fwd, mask, index, fields, low_own, high_own, fwd_strip, mask_strip, line, level, sems,
):
    copies = [
        pltpu.make_async_copy(src, dst, sems.at[n])
        for n, (src, dst) in enumerate(
            (
                (fwd_hbm, fwd), (mask_hbm, mask), (level_hbm, level), (index_hbm, index),
                (adj_hbm, adj),
            )
        )
    ]
    for copy in copies:
        copy.start()
    for copy in copies[:4]:
        copy.wait()
    for z in range(2):
        values = flow_fields(
            [fwd[q, z].astype(jnp.float32) for q in range(19)], level[z], mask[z]
        )
        for k in range(FIELDS):
            fields[k, z] = values[k]
    for q in range(19):
        fwd_strip[q] = strip_of([fwd[q, z].astype(jnp.float32) for z in range(2)])
    mask_strip[...] = strip_of([mask[z].astype(jnp.float32) for z in range(2)])
    where = index[...].astype(jnp.float32)
    lane = iota(where.shape, 1)
    where = jnp.where(lane < Z_LANES // 2, turned(where, RIGHT, 1), turned(where, LEFT, 1))
    line[...] = jnp.broadcast_to(edge_line(where), line.shape)
    copies[4].wait()
    low, high = pack_sides(lambda n, z: adj[n, z] if n < 19 else fields[n - 19, z])
    low_own[...] = low
    high_own[...] = high


def side_kernel(got_outer, got_inner, low_own, high_own, outer, inner, adj_rim, field_rim):
    even_x = is_even("gx")
    row = iota((8, 128), 0)

    def received(tile):
        from_in = got_inner[tile]
        from_out = got_outer[tile]
        return jnp.where(even_x, from_out, from_in), jnp.where(even_x, from_in, from_out)

    for n, (up, down) in enumerate(MIRRORS):
        low, high = received(n)
        for z in range(2):
            adj_rim[up, z] = jnp.where(row < 4, turned(high, -3 * z, 0), turned(low, 1 - z, 0))
            adj_rim[down, z] = jnp.where(row < 4, turned(high, 2 - z, 0), turned(low, 5 - 3 * z, 0))
    for n in range(0, len(FLAT), 2):
        low, high = received(len(MIRRORS) + n // 2)
        for m, item in enumerate(FLAT[n : n + 2]):
            for z in range(2):
                at = 4 * m + 2 * z
                rim = jnp.where(row < 4, turned(high, -at, 0), turned(low, 6 - at, 0))
                if item < 19:
                    adj_rim[item, z] = rim
                else:
                    field_rim[item - 19, z] = rim
    low, high = pack_sides(lambda n, z: adj_rim[n, z] if n < 19 else field_rim[n - 19, z])
    low = jnp.concatenate([low_own[...], low], axis=0)
    high = jnp.concatenate([high_own[...], high], axis=0)
    even_y = is_even("gy")
    inner[...] = jnp.where(even_y, high, low)
    outer[...] = jnp.where(even_y, low, high)


def sensitivity_of(pulled, popul, velocity):
    f_even, f_odd = split_pairs(popul)
    density = popul[0]
    for n in range(9):
        density = density + f_even[n]
    even, odd = split_pairs(pulled)
    total, first, second = moments(even, odd, pulled[0])
    flux = contract(second, velocity)
    even_sum = even[0] * f_even[0]
    odd_sum = odd[0] * f_odd[0]
    for n in range(1, 9):
        even_sum = even_sum + even[n] * f_even[n]
        odd_sum = odd_sum + odd[n] * f_odd[n]
    relaxed = (
        total * (1.0 - 1.5 * dot3(velocity, velocity))
        + 3.0 * dot3(velocity, first)
        + 4.5 * dot3(velocity, flux)
    )
    half = 0.5 * relax_rate
    return (
        half * even_sum
        + (half - 1.0) * odd_sum
        + relax_rate * (popul[0] * pulled[0])
        - (relax_rate / 36.0) * (density * relaxed)
    )


def hot_rows(values, owner, slot, owners, chunk):
    top = values.astype(jnp.bfloat16).astype(jnp.float32)
    hot = iota((owners, 128), 0) == owner
    lhs = jnp.concatenate(
        [
            jnp.where(hot, top, 0.0).astype(jnp.bfloat16),
            jnp.where(hot, values - top, 0.0).astype(jnp.bfloat16),
        ],
        axis=0,
    )
    rhs = jnp.where(iota((chunk, 128), 0) == slot, 1.0, 0.0).astype(jnp.bfloat16)
    return lhs, rhs


def hot_product(lhs, rhs):
    return lax.dot_general(
        lhs, rhs, (((1,), (1,)), ((), ())), preferred_element_type=jnp.float32
    )


def split_index(index, chunk):
    if chunk & (chunk - 1):
        owner = lax.div(index, jnp.full(index.shape, chunk, index.dtype))
    else:
        owner = index >> (chunk.bit_length() - 1)
    return owner, index - owner * chunk


def main_kernel(
    owners, chunk, adj, adj_rim, fields, field_rim, fwd, mask, index,
    grid, inside, strip, field_strip, state, pulls, summed,
):
    rows = adj.shape[2]
    full = rows + 8
    for step_num in range(STEPS):
        final = step_num == STEPS - 1
        for q in range(19):
            shift_x, shift_y, shift_z = SPEEDS[q]
            if step_num == 0:
                start = [jnp.concatenate([adj[q, z], adj_rim[q, z]], axis=0) for z in range(2)]
            both = []
            for z in range(2):
                src = (z + shift_z) % 2
                main = start[src] if step_num == 0 else state[q, src]
                main = turned(turned(main, -shift_x, 0), -shift_y, 1)
                pulls[q, z] = main
                both.append(main)
                own = main[:rows]
                summed[q, z] = own if step_num == 0 else summed[q, z] + own
            if step_num == 0:
                strip[q] = strip_of(both)
        for z in range(2):
            for t in range((rows if final else full) // 8):
                at = slice(8 * t, 8 * t + 8)
                if 8 * t < rows:
                    here = [fields[k, z, at, :] for k in range(FIELDS)]
                else:
                    here = [field_rim[k, z] for k in range(FIELDS)]
                out = collide([pulls[q, z, at, :] for q in range(19)], here[:3], here[3], here[4])
                into = inside if final else state
                for q in range(19):
                    into[q, z, at, :] = out[q]
    for k in range(FIELDS):
        field_strip[k] = strip_of(
            [jnp.concatenate([fields[k, z], field_rim[k, z]], axis=0) for z in range(2)]
        )
    column = None
    for z in range(2):
        term = sensitivity_of(
            [summed[q, z] for q in range(19)],
            [fwd[q, z].astype(jnp.float32) for q in range(19)],
            [fields[k, z] for k in range(3)],
        ) * mask[z].astype(jnp.float32)
        column = term if column is None else column + term
    lane = iota(column.shape, 1)
    column = jnp.where((lane >= 3) & (lane < 125), column * (porous_max / (LEVELS - 1)), 0.0)
    owner, slot = split_index(index[...], chunk)
    acc = None
    for x in range(0, rows, 2):
        parts = [
            hot_rows(column[r : r + 1], owner[r : r + 1], slot[r : r + 1], owners, chunk)
            for r in (x, x + 1)
        ]
        part = hot_product(
            jnp.concatenate([p[0] for p in parts], axis=1),
            jnp.concatenate([p[1] for p in parts], axis=1),
        )
        acc = part if acc is None else acc + part
    grid[...] = acc[:owners] + acc[owners:]


def strip_kernel(
    got_outer, got_inner, strip, field_strip, fwd_strip, mask_strip, inside,
    column, out, state, summed, pulls, field_state,
):
    full = strip.shape[1]
    rows = full - 8
    even_y = is_even("gy")
    from_in = got_inner[...]
    from_out = got_outer[...]
    low = jnp.where(even_y, from_out, from_in)
    high = jnp.where(even_y, from_in, from_out)
    lane = iota((full, 128), 1) & (Z_LANES - 1)
    half = Z_LANES // 2
    deep = jnp.where(lane < 3 * len(DEEP), high, turned(low, LEFT - 3 - RIGHT, 1))
    thin = jnp.where(lane >= half, high, turned(low, LEFT - 2 - RIGHT, 1))
    moved = {
        (width, shift): turned(both, -shift, 0)
        for width, both in ((3, deep), (2, thin))
        for shift in (-1, 0, 1)
    }

    def joined(n, own, shift_x=0, shift_y=0, shift_z=0):
        width = WIDTHS[n]
        turn = RIGHT - STARTS[n] - shift_y + Z_LANES * (shift_z % 2)
        right = RIGHT - shift_y
        left = LEFT - width - shift_y
        inside = ((lane >= right) & (lane < right + width)) | ((lane >= left) & (lane < left + width))
        return jnp.where(inside, turned(moved[width, shift_x], turn, 1), own)

    for k in range(FIELDS):
        field_state[k] = joined(19 + k, field_strip[k])
    for step_num in range(STEPS):
        final = step_num == STEPS - 1
        for q in range(19):
            shift_x, shift_y, shift_z = SPEEDS[q]
            if step_num == 0:
                tile = joined(q, strip[q], shift_x, shift_y, shift_z)
            else:
                tile = turned(state[q], -shift_x, 0)
                tile = turned(tile, Z_LANES * (shift_z % 2) - shift_y, 1)
            own = tile[:rows]
            pulls[q] = tile
            summed[q] = own if step_num == 0 else summed[q] + own
        for t in range((rows if final else full) // 8):
            at = slice(8 * t, 8 * t + 8)
            here = [field_state[k, at, :] for k in range(FIELDS)]
            result = collide([pulls[q, at, :] for q in range(19)], here[:3], here[3], here[4])
            for q in range(19):
                state[q, at, :] = result[q]
    term = sensitivity_of(
        [summed[q] for q in range(19)],
        [fwd_strip[q] for q in range(19)],
        [field_strip[k, :rows, :] for k in range(3)],
    ) * mask_strip[...]
    column[...] = (term + turned(term, Z_LANES, 1)) * (porous_max / (LEVELS - 1))
    own_lane = iota((rows, 128), 1)
    spot = own_lane & (Z_LANES - 1)
    for q in range(19):
        edge = state[q, :rows, :]
        edge = jnp.where(spot < RIGHT, edge, turned(edge, RIGHT - LEFT, 1))
        for z in range(2):
            out[q, z] = jnp.where(
                (own_lane >= 125) | (own_lane < 3),
                turned(edge, -RIGHT - z * Z_LANES, 1),
                inside[q, z],
            )


def sum_kernel(owners, chunk, column, line, grid_inside, after, grid):
    values = edge_line(column[...])
    owner, slot = split_index(line[0:1, :].astype(jnp.int32), chunk)
    acc = hot_product(*hot_rows(values, owner, slot, owners, chunk))
    grid[...] = grid_inside[...] + (acc[:owners] + acc[owners:])


def tail_kernel(received, out, adjoint_start, owned, block, sems):
    copy_out = pltpu.make_async_copy(out, adjoint_start, sems.at[0])
    copy_out.start()
    total = jnp.sum(received[...], axis=0, keepdims=True)
    cols = block.shape[1]
    for r in range(block.shape[0]):
        block[r : r + 1, :] = turned(total, -r * cols, 1)[:, :cols]
    copy_owned = pltpu.make_async_copy(block, owned, sems.at[1])
    copy_owned.start()
    copy_owned.wait()
    copy_out.wait()


def call(kernel, out_types, args, scratch=(), flops=0, from_hbm=0, to=pltpu.VMEM):
    moved = sum(a.size * a.dtype.itemsize for a in args)
    spaces = [pltpu.HBM] * from_hbm + [pltpu.VMEM] * (len(args) - from_hbm)
    return pl.pallas_call(
        kernel,
        out_shape=[to(shape, dtype) for shape, dtype in out_types],
        in_specs=[pl.BlockSpec(memory_space=space) for space in spaces],
        out_specs=[pl.BlockSpec(memory_space=to)] * len(out_types),
        scratch_shapes=list(scratch),
        compiler_params=pltpu.CompilerParams(vmem_limit_bytes=16 << 20),
        cost_estimate=pl.CostEstimate(flops=flops, bytes_accessed=moved, transcendentals=0),
    )(*[pltpu.with_memory_space_constraint(a, space) for a, space in zip(args, spaces)])


def per_device(adjoint_end, forward_pop, porosity_level, fluid_mask, design_index):
    depth, tile_x, tile_y = adjoint_end.shape[1:]
    full = tile_x + 8
    gx_count = lax.axis_size("gx")
    gy_count = lax.axis_size("gy")
    owners = gx_count * gy_count
    design_cols = tile_x * gx_count // 4
    design_rows = tile_y * gy_count // 4
    chunk = design_rows * design_cols // owners
    f32 = jnp.float32
    own = ((19, depth, tile_x, tile_y), f32)
    wide = pltpu.VMEM((19, depth, full, tile_y), f32)

    message = ((X_TILES, 8, tile_y), f32)
    static = [porosity_level, fluid_mask]
    outer, inner = call(
        edge_kernel,
        [message, message],
        [adjoint_end, forward_pop, *static],
        [
            pltpu.VMEM((19, depth, 8, tile_y), f32),
            pltpu.VMEM((19, depth, 2, tile_y), forward_pop.dtype),
            pltpu.VMEM((19, depth, 2, tile_y), forward_pop.dtype),
            *[pltpu.VMEM(a.shape, a.dtype) for a in static],
            pltpu.VMEM((FIELDS, depth, 8, tile_y), f32),
            pltpu.SemaphoreType.DMA((6,)),
        ],
        from_hbm=4,
    )
    got_outer = lax.ppermute(outer, "gx", swap_pairs(gx_count, 1))
    got_inner = lax.ppermute(inner, "gx", swap_pairs(gx_count, 0))
    flat = ((tile_x, 128), f32)
    adj, fwd, mask, index, fields, low_own, high_own, fwd_strip, mask_strip, line = call(
        own_kernel,
        [
            own, (forward_pop.shape, forward_pop.dtype), (fluid_mask.shape, fluid_mask.dtype),
            (design_index.shape, design_index.dtype), ((FIELDS, depth, tile_x, tile_y), f32),
            flat, flat, ((19, tile_x, 128), f32), flat, ((8, 128), f32),
        ],
        [adjoint_end, forward_pop, *static, design_index, outer],
        [
            pltpu.VMEM(porosity_level.shape, porosity_level.dtype),
            pltpu.SemaphoreType.DMA((5,)),
        ],
        flops=10**6,
        from_hbm=5,
    )
    outer, inner, adj_rim, field_rim = call(
        side_kernel,
        [
            ((full, 128), f32), ((full, 128), f32), ((19, depth, 8, tile_y), f32),
            ((FIELDS, depth, 8, tile_y), f32),
        ],
        [got_outer, got_inner, low_own, high_own],
    )
    got_outer = lax.ppermute(outer, "gy", swap_pairs(gy_count, 1))
    got_inner = lax.ppermute(inner, "gy", swap_pairs(gy_count, 0))
    grid, inside, strip, field_strip = call(
        lambda *refs: main_kernel(owners, chunk, *refs),
        [((owners, chunk), f32), own, ((19, full, 128), f32), ((FIELDS, full, 128), f32)],
        [adj, adj_rim, fields, field_rim, fwd, mask, index],
        [wide, wide, pltpu.VMEM(*own)],
        flops=10**6,
    )
    column, out = call(
        strip_kernel,
        [flat, own],
        [got_outer, got_inner, strip, field_strip, fwd_strip, mask_strip, inside],
        [
            pltpu.VMEM((19, full, 128), f32), pltpu.VMEM((19, tile_x, 128), f32),
            pltpu.VMEM((19, full, 128), f32), pltpu.VMEM((FIELDS, full, 128), f32),
        ],
    )
    (grid,) = call(
        lambda *refs: sum_kernel(owners, chunk, *refs),
        [((owners, chunk), f32)],
        [column, line, grid, out],
    )
    received = lax.all_to_all(
        grid.reshape(owners, 1, chunk), BOTH, split_axis=0, concat_axis=0, tiled=True
    )
    block = ((design_rows // owners, design_cols), f32)
    return tuple(
        call(
            tail_kernel,
            [own, block],
            [received.reshape(owners, chunk), out],
            [pltpu.VMEM(*block), pltpu.SemaphoreType.DMA((2,))],
            to=pltpu.HBM,
        )
    )


def solution(mesh):
    in_specs = (
        P(None, None, "gx", "gy"),
        P(None, None, "gx", "gy"),
        P(None, "gx", "gy"),
        P(None, "gx", "gy"),
        P("gx", "gy"),
    )
    out_specs = (P(None, None, "gx", "gy"), P(("gx", "gy"), None))
    return jax.shard_map(
        per_device, mesh=mesh, in_specs=in_specs, out_specs=out_specs, check_vma=False
    )
```

```python
import jax
import jax.numpy as jnp
from jax import lax
from jax.experimental import pallas as pl
from jax.experimental.pallas import tpu as pltpu
from jax.sharding import PartitionSpec as P

STEPS = 3
LEVELS = 8
BOTH = ("gx", "gy")
FIELDS = 5

relax_rate = 1.25
porous_max = 0.5


def lattice_table():
    speeds = [[0, 0, 0]]
    for axis_index in range(3):
        for sign_value in (1, -1):
            vector_row = [0, 0, 0]
            vector_row[axis_index] = sign_value
            speeds.append(vector_row)
    for plane_pair in ((0, 1), (0, 2), (1, 2)):
        for first_sign in (1, -1):
            for second_sign in (1, -1):
                vector_row = [0, 0, 0]
                vector_row[plane_pair[0]] = first_sign
                vector_row[plane_pair[1]] = second_sign
                speeds.append(vector_row)
    return speeds


SPEEDS = lattice_table()
PAIRS = ((1, 2), (3, 4), (5, 6), (7, 10), (8, 9), (11, 14), (12, 13), (15, 18), (16, 17))

Z_LANES = 64
WIDTHS = [3 if SPEEDS[q][1] != 0 else 2 for q in range(19)] + [2] * FIELDS
DEEP = [n for n in range(19) if WIDTHS[n] == 3]
THIN = [n for n in range(19 + FIELDS) if WIDTHS[n] == 2]
STARTS = [
    3 * DEEP.index(n) if n in DEEP else Z_LANES // 2 + 2 * THIN.index(n) for n in range(19 + FIELDS)
]


def swap_pairs(count, parity):
    pairs = []
    for i in range(count):
        j = (i ^ 1) if parity == 0 else ((i - 1) ^ 1) + 1
        if 0 <= j < count:
            pairs.append((i, j))
    return pairs


def is_even(axis):
    return lax.rem(lax.axis_index(axis), 2) == 0


def iota(shape, dim):
    return lax.broadcasted_iota(jnp.int32, shape, dim)


def moments(even, odd, rest):
    e_x, e_y, e_z, e_xy, e_xw, e_xz, e_xv, e_yz, e_yv = even
    o_x, o_y, o_z, o_xy, o_xw, o_xz, o_xv, o_yz, o_yv = odd
    d_xy = e_xy + e_xw
    d_xz = e_xz + e_xv
    d_yz = e_yz + e_yv
    s_xx = 2.0 * e_x + (d_xy + d_xz)
    s_yy = 2.0 * e_y + (d_xy + d_yz)
    s_zz = 2.0 * e_z + (d_xz + d_yz)
    s_xy = e_xy - e_xw
    s_xz = e_xz - e_xv
    s_yz = e_yz - e_yv
    total = 12.0 * rest + 2.0 * ((e_x + e_y) + e_z) + ((d_xy + d_xz) + d_yz)
    v_x = 2.0 * o_x + ((o_xy + o_xw) + (o_xz + o_xv))
    v_y = 2.0 * o_y + ((o_xy - o_xw) + (o_yz + o_yv))
    v_z = 2.0 * o_z + ((o_xz - o_xv) + (o_yz - o_yv))
    return total, (v_x, v_y, v_z), ((s_xx, s_xy, s_xz), (s_xy, s_yy, s_yz), (s_xz, s_yz, s_zz))


def contract(second, velocity):
    return [
        second[k][0] * velocity[0] + second[k][1] * velocity[1] + second[k][2] * velocity[2]
        for k in range(3)
    ]


def dot3(a, b):
    return a[0] * b[0] + a[1] * b[1] + a[2] * b[2]


def split_pairs(pulled):
    even = [pulled[i] + pulled[j] for i, j in PAIRS]
    odd = [pulled[i] - pulled[j] for i, j in PAIRS]
    return even, odd


def collide(pulled, velocity, keep, porosity):
    even, odd = split_pairs(pulled)
    total, first, second = moments(even, odd, pulled[0])
    flux = contract(second, velocity)
    twice = dot3(velocity, flux)
    gain = keep * (relax_rate / 36.0)
    stay = keep * (1.0 - relax_rate)
    base = gain * (total * (1.0 + 1.5 * dot3(velocity, velocity)) - 4.5 * twice)
    turn = [gain * (3.0 * (first[k] - velocity[k] * total) + 9.0 * flux[k]) for k in range(3)]
    both = 0.5 * (stay + porosity)
    diff = 0.5 * (stay - porosity)
    results = [None] * 19
    results[0] = (stay + porosity) * pulled[0] + base
    for n, (i, j) in enumerate(PAIRS):
        along = None
        for k in range(3):
            if SPEEDS[i][k] == 1:
                along = turn[k] if along is None else along + turn[k]
            elif SPEEDS[i][k] == -1:
                along = along - turn[k]
        same = both * even[n] + base
        swing = diff * odd[n] + along
        results[i] = same + swing
        results[j] = same - swing
    return results


MIRRORS = [
    (q, SPEEDS.index([-SPEEDS[q][0], SPEEDS[q][1], SPEEDS[q][2]]))
    for q in range(19)
    if SPEEDS[q][0] == 1
]
FLAT = [q for q in range(19) if SPEEDS[q][0] == 0] + list(range(19, 19 + FIELDS))
X_TILES = len(MIRRORS) + (len(FLAT) + 1) // 2


def turned(tile, shift, axis):
    shift = shift % tile.shape[axis]
    return tile if shift == 0 else pltpu.roll(tile, shift, axis)


def flow_fields(popul, level, mask):
    even, odd = split_pairs(popul)
    density = popul[0]
    for n in range(9):
        density = density + even[n]
    o_x, o_y, o_z, o_xy, o_xw, o_xz, o_xv, o_yz, o_yv = odd
    per_mass = 1.0 / density
    porosity = jnp.where(mask == 1, level.astype(jnp.float32) * (porous_max / (LEVELS - 1)), 1.0)
    return (
        (o_x + ((o_xy + o_xw) + (o_xz + o_xv))) * per_mass,
        (o_y + ((o_xy - o_xw) + (o_yz + o_yv))) * per_mass,
        (o_z + ((o_xz - o_xv) + (o_yz - o_yv))) * per_mass,
        1.0 - porosity,
        porosity,
    )


def parts_of(count, pieces):
    return [slice(count * n // pieces, count * (n + 1) // pieces) for n in range(pieces)]


def edge_kernel(
    adj_hbm, fwd_hbm, level_hbm, mask_hbm, outer, inner, adj, fwd_top, fwd_end, level, mask,
    fields, sems,
):
    rows = adj_hbm.shape[2]
    pairs = [(mask_hbm, mask), (level_hbm, level)]
    for part in parts_of(19, 1):
        pairs.append((fwd_hbm.at[part, :, pl.ds(0, 2), :], fwd_top.at[part]))
        pairs.append((fwd_hbm.at[part, :, pl.ds(rows - 2, 2), :], fwd_end.at[part]))
    early = len(pairs)
    for part in parts_of(19, 2):
        pairs.append((adj_hbm.at[part, :, pl.ds(0, 3), :], adj.at[part, :, pl.ds(0, 3), :]))
        pairs.append((adj_hbm.at[part, :, pl.ds(rows - 3, 3), :], adj.at[part, :, pl.ds(5, 3), :]))
    copies = [
        pltpu.make_async_copy(src, dst, sems.at[n]) for n, (src, dst) in enumerate(pairs)
    ]
    for n, copy in enumerate(copies):
        copy.start()
    for copy in copies[:early]:
        copy.wait()
    for z in range(2):
        for fwd, at, to in ((fwd_top, 0, 0), (fwd_end, rows - 2, 6)):
            values = flow_fields(
                [fwd[q, z].astype(jnp.float32) for q in range(19)],
                level[z, at : at + 2, :],
                mask[z, at : at + 2, :],
            )
            for k in range(FIELDS):
                fields[k, z, to : to + 2, :] = values[k]
    for copy in copies[early:]:
        copy.wait()
    even_x = is_even("gx")
    row = iota((8, 128), 0)

    def tile_of(n, z):
        return adj[n, z] if n < 19 else fields[n - 19, z]

    for n, (up, down) in enumerate(MIRRORS):
        low = jnp.where(row < 3, tile_of(up, 0), turned(tile_of(up, 1), 3, 0))
        low = jnp.where(row < 6, low, turned(tile_of(down, 0), 6, 0))
        low = jnp.where(row < 7, low, turned(tile_of(down, 1), 7, 0))
        high = jnp.where(row < 3, turned(tile_of(down, 0), 3, 0), turned(tile_of(down, 1), 6, 0))
        high = jnp.where(row < 6, high, turned(tile_of(up, 0), 7, 0))
        high = jnp.where(row < 7, high, tile_of(up, 1))
        inner[n] = jnp.where(even_x, high, low)
        outer[n] = jnp.where(even_x, low, high)
    for n in range(0, len(FLAT), 2):
        low = high = None
        for m, item in enumerate(FLAT[n : n + 2]):
            for z in range(2):
                at = 4 * m + 2 * z
                up = turned(tile_of(item, z), at, 0)
                down = turned(tile_of(item, z), at + 2, 0)
                low = up if low is None else jnp.where(row < at, low, up)
                high = down if high is None else jnp.where(row < at, high, down)
        tile = len(MIRRORS) + n // 2
        inner[tile] = jnp.where(even_x, high, low)
        outer[tile] = jnp.where(even_x, low, high)


RIGHT = 16
LEFT = 50


def strip_of(pair):
    lane = iota(pair[0].shape, 1)
    parts = [turned(pair[z], side + z * Z_LANES, 1) for z in range(2) for side in (RIGHT, LEFT)]
    strip = parts[3]
    for n in (2, 1, 0):
        strip = jnp.where(lane < 32 * (n + 1), parts[n], strip)
    return strip


def pack_sides(tiles):
    low = high = None
    for z in range(2):
        for n in DEEP + THIN:
            at = z * Z_LANES + STARTS[n]
            tile = tiles(n, z)
            up = turned(tile, at, 1)
            down = turned(tile, at + WIDTHS[n], 1)
            lane = iota(tile.shape, 1)
            low = up if low is None else jnp.where(lane >= at, up, low)
            high = down if high is None else jnp.where(lane >= at, down, high)
    return low, high


def edge_line(block):
    lane = iota(block.shape, 1)
    right = (lane >= RIGHT - 3) & (lane < RIGHT)
    left = (lane >= LEFT) & (lane < LEFT + 3)
    block = jnp.where(right | left, block, 0.0)
    return jnp.sum(pltpu.roll(block, 0, 1, stride=8, stride_axis=0), axis=0, keepdims=True)


def own_kernel(
    adj_hbm, fwd_hbm, level_hbm, mask_hbm, index_hbm, after,
    adj, fwd, mask, index, fields, low_own, high_own, fwd_strip, mask_strip, line, level, sems,
):
    copies = [
        pltpu.make_async_copy(src, dst, sems.at[n])
        for n, (src, dst) in enumerate(
            (
                (fwd_hbm, fwd), (mask_hbm, mask), (level_hbm, level), (index_hbm, index),
                (adj_hbm, adj),
            )
        )
    ]
    for copy in copies:
        copy.start()
    for copy in copies[:4]:
        copy.wait()
    for z in range(2):
        values = flow_fields(
            [fwd[q, z].astype(jnp.float32) for q in range(19)], level[z], mask[z]
        )
        for k in range(FIELDS):
            fields[k, z] = values[k]
    for q in range(19):
        fwd_strip[q] = strip_of([fwd[q, z].astype(jnp.float32) for z in range(2)])
    mask_strip[...] = strip_of([mask[z].astype(jnp.float32) for z in range(2)])
    where = index[...].astype(jnp.float32)
    lane = iota(where.shape, 1)
    where = jnp.where(lane < Z_LANES // 2, turned(where, RIGHT, 1), turned(where, LEFT, 1))
    line[...] = jnp.broadcast_to(edge_line(where), line.shape)
    copies[4].wait()
    low, high = pack_sides(lambda n, z: adj[n, z] if n < 19 else fields[n - 19, z])
    low_own[...] = low
    high_own[...] = high


def side_kernel(got_outer, got_inner, low_own, high_own, outer, inner, adj_rim, field_rim):
    even_x = is_even("gx")
    row = iota((8, 128), 0)

    def received(tile):
        from_in = got_inner[tile]
        from_out = got_outer[tile]
        return jnp.where(even_x, from_out, from_in), jnp.where(even_x, from_in, from_out)

    for n, (up, down) in enumerate(MIRRORS):
        low, high = received(n)
        for z in range(2):
            adj_rim[up, z] = jnp.where(row < 4, turned(high, -3 * z, 0), turned(low, 1 - z, 0))
            adj_rim[down, z] = jnp.where(row < 4, turned(high, 2 - z, 0), turned(low, 5 - 3 * z, 0))
    for n in range(0, len(FLAT), 2):
        low, high = received(len(MIRRORS) + n // 2)
        for m, item in enumerate(FLAT[n : n + 2]):
            for z in range(2):
                at = 4 * m + 2 * z
                rim = jnp.where(row < 4, turned(high, -at, 0), turned(low, 6 - at, 0))
                if item < 19:
                    adj_rim[item, z] = rim
                else:
                    field_rim[item - 19, z] = rim
    low, high = pack_sides(lambda n, z: adj_rim[n, z] if n < 19 else field_rim[n - 19, z])
    low = jnp.concatenate([low_own[...], low], axis=0)
    high = jnp.concatenate([high_own[...], high], axis=0)
    even_y = is_even("gy")
    inner[...] = jnp.where(even_y, high, low)
    outer[...] = jnp.where(even_y, low, high)


def sensitivity_of(pulled, popul, velocity):
    f_even, f_odd = split_pairs(popul)
    density = popul[0]
    for n in range(9):
        density = density + f_even[n]
    even, odd = split_pairs(pulled)
    total, first, second = moments(even, odd, pulled[0])
    flux = contract(second, velocity)
    even_sum = even[0] * f_even[0]
    odd_sum = odd[0] * f_odd[0]
    for n in range(1, 9):
        even_sum = even_sum + even[n] * f_even[n]
        odd_sum = odd_sum + odd[n] * f_odd[n]
    relaxed = (
        total * (1.0 - 1.5 * dot3(velocity, velocity))
        + 3.0 * dot3(velocity, first)
        + 4.5 * dot3(velocity, flux)
    )
    half = 0.5 * relax_rate
    return (
        half * even_sum
        + (half - 1.0) * odd_sum
        + relax_rate * (popul[0] * pulled[0])
        - (relax_rate / 36.0) * (density * relaxed)
    )


def hot_rows(values, owner, slot, owners, chunk):
    top = values.astype(jnp.bfloat16).astype(jnp.float32)
    hot = iota((owners, 128), 0) == owner
    lhs = jnp.concatenate(
        [
            jnp.where(hot, top, 0.0).astype(jnp.bfloat16),
            jnp.where(hot, values - top, 0.0).astype(jnp.bfloat16),
        ],
        axis=0,
    )
    rhs = jnp.where(iota((chunk, 128), 0) == slot, 1.0, 0.0).astype(jnp.bfloat16)
    return lhs, rhs


def hot_product(lhs, rhs):
    return lax.dot_general(
        lhs, rhs, (((1,), (1,)), ((), ())), preferred_element_type=jnp.float32
    )


def split_index(index, chunk):
    if chunk & (chunk - 1):
        owner = lax.div(index, jnp.full(index.shape, chunk, index.dtype))
    else:
        owner = index >> (chunk.bit_length() - 1)
    return owner, index - owner * chunk


def main_kernel(
    owners, chunk, adj, adj_rim, fields, field_rim, fwd, mask, index,
    grid, inside, strip, field_strip, state, pulls, summed,
):
    rows = adj.shape[2]
    full = rows + 8
    for step_num in range(STEPS):
        final = step_num == STEPS - 1
        for q in range(19):
            shift_x, shift_y, shift_z = SPEEDS[q]
            if step_num == 0:
                start = [jnp.concatenate([adj[q, z], adj_rim[q, z]], axis=0) for z in range(2)]
            both = []
            for z in range(2):
                src = (z + shift_z) % 2
                main = start[src] if step_num == 0 else state[q, src]
                main = turned(turned(main, -shift_x, 0), -shift_y, 1)
                pulls[q, z] = main
                both.append(main)
                own = main[:rows]
                summed[q, z] = own if step_num == 0 else summed[q, z] + own
            if step_num == 0:
                strip[q] = strip_of(both)
        for z in range(2):
            for t in range((rows if final else full) // 8):
                at = slice(8 * t, 8 * t + 8)
                if 8 * t < rows:
                    here = [fields[k, z, at, :] for k in range(FIELDS)]
                else:
                    here = [field_rim[k, z] for k in range(FIELDS)]
                out = collide([pulls[q, z, at, :] for q in range(19)], here[:3], here[3], here[4])
                into = inside if final else state
                for q in range(19):
                    into[q, z, at, :] = out[q]
    for k in range(FIELDS):
        field_strip[k] = strip_of(
            [jnp.concatenate([fields[k, z], field_rim[k, z]], axis=0) for z in range(2)]
        )
    column = None
    for z in range(2):
        term = sensitivity_of(
            [summed[q, z] for q in range(19)],
            [fwd[q, z].astype(jnp.float32) for q in range(19)],
            [fields[k, z] for k in range(3)],
        ) * mask[z].astype(jnp.float32)
        column = term if column is None else column + term
    lane = iota(column.shape, 1)
    column = jnp.where((lane >= 3) & (lane < 125), column * (porous_max / (LEVELS - 1)), 0.0)
    owner, slot = split_index(index[...], chunk)
    acc = None
    for x in range(0, rows, 2):
        parts = [
            hot_rows(column[r : r + 1], owner[r : r + 1], slot[r : r + 1], owners, chunk)
            for r in (x, x + 1)
        ]
        part = hot_product(
            jnp.concatenate([p[0] for p in parts], axis=1),
            jnp.concatenate([p[1] for p in parts], axis=1),
        )
        acc = part if acc is None else acc + part
    grid[...] = acc[:owners] + acc[owners:]


def strip_kernel(
    got_outer, got_inner, strip, field_strip, fwd_strip, mask_strip, inside,
    column, out, state, summed, pulls, field_state,
):
    full = strip.shape[1]
    rows = full - 8
    even_y = is_even("gy")
    from_in = got_inner[...]
    from_out = got_outer[...]
    low = jnp.where(even_y, from_out, from_in)
    high = jnp.where(even_y, from_in, from_out)
    lane = iota((full, 128), 1) & (Z_LANES - 1)
    half = Z_LANES // 2
    deep = jnp.where(lane < 3 * len(DEEP), high, turned(low, LEFT - 3 - RIGHT, 1))
    thin = jnp.where(lane >= half, high, turned(low, LEFT - 2 - RIGHT, 1))
    moved = {
        (width, shift): turned(both, -shift, 0)
        for width, both in ((3, deep), (2, thin))
        for shift in (-1, 0, 1)
    }

    def joined(n, own, shift_x=0, shift_y=0, shift_z=0):
        width = WIDTHS[n]
        turn = RIGHT - STARTS[n] - shift_y + Z_LANES * (shift_z % 2)
        right = RIGHT - shift_y
        left = LEFT - width - shift_y
        inside = ((lane >= right) & (lane < right + width)) | ((lane >= left) & (lane < left + width))
        return jnp.where(inside, turned(moved[width, shift_x], turn, 1), own)

    for k in range(FIELDS):
        field_state[k] = joined(19 + k, field_strip[k])
    for step_num in range(STEPS):
        final = step_num == STEPS - 1
        for q in range(19):
            shift_x, shift_y, shift_z = SPEEDS[q]
            if step_num == 0:
                tile = joined(q, strip[q], shift_x, shift_y, shift_z)
            else:
                tile = turned(state[q], -shift_x, 0)
                tile = turned(tile, Z_LANES * (shift_z % 2) - shift_y, 1)
            own = tile[:rows]
            pulls[q] = tile
            summed[q] = own if step_num == 0 else summed[q] + own
        for t in range((rows if final else full) // 8):
            at = slice(8 * t, 8 * t + 8)
            here = [field_state[k, at, :] for k in range(FIELDS)]
            result = collide([pulls[q, at, :] for q in range(19)], here[:3], here[3], here[4])
            for q in range(19):
                state[q, at, :] = result[q]
    term = sensitivity_of(
        [summed[q] for q in range(19)],
        [fwd_strip[q] for q in range(19)],
        [field_strip[k, :rows, :] for k in range(3)],
    ) * mask_strip[...]
    column[...] = (term + turned(term, Z_LANES, 1)) * (porous_max / (LEVELS - 1))
    own_lane = iota((rows, 128), 1)
    spot = own_lane & (Z_LANES - 1)
    for q in range(19):
        edge = state[q, :rows, :]
        edge = jnp.where(spot < RIGHT, edge, turned(edge, RIGHT - LEFT, 1))
        for z in range(2):
            out[q, z] = jnp.where(
                (own_lane >= 125) | (own_lane < 3),
                turned(edge, -RIGHT - z * Z_LANES, 1),
                inside[q, z],
            )


def sum_kernel(owners, chunk, column, line, grid_inside, after, grid):
    values = edge_line(column[...])
    owner, slot = split_index(line[0:1, :].astype(jnp.int32), chunk)
    acc = hot_product(*hot_rows(values, owner, slot, owners, chunk))
    grid[...] = grid_inside[...] + (acc[:owners] + acc[owners:])


def tail_kernel(received, out, adjoint_start, owned, block, sems):
    copy_out = pltpu.make_async_copy(out, adjoint_start, sems.at[0])
    copy_out.start()
    total = jnp.sum(received[...], axis=0, keepdims=True)
    cols = block.shape[1]
    for r in range(block.shape[0]):
        block[r : r + 1, :] = turned(total, -r * cols, 1)[:, :cols]
    copy_owned = pltpu.make_async_copy(block, owned, sems.at[1])
    copy_owned.start()
    copy_owned.wait()
    copy_out.wait()


def call(kernel, out_types, args, scratch=(), flops=0, from_hbm=0, to=pltpu.VMEM):
    moved = sum(a.size * a.dtype.itemsize for a in args)
    spaces = [pltpu.HBM] * from_hbm + [pltpu.VMEM] * (len(args) - from_hbm)
    return pl.pallas_call(
        kernel,
        out_shape=[to(shape, dtype) for shape, dtype in out_types],
        in_specs=[pl.BlockSpec(memory_space=space) for space in spaces],
        out_specs=[pl.BlockSpec(memory_space=to)] * len(out_types),
        scratch_shapes=list(scratch),
        compiler_params=pltpu.CompilerParams(vmem_limit_bytes=16 << 20),
        cost_estimate=pl.CostEstimate(flops=flops, bytes_accessed=moved, transcendentals=0),
    )(*[pltpu.with_memory_space_constraint(a, space) for a, space in zip(args, spaces)])


def per_device(adjoint_end, forward_pop, porosity_level, fluid_mask, design_index):
    depth, tile_x, tile_y = adjoint_end.shape[1:]
    full = tile_x + 8
    gx_count = lax.axis_size("gx")
    gy_count = lax.axis_size("gy")
    owners = gx_count * gy_count
    design_cols = tile_x * gx_count // 4
    design_rows = tile_y * gy_count // 4
    chunk = design_rows * design_cols // owners
    f32 = jnp.float32
    own = ((19, depth, tile_x, tile_y), f32)
    wide = pltpu.VMEM((19, depth, full, tile_y), f32)

    message = ((X_TILES, 8, tile_y), f32)
    static = [porosity_level, fluid_mask]
    outer, inner = call(
        edge_kernel,
        [message, message],
        [adjoint_end, forward_pop, *static],
        [
            pltpu.VMEM((19, depth, 8, tile_y), f32),
            pltpu.VMEM((19, depth, 2, tile_y), forward_pop.dtype),
            pltpu.VMEM((19, depth, 2, tile_y), forward_pop.dtype),
            *[pltpu.VMEM(a.shape, a.dtype) for a in static],
            pltpu.VMEM((FIELDS, depth, 8, tile_y), f32),
            pltpu.SemaphoreType.DMA((8,)),
        ],
        from_hbm=4,
    )
    got_outer = lax.ppermute(outer, "gx", swap_pairs(gx_count, 1))
    got_inner = lax.ppermute(inner, "gx", swap_pairs(gx_count, 0))
    flat = ((tile_x, 128), f32)
    adj, fwd, mask, index, fields, low_own, high_own, fwd_strip, mask_strip, line = call(
        own_kernel,
        [
            own, (forward_pop.shape, forward_pop.dtype), (fluid_mask.shape, fluid_mask.dtype),
            (design_index.shape, design_index.dtype), ((FIELDS, depth, tile_x, tile_y), f32),
            flat, flat, ((19, tile_x, 128), f32), flat, ((8, 128), f32),
        ],
        [adjoint_end, forward_pop, *static, design_index, outer],
        [
            pltpu.VMEM(porosity_level.shape, porosity_level.dtype),
            pltpu.SemaphoreType.DMA((5,)),
        ],
        flops=10**6,
        from_hbm=5,
    )
    outer, inner, adj_rim, field_rim = call(
        side_kernel,
        [
            ((full, 128), f32), ((full, 128), f32), ((19, depth, 8, tile_y), f32),
            ((FIELDS, depth, 8, tile_y), f32),
        ],
        [got_outer, got_inner, low_own, high_own],
    )
    got_outer = lax.ppermute(outer, "gy", swap_pairs(gy_count, 1))
    got_inner = lax.ppermute(inner, "gy", swap_pairs(gy_count, 0))
    grid, inside, strip, field_strip = call(
        lambda *refs: main_kernel(owners, chunk, *refs),
        [((owners, chunk), f32), own, ((19, full, 128), f32), ((FIELDS, full, 128), f32)],
        [adj, adj_rim, fields, field_rim, fwd, mask, index],
        [wide, wide, pltpu.VMEM(*own)],
        flops=10**6,
    )
    column, out = call(
        strip_kernel,
        [flat, own],
        [got_outer, got_inner, strip, field_strip, fwd_strip, mask_strip, inside],
        [
            pltpu.VMEM((19, full, 128), f32), pltpu.VMEM((19, tile_x, 128), f32),
            pltpu.VMEM((19, full, 128), f32), pltpu.VMEM((FIELDS, full, 128), f32),
        ],
    )
    (grid,) = call(
        lambda *refs: sum_kernel(owners, chunk, *refs),
        [((owners, chunk), f32)],
        [column, line, grid, out],
    )
    received = lax.all_to_all(
        grid.reshape(owners, 1, chunk), BOTH, split_axis=0, concat_axis=0, tiled=True
    )
    block = ((design_rows // owners, design_cols), f32)
    return tuple(
        call(
            tail_kernel,
            [own, block],
            [received.reshape(owners, chunk), out],
            [pltpu.VMEM(*block), pltpu.SemaphoreType.DMA((2,))],
            to=pltpu.HBM,
        )
    )


def solution(mesh):
    in_specs = (
        P(None, None, "gx", "gy"),
        P(None, None, "gx", "gy"),
        P(None, "gx", "gy"),
        P(None, "gx", "gy"),
        P("gx", "gy"),
    )
    out_specs = (P(None, None, "gx", "gy"), P(("gx", "gy"), None))
    return jax.shard_map(
        per_device, mesh=mesh, in_specs=in_specs, out_specs=out_specs, check_vma=False
    )
```

```python
import jax
import jax.numpy as jnp
from jax import lax
from jax.experimental import pallas as pl
from jax.experimental.pallas import tpu as pltpu
from jax.sharding import PartitionSpec as P

STEPS = 3
LEVELS = 8
BOTH = ("gx", "gy")
FIELDS = 5

relax_rate = 1.25
porous_max = 0.5


def lattice_table():
    speeds = [[0, 0, 0]]
    for axis_index in range(3):
        for sign_value in (1, -1):
            vector_row = [0, 0, 0]
            vector_row[axis_index] = sign_value
            speeds.append(vector_row)
    for plane_pair in ((0, 1), (0, 2), (1, 2)):
        for first_sign in (1, -1):
            for second_sign in (1, -1):
                vector_row = [0, 0, 0]
                vector_row[plane_pair[0]] = first_sign
                vector_row[plane_pair[1]] = second_sign
                speeds.append(vector_row)
    return speeds


SPEEDS = lattice_table()
PAIRS = ((1, 2), (3, 4), (5, 6), (7, 10), (8, 9), (11, 14), (12, 13), (15, 18), (16, 17))

Z_LANES = 64
WIDTHS = [3 if SPEEDS[q][1] != 0 else 2 for q in range(19)] + [2] * FIELDS
DEEP = [n for n in range(19) if WIDTHS[n] == 3]
THIN = [n for n in range(19 + FIELDS) if WIDTHS[n] == 2]
STARTS = [
    3 * DEEP.index(n) if n in DEEP else Z_LANES // 2 + 2 * THIN.index(n) for n in range(19 + FIELDS)
]


def swap_pairs(count, parity):
    pairs = []
    for i in range(count):
        j = (i ^ 1) if parity == 0 else ((i - 1) ^ 1) + 1
        if 0 <= j < count:
            pairs.append((i, j))
    return pairs


def is_even(axis):
    return lax.rem(lax.axis_index(axis), 2) == 0


def iota(shape, dim):
    return lax.broadcasted_iota(jnp.int32, shape, dim)


def moments(even, odd, rest):
    e_x, e_y, e_z, e_xy, e_xw, e_xz, e_xv, e_yz, e_yv = even
    o_x, o_y, o_z, o_xy, o_xw, o_xz, o_xv, o_yz, o_yv = odd
    d_xy = e_xy + e_xw
    d_xz = e_xz + e_xv
    d_yz = e_yz + e_yv
    s_xx = 2.0 * e_x + (d_xy + d_xz)
    s_yy = 2.0 * e_y + (d_xy + d_yz)
    s_zz = 2.0 * e_z + (d_xz + d_yz)
    s_xy = e_xy - e_xw
    s_xz = e_xz - e_xv
    s_yz = e_yz - e_yv
    total = 12.0 * rest + 2.0 * ((e_x + e_y) + e_z) + ((d_xy + d_xz) + d_yz)
    v_x = 2.0 * o_x + ((o_xy + o_xw) + (o_xz + o_xv))
    v_y = 2.0 * o_y + ((o_xy - o_xw) + (o_yz + o_yv))
    v_z = 2.0 * o_z + ((o_xz - o_xv) + (o_yz - o_yv))
    return total, (v_x, v_y, v_z), ((s_xx, s_xy, s_xz), (s_xy, s_yy, s_yz), (s_xz, s_yz, s_zz))


def contract(second, velocity):
    return [
        second[k][0] * velocity[0] + second[k][1] * velocity[1] + second[k][2] * velocity[2]
        for k in range(3)
    ]


def dot3(a, b):
    return a[0] * b[0] + a[1] * b[1] + a[2] * b[2]


def split_pairs(pulled):
    even = [pulled[i] + pulled[j] for i, j in PAIRS]
    odd = [pulled[i] - pulled[j] for i, j in PAIRS]
    return even, odd


def collide(pulled, velocity, keep, porosity):
    even, odd = split_pairs(pulled)
    total, first, second = moments(even, odd, pulled[0])
    flux = contract(second, velocity)
    twice = dot3(velocity, flux)
    gain = keep * (relax_rate / 36.0)
    stay = keep * (1.0 - relax_rate)
    base = gain * (total * (1.0 + 1.5 * dot3(velocity, velocity)) - 4.5 * twice)
    turn = [gain * (3.0 * (first[k] - velocity[k] * total) + 9.0 * flux[k]) for k in range(3)]
    both = 0.5 * (stay + porosity)
    diff = 0.5 * (stay - porosity)
    results = [None] * 19
    results[0] = (stay + porosity) * pulled[0] + base
    for n, (i, j) in enumerate(PAIRS):
        along = None
        for k in range(3):
            if SPEEDS[i][k] == 1:
                along = turn[k] if along is None else along + turn[k]
            elif SPEEDS[i][k] == -1:
                along = along - turn[k]
        same = both * even[n] + base
        swing = diff * odd[n] + along
        results[i] = same + swing
        results[j] = same - swing
    return results


MIRRORS = [
    (q, SPEEDS.index([-SPEEDS[q][0], SPEEDS[q][1], SPEEDS[q][2]]))
    for q in range(19)
    if SPEEDS[q][0] == 1
]
FLAT = [q for q in range(19) if SPEEDS[q][0] == 0] + list(range(19, 19 + FIELDS))
X_TILES = len(MIRRORS) + (len(FLAT) + 1) // 2


def turned(tile, shift, axis):
    shift = shift % tile.shape[axis]
    return tile if shift == 0 else pltpu.roll(tile, shift, axis)


def flow_fields(popul, level, mask):
    even, odd = split_pairs(popul)
    density = popul[0]
    for n in range(9):
        density = density + even[n]
    o_x, o_y, o_z, o_xy, o_xw, o_xz, o_xv, o_yz, o_yv = odd
    per_mass = 1.0 / density
    porosity = jnp.where(mask == 1, level.astype(jnp.float32) * (porous_max / (LEVELS - 1)), 1.0)
    return (
        (o_x + ((o_xy + o_xw) + (o_xz + o_xv))) * per_mass,
        (o_y + ((o_xy - o_xw) + (o_yz + o_yv))) * per_mass,
        (o_z + ((o_xz - o_xv) + (o_yz - o_yv))) * per_mass,
        1.0 - porosity,
        porosity,
    )


def parts_of(count, pieces):
    return [slice(count * n // pieces, count * (n + 1) // pieces) for n in range(pieces)]


def edge_kernel(
    adj_hbm, fwd_hbm, level_hbm, mask_hbm, outer, inner, adj, fwd_top, fwd_end, level, mask,
    fields, sems,
):
    rows = adj_hbm.shape[2]
    pairs = [(mask_hbm, mask), (level_hbm, level)]
    for part in parts_of(19, 1):
        pairs.append((fwd_hbm.at[part, :, pl.ds(0, 2), :], fwd_top.at[part]))
        pairs.append((fwd_hbm.at[part, :, pl.ds(rows - 2, 2), :], fwd_end.at[part]))
    early = len(pairs)
    for part in parts_of(19, 2):
        pairs.append((adj_hbm.at[part, :, pl.ds(0, 3), :], adj.at[part, :, pl.ds(0, 3), :]))
        pairs.append((adj_hbm.at[part, :, pl.ds(rows - 3, 3), :], adj.at[part, :, pl.ds(5, 3), :]))
    copies = [
        pltpu.make_async_copy(src, dst, sems.at[n]) for n, (src, dst) in enumerate(pairs)
    ]
    for n, copy in enumerate(copies):
        copy.start(priority=n % 2)
    for copy in copies[:early]:
        copy.wait()
    for z in range(2):
        for fwd, at, to in ((fwd_top, 0, 0), (fwd_end, rows - 2, 6)):
            values = flow_fields(
                [fwd[q, z].astype(jnp.float32) for q in range(19)],
                level[z, at : at + 2, :],
                mask[z, at : at + 2, :],
            )
            for k in range(FIELDS):
                fields[k, z, to : to + 2, :] = values[k]
    for copy in copies[early:]:
        copy.wait()
    even_x = is_even("gx")
    row = iota((8, 128), 0)

    def tile_of(n, z):
        return adj[n, z] if n < 19 else fields[n - 19, z]

    for n, (up, down) in enumerate(MIRRORS):
        low = jnp.where(row < 3, tile_of(up, 0), turned(tile_of(up, 1), 3, 0))
        low = jnp.where(row < 6, low, turned(tile_of(down, 0), 6, 0))
        low = jnp.where(row < 7, low, turned(tile_of(down, 1), 7, 0))
        high = jnp.where(row < 3, turned(tile_of(down, 0), 3, 0), turned(tile_of(down, 1), 6, 0))
        high = jnp.where(row < 6, high, turned(tile_of(up, 0), 7, 0))
        high = jnp.where(row < 7, high, tile_of(up, 1))
        inner[n] = jnp.where(even_x, high, low)
        outer[n] = jnp.where(even_x, low, high)
    for n in range(0, len(FLAT), 2):
        low = high = None
        for m, item in enumerate(FLAT[n : n + 2]):
            for z in range(2):
                at = 4 * m + 2 * z
                up = turned(tile_of(item, z), at, 0)
                down = turned(tile_of(item, z), at + 2, 0)
                low = up if low is None else jnp.where(row < at, low, up)
                high = down if high is None else jnp.where(row < at, high, down)
        tile = len(MIRRORS) + n // 2
        inner[tile] = jnp.where(even_x, high, low)
        outer[tile] = jnp.where(even_x, low, high)


RIGHT = 16
LEFT = 50


def strip_of(pair):
    lane = iota(pair[0].shape, 1)
    parts = [turned(pair[z], side + z * Z_LANES, 1) for z in range(2) for side in (RIGHT, LEFT)]
    strip = parts[3]
    for n in (2, 1, 0):
        strip = jnp.where(lane < 32 * (n + 1), parts[n], strip)
    return strip


def pack_sides(tiles):
    low = high = None
    for z in range(2):
        for n in DEEP + THIN:
            at = z * Z_LANES + STARTS[n]
            tile = tiles(n, z)
            up = turned(tile, at, 1)
            down = turned(tile, at + WIDTHS[n], 1)
            lane = iota(tile.shape, 1)
            low = up if low is None else jnp.where(lane >= at, up, low)
            high = down if high is None else jnp.where(lane >= at, down, high)
    return low, high


def edge_line(block):
    lane = iota(block.shape, 1)
    right = (lane >= RIGHT - 3) & (lane < RIGHT)
    left = (lane >= LEFT) & (lane < LEFT + 3)
    block = jnp.where(right | left, block, 0.0)
    return jnp.sum(pltpu.roll(block, 0, 1, stride=8, stride_axis=0), axis=0, keepdims=True)


def own_kernel(
    adj_hbm, fwd_hbm, level_hbm, mask_hbm, index_hbm, after,
    adj, fwd, mask, index, fields, low_own, high_own, fwd_strip, mask_strip, line, level, sems,
):
    copies = [
        pltpu.make_async_copy(src, dst, sems.at[n])
        for n, (src, dst) in enumerate(
            (
                (fwd_hbm, fwd), (mask_hbm, mask), (level_hbm, level), (index_hbm, index),
                (adj_hbm, adj),
            )
        )
    ]
    for copy in copies:
        copy.start()
    for copy in copies[:4]:
        copy.wait()
    for z in range(2):
        values = flow_fields(
            [fwd[q, z].astype(jnp.float32) for q in range(19)], level[z], mask[z]
        )
        for k in range(FIELDS):
            fields[k, z] = values[k]
    for q in range(19):
        fwd_strip[q] = strip_of([fwd[q, z].astype(jnp.float32) for z in range(2)])
    mask_strip[...] = strip_of([mask[z].astype(jnp.float32) for z in range(2)])
    where = index[...].astype(jnp.float32)
    lane = iota(where.shape, 1)
    where = jnp.where(lane < Z_LANES // 2, turned(where, RIGHT, 1), turned(where, LEFT, 1))
    line[...] = jnp.broadcast_to(edge_line(where), line.shape)
    copies[4].wait()
    low, high = pack_sides(lambda n, z: adj[n, z] if n < 19 else fields[n - 19, z])
    low_own[...] = low
    high_own[...] = high


def side_kernel(got_outer, got_inner, low_own, high_own, outer, inner, adj_rim, field_rim):
    even_x = is_even("gx")
    row = iota((8, 128), 0)

    def received(tile):
        from_in = got_inner[tile]
        from_out = got_outer[tile]
        return jnp.where(even_x, from_out, from_in), jnp.where(even_x, from_in, from_out)

    for n, (up, down) in enumerate(MIRRORS):
        low, high = received(n)
        for z in range(2):
            adj_rim[up, z] = jnp.where(row < 4, turned(high, -3 * z, 0), turned(low, 1 - z, 0))
            adj_rim[down, z] = jnp.where(row < 4, turned(high, 2 - z, 0), turned(low, 5 - 3 * z, 0))
    for n in range(0, len(FLAT), 2):
        low, high = received(len(MIRRORS) + n // 2)
        for m, item in enumerate(FLAT[n : n + 2]):
            for z in range(2):
                at = 4 * m + 2 * z
                rim = jnp.where(row < 4, turned(high, -at, 0), turned(low, 6 - at, 0))
                if item < 19:
                    adj_rim[item, z] = rim
                else:
                    field_rim[item - 19, z] = rim
    low, high = pack_sides(lambda n, z: adj_rim[n, z] if n < 19 else field_rim[n - 19, z])
    low = jnp.concatenate([low_own[...], low], axis=0)
    high = jnp.concatenate([high_own[...], high], axis=0)
    even_y = is_even("gy")
    inner[...] = jnp.where(even_y, high, low)
    outer[...] = jnp.where(even_y, low, high)


def sensitivity_of(pulled, popul, velocity):
    f_even, f_odd = split_pairs(popul)
    density = popul[0]
    for n in range(9):
        density = density + f_even[n]
    even, odd = split_pairs(pulled)
    total, first, second = moments(even, odd, pulled[0])
    flux = contract(second, velocity)
    even_sum = even[0] * f_even[0]
    odd_sum = odd[0] * f_odd[0]
    for n in range(1, 9):
        even_sum = even_sum + even[n] * f_even[n]
        odd_sum = odd_sum + odd[n] * f_odd[n]
    relaxed = (
        total * (1.0 - 1.5 * dot3(velocity, velocity))
        + 3.0 * dot3(velocity, first)
        + 4.5 * dot3(velocity, flux)
    )
    half = 0.5 * relax_rate
    return (
        half * even_sum
        + (half - 1.0) * odd_sum
        + relax_rate * (popul[0] * pulled[0])
        - (relax_rate / 36.0) * (density * relaxed)
    )


def hot_rows(values, owner, slot, owners, chunk):
    top = values.astype(jnp.bfloat16).astype(jnp.float32)
    hot = iota((owners, 128), 0) == owner
    lhs = jnp.concatenate(
        [
            jnp.where(hot, top, 0.0).astype(jnp.bfloat16),
            jnp.where(hot, values - top, 0.0).astype(jnp.bfloat16),
        ],
        axis=0,
    )
    rhs = jnp.where(iota((chunk, 128), 0) == slot, 1.0, 0.0).astype(jnp.bfloat16)
    return lhs, rhs


def hot_product(lhs, rhs):
    return lax.dot_general(
        lhs, rhs, (((1,), (1,)), ((), ())), preferred_element_type=jnp.float32
    )


def split_index(index, chunk):
    if chunk & (chunk - 1):
        owner = lax.div(index, jnp.full(index.shape, chunk, index.dtype))
    else:
        owner = index >> (chunk.bit_length() - 1)
    return owner, index - owner * chunk


def main_kernel(
    owners, chunk, adj, adj_rim, fields, field_rim, fwd, mask, index,
    grid, inside, strip, field_strip, state, pulls, summed,
):
    rows = adj.shape[2]
    full = rows + 8
    for step_num in range(STEPS):
        final = step_num == STEPS - 1
        for q in range(19):
            shift_x, shift_y, shift_z = SPEEDS[q]
            if step_num == 0:
                start = [jnp.concatenate([adj[q, z], adj_rim[q, z]], axis=0) for z in range(2)]
            both = []
            for z in range(2):
                src = (z + shift_z) % 2
                main = start[src] if step_num == 0 else state[q, src]
                main = turned(turned(main, -shift_x, 0), -shift_y, 1)
                pulls[q, z] = main
                both.append(main)
                own = main[:rows]
                summed[q, z] = own if step_num == 0 else summed[q, z] + own
            if step_num == 0:
                strip[q] = strip_of(both)
        for z in range(2):
            for t in range((rows if final else full) // 8):
                at = slice(8 * t, 8 * t + 8)
                if 8 * t < rows:
                    here = [fields[k, z, at, :] for k in range(FIELDS)]
                else:
                    here = [field_rim[k, z] for k in range(FIELDS)]
                out = collide([pulls[q, z, at, :] for q in range(19)], here[:3], here[3], here[4])
                into = inside if final else state
                for q in range(19):
                    into[q, z, at, :] = out[q]
    for k in range(FIELDS):
        field_strip[k] = strip_of(
            [jnp.concatenate([fields[k, z], field_rim[k, z]], axis=0) for z in range(2)]
        )
    column = None
    for z in range(2):
        term = sensitivity_of(
            [summed[q, z] for q in range(19)],
            [fwd[q, z].astype(jnp.float32) for q in range(19)],
            [fields[k, z] for k in range(3)],
        ) * mask[z].astype(jnp.float32)
        column = term if column is None else column + term
    lane = iota(column.shape, 1)
    column = jnp.where((lane >= 3) & (lane < 125), column * (porous_max / (LEVELS - 1)), 0.0)
    owner, slot = split_index(index[...], chunk)
    acc = None
    for x in range(0, rows, 2):
        parts = [
            hot_rows(column[r : r + 1], owner[r : r + 1], slot[r : r + 1], owners, chunk)
            for r in (x, x + 1)
        ]
        part = hot_product(
            jnp.concatenate([p[0] for p in parts], axis=1),
            jnp.concatenate([p[1] for p in parts], axis=1),
        )
        acc = part if acc is None else acc + part
    grid[...] = acc[:owners] + acc[owners:]


def strip_kernel(
    got_outer, got_inner, strip, field_strip, fwd_strip, mask_strip, inside,
    column, out, state, summed, pulls, field_state,
):
    full = strip.shape[1]
    rows = full - 8
    even_y = is_even("gy")
    from_in = got_inner[...]
    from_out = got_outer[...]
    low = jnp.where(even_y, from_out, from_in)
    high = jnp.where(even_y, from_in, from_out)
    lane = iota((full, 128), 1) & (Z_LANES - 1)
    half = Z_LANES // 2
    deep = jnp.where(lane < 3 * len(DEEP), high, turned(low, LEFT - 3 - RIGHT, 1))
    thin = jnp.where(lane >= half, high, turned(low, LEFT - 2 - RIGHT, 1))
    moved = {
        (width, shift): turned(both, -shift, 0)
        for width, both in ((3, deep), (2, thin))
        for shift in (-1, 0, 1)
    }

    def joined(n, own, shift_x=0, shift_y=0, shift_z=0):
        width = WIDTHS[n]
        turn = RIGHT - STARTS[n] - shift_y + Z_LANES * (shift_z % 2)
        right = RIGHT - shift_y
        left = LEFT - width - shift_y
        inside = ((lane >= right) & (lane < right + width)) | ((lane >= left) & (lane < left + width))
        return jnp.where(inside, turned(moved[width, shift_x], turn, 1), own)

    for k in range(FIELDS):
        field_state[k] = joined(19 + k, field_strip[k])
    for step_num in range(STEPS):
        final = step_num == STEPS - 1
        for q in range(19):
            shift_x, shift_y, shift_z = SPEEDS[q]
            if step_num == 0:
                tile = joined(q, strip[q], shift_x, shift_y, shift_z)
            else:
                tile = turned(state[q], -shift_x, 0)
                tile = turned(tile, Z_LANES * (shift_z % 2) - shift_y, 1)
            own = tile[:rows]
            pulls[q] = tile
            summed[q] = own if step_num == 0 else summed[q] + own
        for t in range((rows if final else full) // 8):
            at = slice(8 * t, 8 * t + 8)
            here = [field_state[k, at, :] for k in range(FIELDS)]
            result = collide([pulls[q, at, :] for q in range(19)], here[:3], here[3], here[4])
            for q in range(19):
                state[q, at, :] = result[q]
    term = sensitivity_of(
        [summed[q] for q in range(19)],
        [fwd_strip[q] for q in range(19)],
        [field_strip[k, :rows, :] for k in range(3)],
    ) * mask_strip[...]
    column[...] = (term + turned(term, Z_LANES, 1)) * (porous_max / (LEVELS - 1))
    own_lane = iota((rows, 128), 1)
    spot = own_lane & (Z_LANES - 1)
    for q in range(19):
        edge = state[q, :rows, :]
        edge = jnp.where(spot < RIGHT, edge, turned(edge, RIGHT - LEFT, 1))
        for z in range(2):
            out[q, z] = jnp.where(
                (own_lane >= 125) | (own_lane < 3),
                turned(edge, -RIGHT - z * Z_LANES, 1),
                inside[q, z],
            )


def sum_kernel(owners, chunk, column, line, grid_inside, after, grid):
    values = edge_line(column[...])
    owner, slot = split_index(line[0:1, :].astype(jnp.int32), chunk)
    acc = hot_product(*hot_rows(values, owner, slot, owners, chunk))
    grid[...] = grid_inside[...] + (acc[:owners] + acc[owners:])


def tail_kernel(received, out, adjoint_start, owned, block, sems):
    copy_out = pltpu.make_async_copy(out, adjoint_start, sems.at[0])
    copy_out.start()
    total = jnp.sum(received[...], axis=0, keepdims=True)
    cols = block.shape[1]
    for r in range(block.shape[0]):
        block[r : r + 1, :] = turned(total, -r * cols, 1)[:, :cols]
    copy_owned = pltpu.make_async_copy(block, owned, sems.at[1])
    copy_owned.start()
    copy_owned.wait()
    copy_out.wait()


def call(kernel, out_types, args, scratch=(), flops=0, from_hbm=0, to=pltpu.VMEM):
    moved = sum(a.size * a.dtype.itemsize for a in args)
    spaces = [pltpu.HBM] * from_hbm + [pltpu.VMEM] * (len(args) - from_hbm)
    return pl.pallas_call(
        kernel,
        out_shape=[to(shape, dtype) for shape, dtype in out_types],
        in_specs=[pl.BlockSpec(memory_space=space) for space in spaces],
        out_specs=[pl.BlockSpec(memory_space=to)] * len(out_types),
        scratch_shapes=list(scratch),
        compiler_params=pltpu.CompilerParams(vmem_limit_bytes=16 << 20),
        cost_estimate=pl.CostEstimate(flops=flops, bytes_accessed=moved, transcendentals=0),
    )(*[pltpu.with_memory_space_constraint(a, space) for a, space in zip(args, spaces)])


def per_device(adjoint_end, forward_pop, porosity_level, fluid_mask, design_index):
    depth, tile_x, tile_y = adjoint_end.shape[1:]
    full = tile_x + 8
    gx_count = lax.axis_size("gx")
    gy_count = lax.axis_size("gy")
    owners = gx_count * gy_count
    design_cols = tile_x * gx_count // 4
    design_rows = tile_y * gy_count // 4
    chunk = design_rows * design_cols // owners
    f32 = jnp.float32
    own = ((19, depth, tile_x, tile_y), f32)
    wide = pltpu.VMEM((19, depth, full, tile_y), f32)

    message = ((X_TILES, 8, tile_y), f32)
    static = [porosity_level, fluid_mask]
    outer, inner = call(
        edge_kernel,
        [message, message],
        [adjoint_end, forward_pop, *static],
        [
            pltpu.VMEM((19, depth, 8, tile_y), f32),
            pltpu.VMEM((19, depth, 2, tile_y), forward_pop.dtype),
            pltpu.VMEM((19, depth, 2, tile_y), forward_pop.dtype),
            *[pltpu.VMEM(a.shape, a.dtype) for a in static],
            pltpu.VMEM((FIELDS, depth, 8, tile_y), f32),
            pltpu.SemaphoreType.DMA((8,)),
        ],
        from_hbm=4,
    )
    got_outer = lax.ppermute(outer, "gx", swap_pairs(gx_count, 1))
    got_inner = lax.ppermute(inner, "gx", swap_pairs(gx_count, 0))
    flat = ((tile_x, 128), f32)
    adj, fwd, mask, index, fields, low_own, high_own, fwd_strip, mask_strip, line = call(
        own_kernel,
        [
            own, (forward_pop.shape, forward_pop.dtype), (fluid_mask.shape, fluid_mask.dtype),
            (design_index.shape, design_index.dtype), ((FIELDS, depth, tile_x, tile_y), f32),
            flat, flat, ((19, tile_x, 128), f32), flat, ((8, 128), f32),
        ],
        [adjoint_end, forward_pop, *static, design_index, outer],
        [
            pltpu.VMEM(porosity_level.shape, porosity_level.dtype),
            pltpu.SemaphoreType.DMA((5,)),
        ],
        flops=10**6,
        from_hbm=5,
    )
    outer, inner, adj_rim, field_rim = call(
        side_kernel,
        [
            ((full, 128), f32), ((full, 128), f32), ((19, depth, 8, tile_y), f32),
            ((FIELDS, depth, 8, tile_y), f32),
        ],
        [got_outer, got_inner, low_own, high_own],
    )
    got_outer = lax.ppermute(outer, "gy", swap_pairs(gy_count, 1))
    got_inner = lax.ppermute(inner, "gy", swap_pairs(gy_count, 0))
    grid, inside, strip, field_strip = call(
        lambda *refs: main_kernel(owners, chunk, *refs),
        [((owners, chunk), f32), own, ((19, full, 128), f32), ((FIELDS, full, 128), f32)],
        [adj, adj_rim, fields, field_rim, fwd, mask, index],
        [wide, wide, pltpu.VMEM(*own)],
        flops=10**6,
    )
    column, out = call(
        strip_kernel,
        [flat, own],
        [got_outer, got_inner, strip, field_strip, fwd_strip, mask_strip, inside],
        [
            pltpu.VMEM((19, full, 128), f32), pltpu.VMEM((19, tile_x, 128), f32),
            pltpu.VMEM((19, full, 128), f32), pltpu.VMEM((FIELDS, full, 128), f32),
        ],
    )
    (grid,) = call(
        lambda *refs: sum_kernel(owners, chunk, *refs),
        [((owners, chunk), f32)],
        [column, line, grid, out],
    )
    received = lax.all_to_all(
        grid.reshape(owners, 1, chunk), BOTH, split_axis=0, concat_axis=0, tiled=True
    )
    block = ((design_rows // owners, design_cols), f32)
    return tuple(
        call(
            tail_kernel,
            [own, block],
            [received.reshape(owners, chunk), out],
            [pltpu.VMEM(*block), pltpu.SemaphoreType.DMA((2,))],
            to=pltpu.HBM,
        )
    )


def solution(mesh):
    in_specs = (
        P(None, None, "gx", "gy"),
        P(None, None, "gx", "gy"),
        P(None, "gx", "gy"),
        P(None, "gx", "gy"),
        P("gx", "gy"),
    )
    out_specs = (P(None, None, "gx", "gy"), P(("gx", "gy"), None))
    return jax.shard_map(
        per_device, mesh=mesh, in_specs=in_specs, out_specs=out_specs, check_vma=False
    )
```

```python
import jax
import jax.numpy as jnp
from jax import lax
from jax.experimental import pallas as pl
from jax.experimental.pallas import tpu as pltpu
from jax.sharding import PartitionSpec as P

STEPS = 3
LEVELS = 8
BOTH = ("gx", "gy")
FIELDS = 5

relax_rate = 1.25
porous_max = 0.5


def lattice_table():
    speeds = [[0, 0, 0]]
    for axis_index in range(3):
        for sign_value in (1, -1):
            vector_row = [0, 0, 0]
            vector_row[axis_index] = sign_value
            speeds.append(vector_row)
    for plane_pair in ((0, 1), (0, 2), (1, 2)):
        for first_sign in (1, -1):
            for second_sign in (1, -1):
                vector_row = [0, 0, 0]
                vector_row[plane_pair[0]] = first_sign
                vector_row[plane_pair[1]] = second_sign
                speeds.append(vector_row)
    return speeds


SPEEDS = lattice_table()
PAIRS = ((1, 2), (3, 4), (5, 6), (7, 10), (8, 9), (11, 14), (12, 13), (15, 18), (16, 17))

Z_LANES = 64
WIDTHS = [3 if SPEEDS[q][1] != 0 else 2 for q in range(19)] + [2] * FIELDS
DEEP = [n for n in range(19) if WIDTHS[n] == 3]
THIN = [n for n in range(19 + FIELDS) if WIDTHS[n] == 2]
STARTS = [
    3 * DEEP.index(n) if n in DEEP else Z_LANES // 2 + 2 * THIN.index(n) for n in range(19 + FIELDS)
]


def swap_pairs(count, parity):
    pairs = []
    for i in range(count):
        j = (i ^ 1) if parity == 0 else ((i - 1) ^ 1) + 1
        if 0 <= j < count:
            pairs.append((i, j))
    return pairs


def is_even(axis):
    return lax.rem(lax.axis_index(axis), 2) == 0


def iota(shape, dim):
    return lax.broadcasted_iota(jnp.int32, shape, dim)


def moments(even, odd, rest):
    e_x, e_y, e_z, e_xy, e_xw, e_xz, e_xv, e_yz, e_yv = even
    o_x, o_y, o_z, o_xy, o_xw, o_xz, o_xv, o_yz, o_yv = odd
    d_xy = e_xy + e_xw
    d_xz = e_xz + e_xv
    d_yz = e_yz + e_yv
    s_xx = 2.0 * e_x + (d_xy + d_xz)
    s_yy = 2.0 * e_y + (d_xy + d_yz)
    s_zz = 2.0 * e_z + (d_xz + d_yz)
    s_xy = e_xy - e_xw
    s_xz = e_xz - e_xv
    s_yz = e_yz - e_yv
    total = 12.0 * rest + 2.0 * ((e_x + e_y) + e_z) + ((d_xy + d_xz) + d_yz)
    v_x = 2.0 * o_x + ((o_xy + o_xw) + (o_xz + o_xv))
    v_y = 2.0 * o_y + ((o_xy - o_xw) + (o_yz + o_yv))
    v_z = 2.0 * o_z + ((o_xz - o_xv) + (o_yz - o_yv))
    return total, (v_x, v_y, v_z), ((s_xx, s_xy, s_xz), (s_xy, s_yy, s_yz), (s_xz, s_yz, s_zz))


def contract(second, velocity):
    return [
        second[k][0] * velocity[0] + second[k][1] * velocity[1] + second[k][2] * velocity[2]
        for k in range(3)
    ]


def dot3(a, b):
    return a[0] * b[0] + a[1] * b[1] + a[2] * b[2]


def split_pairs(pulled):
    even = [pulled[i] + pulled[j] for i, j in PAIRS]
    odd = [pulled[i] - pulled[j] for i, j in PAIRS]
    return even, odd


def collide(pulled, velocity, keep, porosity):
    even, odd = split_pairs(pulled)
    total, first, second = moments(even, odd, pulled[0])
    flux = contract(second, velocity)
    twice = dot3(velocity, flux)
    gain = keep * (relax_rate / 36.0)
    stay = keep * (1.0 - relax_rate)
    base = gain * (total * (1.0 + 1.5 * dot3(velocity, velocity)) - 4.5 * twice)
    turn = [gain * (3.0 * (first[k] - velocity[k] * total) + 9.0 * flux[k]) for k in range(3)]
    both = 0.5 * (stay + porosity)
    diff = 0.5 * (stay - porosity)
    results = [None] * 19
    results[0] = (stay + porosity) * pulled[0] + base
    for n, (i, j) in enumerate(PAIRS):
        along = None
        for k in range(3):
            if SPEEDS[i][k] == 1:
                along = turn[k] if along is None else along + turn[k]
            elif SPEEDS[i][k] == -1:
                along = along - turn[k]
        same = both * even[n] + base
        swing = diff * odd[n] + along
        results[i] = same + swing
        results[j] = same - swing
    return results


MIRRORS = [
    (q, SPEEDS.index([-SPEEDS[q][0], SPEEDS[q][1], SPEEDS[q][2]]))
    for q in range(19)
    if SPEEDS[q][0] == 1
]
FLAT = [q for q in range(19) if SPEEDS[q][0] == 0] + list(range(19, 19 + FIELDS))
X_TILES = len(MIRRORS) + (len(FLAT) + 1) // 2


def turned(tile, shift, axis):
    shift = shift % tile.shape[axis]
    return tile if shift == 0 else pltpu.roll(tile, shift, axis)


def flow_fields(popul, level, mask):
    even, odd = split_pairs(popul)
    density = popul[0]
    for n in range(9):
        density = density + even[n]
    o_x, o_y, o_z, o_xy, o_xw, o_xz, o_xv, o_yz, o_yv = odd
    per_mass = 1.0 / density
    porosity = jnp.where(mask == 1, level.astype(jnp.float32) * (porous_max / (LEVELS - 1)), 1.0)
    return (
        (o_x + ((o_xy + o_xw) + (o_xz + o_xv))) * per_mass,
        (o_y + ((o_xy - o_xw) + (o_yz + o_yv))) * per_mass,
        (o_z + ((o_xz - o_xv) + (o_yz - o_yv))) * per_mass,
        1.0 - porosity,
        porosity,
    )


def edge_kernel(
    adj_hbm, fwd_hbm, level_hbm, mask_hbm, outer, inner, adj, fwd_top, fwd_end, level, mask,
    fields, sems,
):
    rows = adj_hbm.shape[2]
    copies = [
        pltpu.make_async_copy(src, dst, sems.at[n])
        for n, (src, dst) in enumerate(
            (
                (fwd_hbm.at[:, :, pl.ds(0, 2), :], fwd_top),
                (fwd_hbm.at[:, :, pl.ds(rows - 2, 2), :], fwd_end),
                (mask_hbm, mask),
                (level_hbm, level),
                (adj_hbm.at[:, :, pl.ds(0, 3), :], adj.at[:, :, pl.ds(0, 3), :]),
                (adj_hbm.at[:, :, pl.ds(rows - 3, 3), :], adj.at[:, :, pl.ds(5, 3), :]),
            )
        )
    ]
    for copy in copies:
        copy.start()
    for copy in copies[:4]:
        copy.wait()
    for z in range(2):
        for fwd, at, to in ((fwd_top, 0, 0), (fwd_end, rows - 2, 6)):
            values = flow_fields(
                [fwd[q, z].astype(jnp.float32) for q in range(19)],
                level[z, at : at + 2, :],
                mask[z, at : at + 2, :],
            )
            for k in range(FIELDS):
                fields[k, z, to : to + 2, :] = values[k]
    for copy in copies[4:]:
        copy.wait()
    even_x = is_even("gx")
    row = iota((8, 128), 0)

    def tile_of(n, z):
        return adj[n, z] if n < 19 else fields[n - 19, z]

    for n, (up, down) in enumerate(MIRRORS):
        low = jnp.where(row < 3, tile_of(up, 0), turned(tile_of(up, 1), 3, 0))
        low = jnp.where(row < 6, low, turned(tile_of(down, 0), 6, 0))
        low = jnp.where(row < 7, low, turned(tile_of(down, 1), 7, 0))
        high = jnp.where(row < 3, turned(tile_of(down, 0), 3, 0), turned(tile_of(down, 1), 6, 0))
        high = jnp.where(row < 6, high, turned(tile_of(up, 0), 7, 0))
        high = jnp.where(row < 7, high, tile_of(up, 1))
        inner[n] = jnp.where(even_x, high, low)
        outer[n] = jnp.where(even_x, low, high)
    for n in range(0, len(FLAT), 2):
        low = high = None
        for m, item in enumerate(FLAT[n : n + 2]):
            for z in range(2):
                at = 4 * m + 2 * z
                up = turned(tile_of(item, z), at, 0)
                down = turned(tile_of(item, z), at + 2, 0)
                low = up if low is None else jnp.where(row < at, low, up)
                high = down if high is None else jnp.where(row < at, high, down)
        tile = len(MIRRORS) + n // 2
        inner[tile] = jnp.where(even_x, high, low)
        outer[tile] = jnp.where(even_x, low, high)


RIGHT = 16
LEFT = 50


def strip_of(pair):
    lane = iota(pair[0].shape, 1)
    parts = [turned(pair[z], side + z * Z_LANES, 1) for z in range(2) for side in (RIGHT, LEFT)]
    strip = parts[3]
    for n in (2, 1, 0):
        strip = jnp.where(lane < 32 * (n + 1), parts[n], strip)
    return strip


def pack_sides(tiles):
    low = high = None
    for z in range(2):
        for n in DEEP + THIN:
            at = z * Z_LANES + STARTS[n]
            tile = tiles(n, z)
            up = turned(tile, at, 1)
            down = turned(tile, at + WIDTHS[n], 1)
            lane = iota(tile.shape, 1)
            low = up if low is None else jnp.where(lane >= at, up, low)
            high = down if high is None else jnp.where(lane >= at, down, high)
    return low, high


def edge_line(block):
    lane = iota(block.shape, 1)
    right = (lane >= RIGHT - 3) & (lane < RIGHT)
    left = (lane >= LEFT) & (lane < LEFT + 3)
    block = jnp.where(right | left, block, 0.0)
    return jnp.sum(pltpu.roll(block, 0, 1, stride=8, stride_axis=0), axis=0, keepdims=True)


def own_kernel(
    adj_hbm, fwd_hbm, level_hbm, mask_hbm, index_hbm, after,
    adj, fwd, mask, index, fields, low_own, high_own, fwd_strip, mask_strip, hot, slots,
    level, sems,
):
    copies = [
        pltpu.make_async_copy(src, dst, sems.at[n])
        for n, (src, dst) in enumerate(
            (
                (fwd_hbm, fwd), (mask_hbm, mask), (level_hbm, level), (index_hbm, index),
                (adj_hbm, adj),
            )
        )
    ]
    for copy in copies:
        copy.start()
    for copy in copies[:4]:
        copy.wait()
    for z in range(2):
        values = flow_fields(
            [fwd[q, z].astype(jnp.float32) for q in range(19)], level[z], mask[z]
        )
        for k in range(FIELDS):
            fields[k, z] = values[k]
    for q in range(19):
        fwd_strip[q] = strip_of([fwd[q, z].astype(jnp.float32) for z in range(2)])
    mask_strip[...] = strip_of([mask[z].astype(jnp.float32) for z in range(2)])
    where = index[...].astype(jnp.float32)
    lane = iota(where.shape, 1)
    where = jnp.where(lane < Z_LANES // 2, turned(where, RIGHT, 1), turned(where, LEFT, 1))
    owner, slot = split_index(edge_line(where).astype(jnp.int32), slots.shape[0])
    hot[...] = jnp.where(iota(hot.shape, 0) == owner, 1.0, 0.0)
    slots[...] = jnp.where(iota(slots.shape, 0) == slot, 1.0, 0.0).astype(jnp.bfloat16)
    copies[4].wait()
    low, high = pack_sides(lambda n, z: adj[n, z] if n < 19 else fields[n - 19, z])
    low_own[...] = low
    high_own[...] = high


def side_kernel(got_outer, got_inner, low_own, high_own, outer, inner, adj_rim, field_rim):
    even_x = is_even("gx")
    row = iota((8, 128), 0)

    def received(tile):
        from_in = got_inner[tile]
        from_out = got_outer[tile]
        return jnp.where(even_x, from_out, from_in), jnp.where(even_x, from_in, from_out)

    for n, (up, down) in enumerate(MIRRORS):
        low, high = received(n)
        for z in range(2):
            adj_rim[up, z] = jnp.where(row < 4, turned(high, -3 * z, 0), turned(low, 1 - z, 0))
            adj_rim[down, z] = jnp.where(row < 4, turned(high, 2 - z, 0), turned(low, 5 - 3 * z, 0))
    for n in range(0, len(FLAT), 2):
        low, high = received(len(MIRRORS) + n // 2)
        for m, item in enumerate(FLAT[n : n + 2]):
            for z in range(2):
                at = 4 * m + 2 * z
                rim = jnp.where(row < 4, turned(high, -at, 0), turned(low, 6 - at, 0))
                if item < 19:
                    adj_rim[item, z] = rim
                else:
                    field_rim[item - 19, z] = rim
    low, high = pack_sides(lambda n, z: adj_rim[n, z] if n < 19 else field_rim[n - 19, z])
    low = jnp.concatenate([low_own[...], low], axis=0)
    high = jnp.concatenate([high_own[...], high], axis=0)
    even_y = is_even("gy")
    inner[...] = jnp.where(even_y, high, low)
    outer[...] = jnp.where(even_y, low, high)


def sensitivity_of(pulled, popul, velocity):
    f_even, f_odd = split_pairs(popul)
    density = popul[0]
    for n in range(9):
        density = density + f_even[n]
    even, odd = split_pairs(pulled)
    total, first, second = moments(even, odd, pulled[0])
    flux = contract(second, velocity)
    even_sum = even[0] * f_even[0]
    odd_sum = odd[0] * f_odd[0]
    for n in range(1, 9):
        even_sum = even_sum + even[n] * f_even[n]
        odd_sum = odd_sum + odd[n] * f_odd[n]
    relaxed = (
        total * (1.0 - 1.5 * dot3(velocity, velocity))
        + 3.0 * dot3(velocity, first)
        + 4.5 * dot3(velocity, flux)
    )
    half = 0.5 * relax_rate
    return (
        half * even_sum
        + (half - 1.0) * odd_sum
        + relax_rate * (popul[0] * pulled[0])
        - (relax_rate / 36.0) * (density * relaxed)
    )


def hot_rows(values, owner, slot, owners, chunk):
    top = values.astype(jnp.bfloat16).astype(jnp.float32)
    hot = iota((owners, 128), 0) == owner
    lhs = jnp.concatenate(
        [
            jnp.where(hot, top, 0.0).astype(jnp.bfloat16),
            jnp.where(hot, values - top, 0.0).astype(jnp.bfloat16),
        ],
        axis=0,
    )
    rhs = jnp.where(iota((chunk, 128), 0) == slot, 1.0, 0.0).astype(jnp.bfloat16)
    return lhs, rhs


def hot_product(lhs, rhs):
    return lax.dot_general(
        lhs, rhs, (((1,), (1,)), ((), ())), preferred_element_type=jnp.float32
    )


def split_index(index, chunk):
    if chunk & (chunk - 1):
        owner = lax.div(index, jnp.full(index.shape, chunk, index.dtype))
    else:
        owner = index >> (chunk.bit_length() - 1)
    return owner, index - owner * chunk


def main_kernel(
    owners, chunk, adj, adj_rim, fields, field_rim, fwd, mask, index,
    grid, inside, strip, field_strip, state, pulls, summed,
):
    rows = adj.shape[2]
    full = rows + 8
    for step_num in range(STEPS):
        final = step_num == STEPS - 1
        for q in range(19):
            shift_x, shift_y, shift_z = SPEEDS[q]
            if step_num == 0:
                start = [jnp.concatenate([adj[q, z], adj_rim[q, z]], axis=0) for z in range(2)]
            both = []
            for z in range(2):
                src = (z + shift_z) % 2
                main = start[src] if step_num == 0 else state[q, src]
                main = turned(turned(main, -shift_x, 0), -shift_y, 1)
                pulls[q, z] = main
                both.append(main)
                own = main[:rows]
                summed[q, z] = own if step_num == 0 else summed[q, z] + own
            if step_num == 0:
                strip[q] = strip_of(both)
        for z in range(2):
            for t in range((rows if final else full) // 8):
                at = slice(8 * t, 8 * t + 8)
                if 8 * t < rows:
                    here = [fields[k, z, at, :] for k in range(FIELDS)]
                else:
                    here = [field_rim[k, z] for k in range(FIELDS)]
                out = collide([pulls[q, z, at, :] for q in range(19)], here[:3], here[3], here[4])
                into = inside if final else state
                for q in range(19):
                    into[q, z, at, :] = out[q]
    for k in range(FIELDS):
        field_strip[k] = strip_of(
            [jnp.concatenate([fields[k, z], field_rim[k, z]], axis=0) for z in range(2)]
        )
    column = None
    for z in range(2):
        term = sensitivity_of(
            [summed[q, z] for q in range(19)],
            [fwd[q, z].astype(jnp.float32) for q in range(19)],
            [fields[k, z] for k in range(3)],
        ) * mask[z].astype(jnp.float32)
        column = term if column is None else column + term
    lane = iota(column.shape, 1)
    column = jnp.where((lane >= 3) & (lane < 125), column * (porous_max / (LEVELS - 1)), 0.0)
    owner, slot = split_index(index[...], chunk)
    acc = None
    for x in range(0, rows, 2):
        parts = [
            hot_rows(column[r : r + 1], owner[r : r + 1], slot[r : r + 1], owners, chunk)
            for r in (x, x + 1)
        ]
        part = hot_product(
            jnp.concatenate([p[0] for p in parts], axis=1),
            jnp.concatenate([p[1] for p in parts], axis=1),
        )
        acc = part if acc is None else acc + part
    grid[...] = acc[:owners] + acc[owners:]


def strip_kernel(
    got_outer, got_inner, strip, field_strip, fwd_strip, mask_strip, inside,
    column, out, state, summed, pulls, field_state,
):
    full = strip.shape[1]
    rows = full - 8
    even_y = is_even("gy")
    from_in = got_inner[...]
    from_out = got_outer[...]
    low = jnp.where(even_y, from_out, from_in)
    high = jnp.where(even_y, from_in, from_out)
    lane = iota((full, 128), 1) & (Z_LANES - 1)
    half = Z_LANES // 2
    deep = jnp.where(lane < 3 * len(DEEP), high, turned(low, LEFT - 3 - RIGHT, 1))
    thin = jnp.where(lane >= half, high, turned(low, LEFT - 2 - RIGHT, 1))
    moved = {
        (width, shift): turned(both, -shift, 0)
        for width, both in ((3, deep), (2, thin))
        for shift in (-1, 0, 1)
    }

    def joined(n, own, shift_x=0, shift_y=0, shift_z=0):
        width = WIDTHS[n]
        turn = RIGHT - STARTS[n] - shift_y + Z_LANES * (shift_z % 2)
        right = RIGHT - shift_y
        left = LEFT - width - shift_y
        inside = ((lane >= right) & (lane < right + width)) | ((lane >= left) & (lane < left + width))
        return jnp.where(inside, turned(moved[width, shift_x], turn, 1), own)

    for k in range(FIELDS):
        field_state[k] = joined(19 + k, field_strip[k])
    for step_num in range(STEPS):
        final = step_num == STEPS - 1
        for q in range(19):
            shift_x, shift_y, shift_z = SPEEDS[q]
            if step_num == 0:
                tile = joined(q, strip[q], shift_x, shift_y, shift_z)
            else:
                tile = turned(state[q], -shift_x, 0)
                tile = turned(tile, Z_LANES * (shift_z % 2) - shift_y, 1)
            own = tile[:rows]
            pulls[q] = tile
            summed[q] = own if step_num == 0 else summed[q] + own
        for t in range((rows if final else full) // 8):
            at = slice(8 * t, 8 * t + 8)
            here = [field_state[k, at, :] for k in range(FIELDS)]
            result = collide([pulls[q, at, :] for q in range(19)], here[:3], here[3], here[4])
            for q in range(19):
                state[q, at, :] = result[q]
    term = sensitivity_of(
        [summed[q] for q in range(19)],
        [fwd_strip[q] for q in range(19)],
        [field_strip[k, :rows, :] for k in range(3)],
    ) * mask_strip[...]
    column[...] = (term + turned(term, Z_LANES, 1)) * (porous_max / (LEVELS - 1))
    own_lane = iota((rows, 128), 1)
    spot = own_lane & (Z_LANES - 1)
    for q in range(19):
        edge = state[q, :rows, :]
        edge = jnp.where(spot < RIGHT, edge, turned(edge, RIGHT - LEFT, 1))
        for z in range(2):
            out[q, z] = jnp.where(
                (own_lane >= 125) | (own_lane < 3),
                turned(edge, -RIGHT - z * Z_LANES, 1),
                inside[q, z],
            )


def sum_kernel(owners, column, hot, slots, grid_inside, after, grid):
    values = edge_line(column[...])
    top = values.astype(jnp.bfloat16).astype(jnp.float32)
    lhs = jnp.concatenate(
        [(hot[...] * top).astype(jnp.bfloat16), (hot[...] * (values - top)).astype(jnp.bfloat16)],
        axis=0,
    )
    acc = hot_product(lhs, slots[...])
    grid[...] = grid_inside[...] + (acc[:owners] + acc[owners:])


def tail_kernel(received, out, adjoint_start, owned, block, sems):
    copy_out = pltpu.make_async_copy(out, adjoint_start, sems.at[0])
    copy_out.start()
    total = jnp.sum(received[...], axis=0, keepdims=True)
    cols = block.shape[1]
    for r in range(block.shape[0]):
        block[r : r + 1, :] = turned(total, -r * cols, 1)[:, :cols]
    copy_owned = pltpu.make_async_copy(block, owned, sems.at[1])
    copy_owned.start()
    copy_owned.wait()
    copy_out.wait()


def call(kernel, out_types, args, scratch=(), flops=0, from_hbm=0, to=pltpu.VMEM):
    moved = sum(a.size * a.dtype.itemsize for a in args)
    spaces = [pltpu.HBM] * from_hbm + [pltpu.VMEM] * (len(args) - from_hbm)
    return pl.pallas_call(
        kernel,
        out_shape=[to(shape, dtype) for shape, dtype in out_types],
        in_specs=[pl.BlockSpec(memory_space=space) for space in spaces],
        out_specs=[pl.BlockSpec(memory_space=to)] * len(out_types),
        scratch_shapes=list(scratch),
        compiler_params=pltpu.CompilerParams(vmem_limit_bytes=16 << 20),
        cost_estimate=pl.CostEstimate(flops=flops, bytes_accessed=moved, transcendentals=0),
    )(*[pltpu.with_memory_space_constraint(a, space) for a, space in zip(args, spaces)])


def per_device(adjoint_end, forward_pop, porosity_level, fluid_mask, design_index):
    depth, tile_x, tile_y = adjoint_end.shape[1:]
    full = tile_x + 8
    gx_count = lax.axis_size("gx")
    gy_count = lax.axis_size("gy")
    owners = gx_count * gy_count
    design_cols = tile_x * gx_count // 4
    design_rows = tile_y * gy_count // 4
    chunk = design_rows * design_cols // owners
    f32 = jnp.float32
    own = ((19, depth, tile_x, tile_y), f32)
    wide = pltpu.VMEM((19, depth, full, tile_y), f32)

    message = ((X_TILES, 8, tile_y), f32)
    static = [porosity_level, fluid_mask]
    outer, inner = call(
        edge_kernel,
        [message, message],
        [adjoint_end, forward_pop, *static],
        [
            pltpu.VMEM((19, depth, 8, tile_y), f32),
            pltpu.VMEM((19, depth, 2, tile_y), forward_pop.dtype),
            pltpu.VMEM((19, depth, 2, tile_y), forward_pop.dtype),
            *[pltpu.VMEM(a.shape, a.dtype) for a in static],
            pltpu.VMEM((FIELDS, depth, 8, tile_y), f32),
            pltpu.SemaphoreType.DMA((6,)),
        ],
        from_hbm=4,
    )
    got_outer = lax.ppermute(outer, "gx", swap_pairs(gx_count, 1))
    got_inner = lax.ppermute(inner, "gx", swap_pairs(gx_count, 0))
    flat = ((tile_x, 128), f32)
    adj, fwd, mask, index, fields, low_own, high_own, fwd_strip, mask_strip, hot, slots = call(
        own_kernel,
        [
            own, (forward_pop.shape, forward_pop.dtype), (fluid_mask.shape, fluid_mask.dtype),
            (design_index.shape, design_index.dtype), ((FIELDS, depth, tile_x, tile_y), f32),
            flat, flat, ((19, tile_x, 128), f32), flat, ((owners, 128), f32),
            ((chunk, 128), jnp.bfloat16),
        ],
        [adjoint_end, forward_pop, *static, design_index, outer],
        [
            pltpu.VMEM(porosity_level.shape, porosity_level.dtype),
            pltpu.SemaphoreType.DMA((5,)),
        ],
        flops=10**6,
        from_hbm=5,
    )
    outer, inner, adj_rim, field_rim = call(
        side_kernel,
        [
            ((full, 128), f32), ((full, 128), f32), ((19, depth, 8, tile_y), f32),
            ((FIELDS, depth, 8, tile_y), f32),
        ],
        [got_outer, got_inner, low_own, high_own],
    )
    got_outer = lax.ppermute(outer, "gy", swap_pairs(gy_count, 1))
    got_inner = lax.ppermute(inner, "gy", swap_pairs(gy_count, 0))
    grid, inside, strip, field_strip = call(
        lambda *refs: main_kernel(owners, chunk, *refs),
        [((owners, chunk), f32), own, ((19, full, 128), f32), ((FIELDS, full, 128), f32)],
        [adj, adj_rim, fields, field_rim, fwd, mask, index],
        [wide, wide, pltpu.VMEM(*own)],
        flops=10**6,
    )
    column, out = call(
        strip_kernel,
        [flat, own],
        [got_outer, got_inner, strip, field_strip, fwd_strip, mask_strip, inside],
        [
            pltpu.VMEM((19, full, 128), f32), pltpu.VMEM((19, tile_x, 128), f32),
            pltpu.VMEM((19, full, 128), f32), pltpu.VMEM((FIELDS, full, 128), f32),
        ],
    )
    (grid,) = call(
        lambda *refs: sum_kernel(owners, *refs),
        [((owners, chunk), f32)],
        [column, hot, slots, grid, out],
    )
    received = lax.all_to_all(
        grid.reshape(owners, 1, chunk), BOTH, split_axis=0, concat_axis=0, tiled=True
    )
    block = ((design_rows // owners, design_cols), f32)
    return tuple(
        call(
            tail_kernel,
            [own, block],
            [received.reshape(owners, chunk), out],
            [pltpu.VMEM(*block), pltpu.SemaphoreType.DMA((2,))],
            to=pltpu.HBM,
        )
    )


def solution(mesh):
    in_specs = (
        P(None, None, "gx", "gy"),
        P(None, None, "gx", "gy"),
        P(None, "gx", "gy"),
        P(None, "gx", "gy"),
        P("gx", "gy"),
    )
    out_specs = (P(None, None, "gx", "gy"), P(("gx", "gy"), None))
    return jax.shard_map(
        per_device, mesh=mesh, in_specs=in_specs, out_specs=out_specs, check_vma=False
    )
```

```python
import jax
import jax.numpy as jnp
from jax import lax
from jax.experimental import pallas as pl
from jax.experimental.pallas import tpu as pltpu
from jax.sharding import PartitionSpec as P

STEPS = 3
LEVELS = 8
BOTH = ("gx", "gy")
FIELDS = 5

relax_rate = 1.25
porous_max = 0.5


def lattice_table():
    speeds = [[0, 0, 0]]
    for axis_index in range(3):
        for sign_value in (1, -1):
            vector_row = [0, 0, 0]
            vector_row[axis_index] = sign_value
            speeds.append(vector_row)
    for plane_pair in ((0, 1), (0, 2), (1, 2)):
        for first_sign in (1, -1):
            for second_sign in (1, -1):
                vector_row = [0, 0, 0]
                vector_row[plane_pair[0]] = first_sign
                vector_row[plane_pair[1]] = second_sign
                speeds.append(vector_row)
    return speeds


SPEEDS = lattice_table()
PAIRS = ((1, 2), (3, 4), (5, 6), (7, 10), (8, 9), (11, 14), (12, 13), (15, 18), (16, 17))

Z_LANES = 64
WIDTHS = [3 if SPEEDS[q][1] != 0 else 2 for q in range(19)] + [2] * FIELDS
DEEP = [n for n in range(19) if WIDTHS[n] == 3]
THIN = [n for n in range(19 + FIELDS) if WIDTHS[n] == 2]
STARTS = [
    3 * DEEP.index(n) if n in DEEP else Z_LANES // 2 + 2 * THIN.index(n) for n in range(19 + FIELDS)
]


def swap_pairs(count, parity):
    pairs = []
    for i in range(count):
        j = (i ^ 1) if parity == 0 else ((i - 1) ^ 1) + 1
        if 0 <= j < count:
            pairs.append((i, j))
    return pairs


def is_even(axis):
    return lax.rem(lax.axis_index(axis), 2) == 0


def iota(shape, dim):
    return lax.broadcasted_iota(jnp.int32, shape, dim)


def moments(even, odd, rest):
    e_x, e_y, e_z, e_xy, e_xw, e_xz, e_xv, e_yz, e_yv = even
    o_x, o_y, o_z, o_xy, o_xw, o_xz, o_xv, o_yz, o_yv = odd
    d_xy = e_xy + e_xw
    d_xz = e_xz + e_xv
    d_yz = e_yz + e_yv
    s_xx = 2.0 * e_x + (d_xy + d_xz)
    s_yy = 2.0 * e_y + (d_xy + d_yz)
    s_zz = 2.0 * e_z + (d_xz + d_yz)
    s_xy = e_xy - e_xw
    s_xz = e_xz - e_xv
    s_yz = e_yz - e_yv
    total = 12.0 * rest + 2.0 * ((e_x + e_y) + e_z) + ((d_xy + d_xz) + d_yz)
    v_x = 2.0 * o_x + ((o_xy + o_xw) + (o_xz + o_xv))
    v_y = 2.0 * o_y + ((o_xy - o_xw) + (o_yz + o_yv))
    v_z = 2.0 * o_z + ((o_xz - o_xv) + (o_yz - o_yv))
    return total, (v_x, v_y, v_z), ((s_xx, s_xy, s_xz), (s_xy, s_yy, s_yz), (s_xz, s_yz, s_zz))


def contract(second, velocity):
    return [
        second[k][0] * velocity[0] + second[k][1] * velocity[1] + second[k][2] * velocity[2]
        for k in range(3)
    ]


def dot3(a, b):
    return a[0] * b[0] + a[1] * b[1] + a[2] * b[2]


def split_pairs(pulled):
    even = [pulled[i] + pulled[j] for i, j in PAIRS]
    odd = [pulled[i] - pulled[j] for i, j in PAIRS]
    return even, odd


def collide(pulled, velocity, keep, porosity):
    even, odd = split_pairs(pulled)
    total, first, second = moments(even, odd, pulled[0])
    flux = contract(second, velocity)
    twice = dot3(velocity, flux)
    gain = keep * (relax_rate / 36.0)
    stay = keep * (1.0 - relax_rate)
    base = gain * (total * (1.0 + 1.5 * dot3(velocity, velocity)) - 4.5 * twice)
    turn = [gain * (3.0 * (first[k] - velocity[k] * total) + 9.0 * flux[k]) for k in range(3)]
    both = 0.5 * (stay + porosity)
    diff = 0.5 * (stay - porosity)
    results = [None] * 19
    results[0] = (stay + porosity) * pulled[0] + base
    for n, (i, j) in enumerate(PAIRS):
        along = None
        for k in range(3):
            if SPEEDS[i][k] == 1:
                along = turn[k] if along is None else along + turn[k]
            elif SPEEDS[i][k] == -1:
                along = along - turn[k]
        same = both * even[n] + base
        swing = diff * odd[n] + along
        results[i] = same + swing
        results[j] = same - swing
    return results


MIRRORS = [
    (q, SPEEDS.index([-SPEEDS[q][0], SPEEDS[q][1], SPEEDS[q][2]]))
    for q in range(19)
    if SPEEDS[q][0] == 1
]
FLAT = [q for q in range(19) if SPEEDS[q][0] == 0] + list(range(19, 19 + FIELDS))
X_TILES = len(MIRRORS) + (len(FLAT) + 1) // 2


def turned(tile, shift, axis):
    shift = shift % tile.shape[axis]
    return tile if shift == 0 else pltpu.roll(tile, shift, axis)


def flow_fields(popul, level, mask):
    even, odd = split_pairs(popul)
    density = popul[0]
    for n in range(9):
        density = density + even[n]
    o_x, o_y, o_z, o_xy, o_xw, o_xz, o_xv, o_yz, o_yv = odd
    per_mass = 1.0 / density
    porosity = jnp.where(mask == 1, level.astype(jnp.float32) * (porous_max / (LEVELS - 1)), 1.0)
    return (
        (o_x + ((o_xy + o_xw) + (o_xz + o_xv))) * per_mass,
        (o_y + ((o_xy - o_xw) + (o_yz + o_yv))) * per_mass,
        (o_z + ((o_xz - o_xv) + (o_yz - o_yv))) * per_mass,
        1.0 - porosity,
        porosity,
    )


def edge_kernel(
    adj_hbm, fwd_hbm, level_hbm, mask_hbm, outer, inner, adj, fwd_top, fwd_end, level, mask,
    fields, sems,
):
    rows = adj_hbm.shape[2]
    copies = [
        pltpu.make_async_copy(src, dst, sems.at[n])
        for n, (src, dst) in enumerate(
            (
                (fwd_hbm.at[:, :, pl.ds(0, 2), :], fwd_top),
                (fwd_hbm.at[:, :, pl.ds(rows - 2, 2), :], fwd_end),
                (mask_hbm, mask),
                (level_hbm, level),
                (adj_hbm.at[:, :, pl.ds(0, 3), :], adj.at[:, :, pl.ds(0, 3), :]),
                (adj_hbm.at[:, :, pl.ds(rows - 3, 3), :], adj.at[:, :, pl.ds(5, 3), :]),
            )
        )
    ]
    for copy in copies:
        copy.start()
    for copy in copies[:4]:
        copy.wait()
    for z in range(2):
        for fwd, at, to in ((fwd_top, 0, 0), (fwd_end, rows - 2, 6)):
            values = flow_fields(
                [fwd[q, z].astype(jnp.float32) for q in range(19)],
                level[z, at : at + 2, :],
                mask[z, at : at + 2, :],
            )
            for k in range(FIELDS):
                fields[k, z, to : to + 2, :] = values[k]
    for copy in copies[4:]:
        copy.wait()
    even_x = is_even("gx")
    row = iota((8, 128), 0)

    def tile_of(n, z):
        return adj[n, z] if n < 19 else fields[n - 19, z]

    for n, (up, down) in enumerate(MIRRORS):
        low = jnp.where(row < 3, tile_of(up, 0), turned(tile_of(up, 1), 3, 0))
        low = jnp.where(row < 6, low, turned(tile_of(down, 0), 6, 0))
        low = jnp.where(row < 7, low, turned(tile_of(down, 1), 7, 0))
        high = jnp.where(row < 3, turned(tile_of(down, 0), 3, 0), turned(tile_of(down, 1), 6, 0))
        high = jnp.where(row < 6, high, turned(tile_of(up, 0), 7, 0))
        high = jnp.where(row < 7, high, tile_of(up, 1))
        inner[n] = jnp.where(even_x, high, low)
        outer[n] = jnp.where(even_x, low, high)
    for n in range(0, len(FLAT), 2):
        low = high = None
        for m, item in enumerate(FLAT[n : n + 2]):
            for z in range(2):
                at = 4 * m + 2 * z
                up = turned(tile_of(item, z), at, 0)
                down = turned(tile_of(item, z), at + 2, 0)
                low = up if low is None else jnp.where(row < at, low, up)
                high = down if high is None else jnp.where(row < at, high, down)
        tile = len(MIRRORS) + n // 2
        inner[tile] = jnp.where(even_x, high, low)
        outer[tile] = jnp.where(even_x, low, high)


RIGHT = 16
LEFT = 50


def strip_of(pair):
    lane = iota(pair[0].shape, 1)
    parts = [turned(pair[z], side + z * Z_LANES, 1) for z in range(2) for side in (RIGHT, LEFT)]
    strip = parts[3]
    for n in (2, 1, 0):
        strip = jnp.where(lane < 32 * (n + 1), parts[n], strip)
    return strip


def pack_sides(tiles):
    low = high = None
    for z in range(2):
        for n in DEEP + THIN:
            at = z * Z_LANES + STARTS[n]
            tile = tiles(n, z)
            up = turned(tile, at, 1)
            down = turned(tile, at + WIDTHS[n], 1)
            lane = iota(tile.shape, 1)
            low = up if low is None else jnp.where(lane >= at, up, low)
            high = down if high is None else jnp.where(lane >= at, down, high)
    return low, high


def edge_line(block):
    lane = iota(block.shape, 1)
    right = (lane >= RIGHT - 3) & (lane < RIGHT)
    left = (lane >= LEFT) & (lane < LEFT + 3)
    block = jnp.where(right | left, block, 0.0)
    return jnp.sum(pltpu.roll(block, 0, 1, stride=8, stride_axis=0), axis=0, keepdims=True)


def own_kernel(
    adj_hbm, fwd_hbm, level_hbm, mask_hbm, index_hbm, after,
    adj, fwd, mask, index, fields, low_own, high_own, fwd_strip, mask_strip, line, level, sems,
):
    copies = [
        pltpu.make_async_copy(src, dst, sems.at[n])
        for n, (src, dst) in enumerate(
            (
                (fwd_hbm, fwd), (mask_hbm, mask), (level_hbm, level), (index_hbm, index),
                (adj_hbm, adj),
            )
        )
    ]
    for copy in copies:
        copy.start()
    for copy in copies[:4]:
        copy.wait()
    for z in range(2):
        values = flow_fields(
            [fwd[q, z].astype(jnp.float32) for q in range(19)], level[z], mask[z]
        )
        for k in range(FIELDS):
            fields[k, z] = values[k]
    for q in range(19):
        fwd_strip[q] = strip_of([fwd[q, z].astype(jnp.float32) for z in range(2)])
    mask_strip[...] = strip_of([mask[z].astype(jnp.float32) for z in range(2)])
    where = index[...].astype(jnp.float32)
    lane = iota(where.shape, 1)
    where = jnp.where(lane < Z_LANES // 2, turned(where, RIGHT, 1), turned(where, LEFT, 1))
    line[...] = jnp.broadcast_to(edge_line(where), line.shape)
    copies[4].wait()
    low, high = pack_sides(lambda n, z: adj[n, z] if n < 19 else fields[n - 19, z])
    low_own[...] = low
    high_own[...] = high


def side_kernel(got_outer, got_inner, low_own, high_own, outer, inner, adj_rim, field_rim):
    even_x = is_even("gx")
    row = iota((8, 128), 0)

    def received(tile):
        from_in = got_inner[tile]
        from_out = got_outer[tile]
        return jnp.where(even_x, from_out, from_in), jnp.where(even_x, from_in, from_out)

    for n, (up, down) in enumerate(MIRRORS):
        low, high = received(n)
        for z in range(2):
            adj_rim[up, z] = jnp.where(row < 4, turned(high, -3 * z, 0), turned(low, 1 - z, 0))
            adj_rim[down, z] = jnp.where(row < 4, turned(high, 2 - z, 0), turned(low, 5 - 3 * z, 0))
    for n in range(0, len(FLAT), 2):
        low, high = received(len(MIRRORS) + n // 2)
        for m, item in enumerate(FLAT[n : n + 2]):
            for z in range(2):
                at = 4 * m + 2 * z
                rim = jnp.where(row < 4, turned(high, -at, 0), turned(low, 6 - at, 0))
                if item < 19:
                    adj_rim[item, z] = rim
                else:
                    field_rim[item - 19, z] = rim
    low, high = pack_sides(lambda n, z: adj_rim[n, z] if n < 19 else field_rim[n - 19, z])
    low = jnp.concatenate([low_own[...], low], axis=0)
    high = jnp.concatenate([high_own[...], high], axis=0)
    even_y = is_even("gy")
    inner[...] = jnp.where(even_y, high, low)
    outer[...] = jnp.where(even_y, low, high)


def sensitivity_of(pulled, popul, velocity):
    f_even, f_odd = split_pairs(popul)
    density = popul[0]
    for n in range(9):
        density = density + f_even[n]
    even, odd = split_pairs(pulled)
    total, first, second = moments(even, odd, pulled[0])
    flux = contract(second, velocity)
    even_sum = even[0] * f_even[0]
    odd_sum = odd[0] * f_odd[0]
    for n in range(1, 9):
        even_sum = even_sum + even[n] * f_even[n]
        odd_sum = odd_sum + odd[n] * f_odd[n]
    relaxed = (
        total * (1.0 - 1.5 * dot3(velocity, velocity))
        + 3.0 * dot3(velocity, first)
        + 4.5 * dot3(velocity, flux)
    )
    half = 0.5 * relax_rate
    return (
        half * even_sum
        + (half - 1.0) * odd_sum
        + relax_rate * (popul[0] * pulled[0])
        - (relax_rate / 36.0) * (density * relaxed)
    )


def hot_rows(values, owner, slot, owners, chunk):
    top = values.astype(jnp.bfloat16).astype(jnp.float32)
    hot = iota((owners, 128), 0) == owner
    lhs = jnp.concatenate(
        [
            jnp.where(hot, top, 0.0).astype(jnp.bfloat16),
            jnp.where(hot, values - top, 0.0).astype(jnp.bfloat16),
        ],
        axis=0,
    )
    rhs = jnp.where(iota((chunk, 128), 0) == slot, 1.0, 0.0).astype(jnp.bfloat16)
    return lhs, rhs


def hot_product(lhs, rhs):
    return lax.dot_general(
        lhs, rhs, (((1,), (1,)), ((), ())), preferred_element_type=jnp.float32
    )


def split_index(index, chunk):
    if chunk & (chunk - 1):
        owner = lax.div(index, jnp.full(index.shape, chunk, index.dtype))
    else:
        owner = index >> (chunk.bit_length() - 1)
    return owner, index - owner * chunk


def main_kernel(
    owners, chunk, adj, adj_rim, fields, field_rim, fwd, mask, index,
    grid, inside, strip, field_strip, state, pulls, summed,
):
    rows = adj.shape[2]
    full = rows + 8
    for step_num in range(STEPS):
        final = step_num == STEPS - 1
        for q in range(19):
            shift_x, shift_y, shift_z = SPEEDS[q]
            if step_num == 0:
                start = [jnp.concatenate([adj[q, z], adj_rim[q, z]], axis=0) for z in range(2)]
            both = []
            for z in range(2):
                src = (z + shift_z) % 2
                main = start[src] if step_num == 0 else state[q, src]
                main = turned(turned(main, -shift_x, 0), -shift_y, 1)
                pulls[q, z] = main
                both.append(main)
                own = main[:rows]
                summed[q, z] = own if step_num == 0 else summed[q, z] + own
            if step_num == 0:
                strip[q] = strip_of(both)
        for z in range(2):
            for t in range((rows if final else full) // 8):
                at = slice(8 * t, 8 * t + 8)
                if 8 * t < rows:
                    here = [fields[k, z, at, :] for k in range(FIELDS)]
                else:
                    here = [field_rim[k, z] for k in range(FIELDS)]
                out = collide([pulls[q, z, at, :] for q in range(19)], here[:3], here[3], here[4])
                into = inside if final else state
                for q in range(19):
                    into[q, z, at, :] = out[q]
    for k in range(FIELDS):
        field_strip[k] = strip_of(
            [jnp.concatenate([fields[k, z], field_rim[k, z]], axis=0) for z in range(2)]
        )
    column = None
    for z in range(2):
        term = sensitivity_of(
            [summed[q, z] for q in range(19)],
            [fwd[q, z].astype(jnp.float32) for q in range(19)],
            [fields[k, z] for k in range(3)],
        ) * mask[z].astype(jnp.float32)
        column = term if column is None else column + term
    lane = iota(column.shape, 1)
    column = jnp.where((lane >= 3) & (lane < 125), column * (porous_max / (LEVELS - 1)), 0.0)
    owner, slot = split_index(index[...], chunk)
    acc = None
    for x in range(0, rows, 2):
        parts = [
            hot_rows(column[r : r + 1], owner[r : r + 1], slot[r : r + 1], owners, chunk)
            for r in (x, x + 1)
        ]
        part = hot_product(
            jnp.concatenate([p[0] for p in parts], axis=1),
            jnp.concatenate([p[1] for p in parts], axis=1),
        )
        acc = part if acc is None else acc + part
    grid[...] = acc[:owners] + acc[owners:]


def strip_kernel(
    got_outer, got_inner, strip, field_strip, fwd_strip, mask_strip, inside,
    column, out, state, summed, pulls, field_state,
):
    full = strip.shape[1]
    rows = full - 8
    even_y = is_even("gy")
    from_in = got_inner[...]
    from_out = got_outer[...]
    low = jnp.where(even_y, from_out, from_in)
    high = jnp.where(even_y, from_in, from_out)
    lane = iota((full, 128), 1) & (Z_LANES - 1)
    half = Z_LANES // 2
    deep = jnp.where(lane < 3 * len(DEEP), high, turned(low, LEFT - 3 - RIGHT, 1))
    thin = jnp.where(lane >= half, high, turned(low, LEFT - 2 - RIGHT, 1))
    moved = {
        (width, shift): turned(both, -shift, 0)
        for width, both in ((3, deep), (2, thin))
        for shift in (-1, 0, 1)
    }

    def joined(n, own, shift_x=0, shift_y=0, shift_z=0):
        width = WIDTHS[n]
        turn = RIGHT - STARTS[n] - shift_y + Z_LANES * (shift_z % 2)
        right = RIGHT - shift_y
        left = LEFT - width - shift_y
        inside = ((lane >= right) & (lane < right + width)) | ((lane >= left) & (lane < left + width))
        return jnp.where(inside, turned(moved[width, shift_x], turn, 1), own)

    for k in range(FIELDS):
        field_state[k] = joined(19 + k, field_strip[k])
    for step_num in range(STEPS):
        final = step_num == STEPS - 1
        for q in range(19):
            shift_x, shift_y, shift_z = SPEEDS[q]
            if step_num == 0:
                tile = joined(q, strip[q], shift_x, shift_y, shift_z)
            else:
                tile = turned(state[q], -shift_x, 0)
                tile = turned(tile, Z_LANES * (shift_z % 2) - shift_y, 1)
            own = tile[:rows]
            pulls[q] = tile
            summed[q] = own if step_num == 0 else summed[q] + own
        for t in range((rows if final else full) // 8):
            at = slice(8 * t, 8 * t + 8)
            here = [field_state[k, at, :] for k in range(FIELDS)]
            result = collide([pulls[q, at, :] for q in range(19)], here[:3], here[3], here[4])
            for q in range(19):
                state[q, at, :] = result[q]
    term = sensitivity_of(
        [summed[q] for q in range(19)],
        [fwd_strip[q] for q in range(19)],
        [field_strip[k, :rows, :] for k in range(3)],
    ) * mask_strip[...]
    column[...] = (term + turned(term, Z_LANES, 1)) * (porous_max / (LEVELS - 1))
    own_lane = iota((rows, 128), 1)
    spot = own_lane & (Z_LANES - 1)
    for q in range(19):
        edge = state[q, :rows, :]
        edge = jnp.where(spot < RIGHT, edge, turned(edge, RIGHT - LEFT, 1))
        for z in range(2):
            out[q, z] = jnp.where(
                (own_lane >= 125) | (own_lane < 3),
                turned(edge, -RIGHT - z * Z_LANES, 1),
                inside[q, z],
            )


def sum_kernel(owners, chunk, column, line, grid_inside, after, grid):
    values = edge_line(column[...])
    owner, slot = split_index(line[0:1, :].astype(jnp.int32), chunk)
    acc = hot_product(*hot_rows(values, owner, slot, owners, chunk))
    grid[...] = grid_inside[...] + (acc[:owners] + acc[owners:])


def tail_kernel(received, out, adjoint_start, owned, block, sems):
    copy_out = pltpu.make_async_copy(out, adjoint_start, sems.at[0])
    copy_out.start()
    total = jnp.sum(received[...], axis=0, keepdims=True)
    cols = block.shape[1]
    for r in range(block.shape[0]):
        block[r : r + 1, :] = turned(total, -r * cols, 1)[:, :cols]
    copy_owned = pltpu.make_async_copy(block, owned, sems.at[1])
    copy_owned.start()
    copy_owned.wait()
    copy_out.wait()


def call(kernel, out_types, args, scratch=(), flops=0, from_hbm=0, to=pltpu.VMEM):
    moved = sum(a.size * a.dtype.itemsize for a in args)
    spaces = [pltpu.HBM] * from_hbm + [pltpu.VMEM] * (len(args) - from_hbm)
    return pl.pallas_call(
        kernel,
        out_shape=[to(shape, dtype) for shape, dtype in out_types],
        in_specs=[pl.BlockSpec(memory_space=space) for space in spaces],
        out_specs=[pl.BlockSpec(memory_space=to)] * len(out_types),
        scratch_shapes=list(scratch),
        compiler_params=pltpu.CompilerParams(vmem_limit_bytes=16 << 20),
        cost_estimate=pl.CostEstimate(flops=flops, bytes_accessed=moved, transcendentals=0),
    )(*[pltpu.with_memory_space_constraint(a, space) for a, space in zip(args, spaces)])


def per_device(adjoint_end, forward_pop, porosity_level, fluid_mask, design_index):
    depth, tile_x, tile_y = adjoint_end.shape[1:]
    full = tile_x + 8
    gx_count = lax.axis_size("gx")
    gy_count = lax.axis_size("gy")
    owners = gx_count * gy_count
    design_cols = tile_x * gx_count // 4
    design_rows = tile_y * gy_count // 4
    chunk = design_rows * design_cols // owners
    f32 = jnp.float32
    own = ((19, depth, tile_x, tile_y), f32)
    wide = pltpu.VMEM((19, depth, full, tile_y), f32)

    message = ((X_TILES, 8, tile_y), f32)
    static = [porosity_level, fluid_mask]
    outer, inner = call(
        edge_kernel,
        [message, message],
        [adjoint_end, forward_pop, *static],
        [
            pltpu.VMEM((19, depth, 8, tile_y), f32),
            pltpu.VMEM((19, depth, 2, tile_y), forward_pop.dtype),
            pltpu.VMEM((19, depth, 2, tile_y), forward_pop.dtype),
            *[pltpu.VMEM(a.shape, a.dtype) for a in static],
            pltpu.VMEM((FIELDS, depth, 8, tile_y), f32),
            pltpu.SemaphoreType.DMA((6,)),
        ],
        from_hbm=4,
    )
    got_outer = lax.ppermute(outer, "gx", swap_pairs(gx_count, 1))
    got_inner = lax.ppermute(inner, "gx", swap_pairs(gx_count, 0))
    flat = ((tile_x, 128), f32)
    adj, fwd, mask, index, fields, low_own, high_own, fwd_strip, mask_strip, line = call(
        own_kernel,
        [
            own, (forward_pop.shape, forward_pop.dtype), (fluid_mask.shape, fluid_mask.dtype),
            (design_index.shape, design_index.dtype), ((FIELDS, depth, tile_x, tile_y), f32),
            flat, flat, ((19, tile_x, 128), f32), flat, ((8, 128), f32),
        ],
        [adjoint_end, forward_pop, *static, design_index, inner],
        [
            pltpu.VMEM(porosity_level.shape, porosity_level.dtype),
            pltpu.SemaphoreType.DMA((5,)),
        ],
        flops=10**6,
        from_hbm=5,
    )
    outer, inner, adj_rim, field_rim = call(
        side_kernel,
        [
            ((full, 128), f32), ((full, 128), f32), ((19, depth, 8, tile_y), f32),
            ((FIELDS, depth, 8, tile_y), f32),
        ],
        [got_outer, got_inner, low_own, high_own],
    )
    got_outer = lax.ppermute(outer, "gy", swap_pairs(gy_count, 1))
    got_inner = lax.ppermute(inner, "gy", swap_pairs(gy_count, 0))
    grid, inside, strip, field_strip = call(
        lambda *refs: main_kernel(owners, chunk, *refs),
        [((owners, chunk), f32), own, ((19, full, 128), f32), ((FIELDS, full, 128), f32)],
        [adj, adj_rim, fields, field_rim, fwd, mask, index],
        [wide, wide, pltpu.VMEM(*own)],
        flops=10**6,
    )
    column, out = call(
        strip_kernel,
        [flat, own],
        [got_outer, got_inner, strip, field_strip, fwd_strip, mask_strip, inside],
        [
            pltpu.VMEM((19, full, 128), f32), pltpu.VMEM((19, tile_x, 128), f32),
            pltpu.VMEM((19, full, 128), f32), pltpu.VMEM((FIELDS, full, 128), f32),
        ],
    )
    (grid,) = call(
        lambda *refs: sum_kernel(owners, chunk, *refs),
        [((owners, chunk), f32)],
        [column, line, grid, out],
    )
    received = lax.all_to_all(
        grid.reshape(owners, 1, chunk), BOTH, split_axis=0, concat_axis=0, tiled=True
    )
    block = ((design_rows // owners, design_cols), f32)
    return tuple(
        call(
            tail_kernel,
            [own, block],
            [received.reshape(owners, chunk), out],
            [pltpu.VMEM(*block), pltpu.SemaphoreType.DMA((2,))],
            to=pltpu.HBM,
        )
    )


def solution(mesh):
    in_specs = (
        P(None, None, "gx", "gy"),
        P(None, None, "gx", "gy"),
        P(None, "gx", "gy"),
        P(None, "gx", "gy"),
        P("gx", "gy"),
    )
    out_specs = (P(None, None, "gx", "gy"), P(("gx", "gy"), None))
    return jax.shard_map(
        per_device, mesh=mesh, in_specs=in_specs, out_specs=out_specs, check_vma=False
    )
```
